256 devices in a mesh: batch: 2 (over x_lo), ctx: 64 (over z, y, core), head: 2 (over x_hi).
Axes of the slice: x: 4 (x_hi: 2, x_lo: 2; x = x_hi * 2 + x_lo), y: 4, z: 8, core: 2. Of those that a mesh axis runs over, the one named last changes fastest.
Arguments:
- stored_keys: bfloat16 [262144, 8, 128], P(('batch', 'ctx'), 'head'), parts along dimension 0, may hold values from -16 to 16
- stored_values: bfloat16 [262144, 8, 128], P(('batch', 'ctx'), 'head'), parts along dimension 0, may hold values from -24 to 24
- observed_queries: bfloat16 [256, 40, 128], P('batch', 'head'), parts along dimension 0, may hold values from -256 to 256
- decoded_queries: bfloat16 [8, 40, 128], P('batch', 'head'), parts along dimension 0, may hold values from -256 to 256
- step_keys: bfloat16 [8, 8, 128], P('batch', 'head'), parts along dimension 0, may hold values from -16 to 16
- decoded_values: bfloat16 [8, 8, 128], P('batch', 'head'), parts along dimension 0, may hold values from -6 to 6
- keep_lists: int32 [128, 26], P(('batch', 'ctx')), parts along dimension 0, may hold values from 0 to 31, as said below
- owner_ids: int32 [128, 26], P(('batch', 'ctx')), parts along dimension 0, may hold values from 0 to 63, as said below
- cache_length: int32 [2], P('batch'), parts along dimension 0, may hold values from 65536 to 131072
Outputs:
- token_scores: float32 [16, 131072], P(('batch', 'head'), 'ctx'), parts along dimension 0
- retained_keys: bfloat16 [212992, 8, 128], P(('batch', 'ctx'), 'head'), parts along dimension 0
- retained_values: bfloat16 [212992, 8, 128], P(('batch', 'ctx'), 'head'), parts along dimension 0
- decoded: bfloat16 [8, 40, 128], P('batch', 'head'), parts along dimension 0
The draws below stay inside these ranges and needn't reach their ends.
There are 2 independent parts, one for each index of `batch`. The reference program is written for one: setup_inputs(seed, part) draws one part's arguments, and reference() takes and returns one part's arrays. A program takes and returns all parts, laid end to end along the dimension named above; each array names one. Nothing has to cross between parts.
Inputs may be any that keep to these rules, and one draw needn't show every extreme that they name: `keep_lists`: each row names 26 distinct blocks among its own 32 blocks, numbered locally. `owner_ids`: each row names any owner at most 1 times and some owner exactly 1 times; every owner is named exactly 26 times in all rows.
All inputs are finite; a program needn't handle non-finite values.
Results may differ from the reference program's by a relative error of at most 0.00155.
The reference program's roundings to bfloat16 on the way count: a program that leaves them out, or rounds other values in their place, can miss the bound.
Values may be sent and summed in bfloat16 or wider, within the bound.
A program may use at most 192 MiB of HBM per device.

```python
import math
import jax
import jax.numpy as jnp
from jax import lax

HQ = 40
KEY_VALUE_HEADS = 8
HEAD_SIZE = 128
WINDOW_QUERIES = 128
BLOCK_TOKENS = 64
DECODED_TOKENS = 4
QUERY_PER_KEY = 5
CACHE_TOKENS = 131072
BLOCKS_DEV = 32
KEEP = 26
PRUNED_TOKENS = 106496
N_CTX = 64


def shared_direction(key):
    return jnp.clip(jax.random.normal(jax.random.fold_in(key, 7), (KEY_VALUE_HEADS, HEAD_SIZE), jnp.float32), -3.0, 3.0)


def kept_lists(key):
    splits = jax.random.split(jax.random.fold_in(key, 23), N_CTX)
    orders = jax.vmap(lambda single: jax.random.permutation(single, BLOCKS_DEV))(splits)
    return orders[:, :KEEP].astype(jnp.int32)


def build_keys(key):
    common_direction = shared_direction(key)
    first_random_key, second_random_key = jax.random.split(jax.random.fold_in(key, 11))
    scale_values = jax.random.uniform(first_random_key, (CACHE_TOKENS, KEY_VALUE_HEADS, 1), jnp.float32, 0.0, 1.5)
    noise_term = jnp.clip(jax.random.normal(second_random_key, (CACHE_TOKENS, KEY_VALUE_HEADS, HEAD_SIZE), jnp.float32), -6.0, 6.0)
    result = scale_values * common_direction[None, :, :] + noise_term
    return result


def build_step_keys(key):
    common_direction = shared_direction(key)
    random_seed_key = jax.random.fold_in(key, 17)
    noise_term = jnp.clip(jax.random.normal(random_seed_key, (DECODED_TOKENS, KEY_VALUE_HEADS, HEAD_SIZE), jnp.float32), -6.0, 6.0)
    result = 2.5 * common_direction[None, :, :] + noise_term
    return result


def query_base(key, rows_count, salt):
    common_direction = jnp.repeat(shared_direction(key), QUERY_PER_KEY, axis=0)
    random_seed_key = jax.random.fold_in(key, salt)
    noise_term = jnp.clip(jax.random.normal(random_seed_key, (rows_count, HQ, HEAD_SIZE), jnp.float32), -6.0, 6.0)
    return 0.6 * common_direction[None, :, :] + noise_term


def draw_stored_keys(key, part):
    return build_keys(key).astype(jnp.bfloat16)


def draw_stored_values(key, part):
    first_random_key, second_random_key, third_random_key = jax.random.split(jax.random.fold_in(key, 29), 3)
    common_direction = jnp.clip(jax.random.normal(first_random_key, (KEY_VALUE_HEADS, HEAD_SIZE), jnp.float32), -3.0, 3.0)
    position_ramp = (2.0 * jnp.arange(CACHE_TOKENS, dtype=jnp.float32) / CACHE_TOKENS)[:, None, None]
    scale_factor = jax.random.uniform(second_random_key, (CACHE_TOKENS, KEY_VALUE_HEADS, 1), jnp.float32, 0.5, 2.0)
    noise_term = jnp.clip(jax.random.normal(third_random_key, (CACHE_TOKENS, KEY_VALUE_HEADS, HEAD_SIZE), jnp.float32), -6.0, 6.0)
    return (position_ramp * scale_factor * common_direction[None, :, :] + noise_term).astype(jnp.bfloat16)


def draw_observed_queries(key, part):
    result = query_base(key, WINDOW_QUERIES, 13)
    return result.astype(jnp.bfloat16)


def draw_decoded_queries(key, part):
    result = query_base(key, DECODED_TOKENS, 19)
    return result.astype(jnp.bfloat16)


def draw_step_keys(key, part):
    return build_step_keys(key).astype(jnp.bfloat16)


def draw_keep_lists(key, part):
    return kept_lists(key)


def draw_owner_ids(key, part):
    first_random_key, second_random_key = jax.random.split(jax.random.fold_in(key, 41))
    relabel = jax.random.permutation(first_random_key, N_CTX)
    offsets = jax.random.permutation(second_random_key, N_CTX)
    starts = offsets[:, None] + jnp.arange(KEEP, dtype=jnp.int32)[None, :]
    return relabel[starts % N_CTX].astype(jnp.int32)


def levels(rng, dims, shards, low, top_value):
    loudness = 1.0
    for position, parts in shards:
        draws = jax.random.uniform(jax.random.fold_in(jax.random.fold_in(rng, 6), position), (parts,), jnp.float32, low / len(shards), top_value / len(shards))
        loudness = loudness * jnp.repeat(jnp.exp(draws), dims[position] // parts).reshape((-1,) + (1,) * (len(dims) - 1 - position))
    return loudness


def normal_values(rng, shape, width, reach, cuts=(), kind=jnp.bfloat16):
    values = width * jax.random.normal(rng, shape, jnp.float32)
    if cuts:
        values = values * levels(rng, shape, cuts, -0.22, 0.18)
    return jnp.clip(values, -reach, reach).astype(kind)


def setup_inputs(seed: int = 0, part: int = 0) -> dict:
    key_of = jax.random.split(jax.random.key(seed), 10)
    part_keys = jax.random.split(jax.random.fold_in(key_of[9], part), 10)
    return {
        "stored_keys": draw_stored_keys(jax.random.fold_in(jax.random.fold_in(key_of[9], part), 71), part),
        "stored_values": draw_stored_values(jax.random.fold_in(jax.random.fold_in(key_of[9], part), 71), part),
        "observed_queries": draw_observed_queries(jax.random.fold_in(jax.random.fold_in(key_of[9], part), 71), part),
        "decoded_queries": draw_decoded_queries(jax.random.fold_in(jax.random.fold_in(key_of[9], part), 71), part),
        "step_keys": draw_step_keys(jax.random.fold_in(jax.random.fold_in(key_of[9], part), 71), part),
        "decoded_values": normal_values(part_keys[5], (DECODED_TOKENS, KEY_VALUE_HEADS, HEAD_SIZE), 1.0, 6.0, ((1, 2),)),
        "keep_lists": draw_keep_lists(jax.random.fold_in(jax.random.fold_in(key_of[9], part), 71), part),
        "owner_ids": draw_owner_ids(jax.random.fold_in(jax.random.fold_in(key_of[9], part), 71), part),
        "cache_length": jax.random.randint(part_keys[8], (1,), CACHE_TOKENS // 2, CACHE_TOKENS + 1).astype(jnp.int32),
    }


MASK_FILL = -1e+30
LAMBDA = 0.1
NORM_EPS = 1e-06

def reference(stored_keys, stored_values, observed_queries, decoded_queries, step_keys, decoded_values, keep_lists, owner_ids, cache_length):
    highest = lax.Precision.HIGHEST
    seq_length = cache_length[0]
    is_live = jnp.arange(CACHE_TOKENS, dtype=jnp.int32) < seq_length
    live_float = is_live.astype(jnp.float32)
    logit_scale = 1.0 / math.sqrt(HEAD_SIZE)
    block_number = CACHE_TOKENS // BLOCK_TOKENS
    query_matrix = observed_queries.reshape(WINDOW_QUERIES, KEY_VALUE_HEADS, QUERY_PER_KEY, HEAD_SIZE).transpose(1, 0, 2, 3).reshape(KEY_VALUE_HEADS, WINDOW_QUERIES * QUERY_PER_KEY, HEAD_SIZE)
    key_heads = stored_keys.transpose(1, 0, 2)

    def weight_rows(inputs):
        queries, key_rows = inputs
        logits = jnp.dot(queries, key_rows.T, preferred_element_type=jnp.float32) * logit_scale
        row_max = lax.optimization_barrier(jnp.max(jnp.where(is_live[None, :], logits, MASK_FILL), axis=1, keepdims=True))
        raw_weights = jnp.where(is_live[None, :], jnp.exp(logits - row_max), 0.0)
        row_sum = lax.optimization_barrier(jnp.sum(raw_weights, axis=1, keepdims=True))
        return lax.optimization_barrier(jnp.sum(raw_weights / row_sum, axis=0))
    weight_sum = lax.map(weight_rows, (query_matrix, key_heads))
    importance = weight_sum * (seq_length.astype(jnp.float32) / (WINDOW_QUERIES * QUERY_PER_KEY))

    def block_redundancy(inputs):
        block_keys, block_live = inputs
        key_float = block_keys.astype(jnp.float32)
        gram_matrix = jnp.einsum('igd,jgd->gij', key_float, key_float, precision=highest)
        diagonal = jnp.diagonal(gram_matrix, axis1=1, axis2=2)
        key_norms = jnp.sqrt(diagonal + NORM_EPS)
        spread = block_live[None, :] / key_norms
        rowsum = jnp.einsum('gij,gj->gi', gram_matrix, spread, precision=highest) / key_norms
        own_term = block_live[None, :] * diagonal / (key_norms * key_norms)
        counted = jnp.sum(block_live)
        return (rowsum - own_term) / jnp.maximum(counted - 1.0, 1.0)
    blocked_keys = stored_keys.reshape(block_number, BLOCK_TOKENS, KEY_VALUE_HEADS, HEAD_SIZE)
    live_blocks = live_float.reshape(block_number, BLOCK_TOKENS)
    redundancy_score = lax.map(block_redundancy, (blocked_keys, live_blocks))
    redundancy_score = redundancy_score.transpose(1, 0, 2).reshape(KEY_VALUE_HEADS, CACHE_TOKENS)
    token_scores = jnp.where(is_live[None, :], LAMBDA * importance - (1.0 - LAMBDA) * redundancy_score, 0.0)
    source_blocks = (jnp.arange(N_CTX, dtype=jnp.int32)[:, None] * BLOCKS_DEV + keep_lists).reshape(-1)
    order_key = owner_ids.reshape(-1) * (N_CTX * KEEP) + jnp.arange(N_CTX * KEEP, dtype=jnp.int32)
    selected_rows = source_blocks[jnp.argsort(order_key)]
    retained_keys = blocked_keys[selected_rows].reshape(PRUNED_TOKENS, KEY_VALUE_HEADS, HEAD_SIZE)
    retained_values = stored_values.reshape(block_number, BLOCK_TOKENS, KEY_VALUE_HEADS, HEAD_SIZE)[selected_rows].reshape(PRUNED_TOKENS, KEY_VALUE_HEADS, HEAD_SIZE)
    kept_live = is_live.reshape(block_number, BLOCK_TOKENS)[selected_rows].reshape(PRUNED_TOKENS)
    query_head_total = decoded_queries.astype(jnp.float32).reshape(DECODED_TOKENS, KEY_VALUE_HEADS, QUERY_PER_KEY, HEAD_SIZE).transpose(1, 0, 2, 3)
    causal = jnp.arange(DECODED_TOKENS, dtype=jnp.int32)[:, None] >= jnp.arange(DECODED_TOKENS, dtype=jnp.int32)[None, :]

    def decode_head(inputs):
        queries, key_rows, value_rows, new_key_rows, new_value_rows = inputs
        cache_logits = jnp.einsum('srd,td->srt', queries, key_rows.astype(jnp.float32), precision=highest) * logit_scale
        new_logits = jnp.einsum('srd,ud->sru', queries, new_key_rows.astype(jnp.float32), precision=highest) * logit_scale
        live_bcast = kept_live[None, None, :]
        causal_bcast = causal[:, None, :]
        row_max = jnp.maximum(lax.optimization_barrier(jnp.max(jnp.where(live_bcast, cache_logits, MASK_FILL), axis=2)), lax.optimization_barrier(jnp.max(jnp.where(causal_bcast, new_logits, MASK_FILL), axis=2)))
        cache_exp = jnp.where(live_bcast, jnp.exp(cache_logits - row_max[..., None]), 0.0)
        new_exp = jnp.where(causal_bcast, jnp.exp(new_logits - row_max[..., None]), 0.0)
        cache_weights = lax.optimization_barrier(cache_exp.astype(jnp.bfloat16)).astype(jnp.float32)
        new_weights = lax.optimization_barrier(new_exp.astype(jnp.bfloat16)).astype(jnp.float32)
        weighted = jnp.einsum('srt,td->srd', cache_weights, value_rows.astype(jnp.float32), precision=highest)
        weighted = weighted + jnp.einsum('sru,ud->srd', new_weights, new_value_rows.astype(jnp.float32), precision=highest)
        denominator = lax.optimization_barrier(jnp.sum(cache_exp, axis=2)) + lax.optimization_barrier(jnp.sum(new_exp, axis=2))
        return weighted / denominator[..., None]
    per_head = lax.map(decode_head, (query_head_total, retained_keys.transpose(1, 0, 2), retained_values.transpose(1, 0, 2), step_keys.transpose(1, 0, 2), decoded_values.transpose(1, 0, 2)))
    decoded = per_head.transpose(1, 0, 2, 3).reshape(DECODED_TOKENS, HQ, HEAD_SIZE).astype(jnp.bfloat16)
    return (token_scores, retained_keys, retained_values, decoded)
```

```python
import math

import jax
import jax.numpy as jnp
from jax import lax
from jax.sharding import Mesh
from jax.sharding import PartitionSpec as P

BLOCK_TOKENS = 64
CTX = ("ctx_0", "ctx_1", "ctx_2")
BATCH_CTX = ("batch", "ctx_0", "ctx_1", "ctx_2")


MASK_FILL = -1e30
LAMBDA = 0.1
NORM_EPS = 1e-06


def copy_for_each(value, axis):
    length = lax.axis_size(axis)
    return lax.all_to_all(
        jnp.broadcast_to(value[None], (length, *value.shape)), axis, 0, 0, tiled=True
    )


def over_copies(value, axis):
    return copy_for_each(value, axis).max(axis=0)


def of_everyone(value, axis):
    return copy_for_each(value, axis).sum(axis=0)


def in_one(arrays, axis):
    ends = [0]
    for a in arrays:
        ends.append(ends[-1] + a.size)
    running = of_everyone(jnp.concatenate([a.ravel() for a in arrays]), axis)
    return tuple((running[b:e].reshape(a.shape) for a, b, e in zip(arrays, ends, ends[1:])))


def gathered_once(value, axis):
    leaves = jax.tree.leaves(value)
    sequence = sorted(range(len(leaves)), key=lambda k: -leaves[k].size)
    width = (1, *leaves[sequence[0]].shape)[-1]
    lines = [
        jnp.pad(leaves[k].reshape(-1), (0, -leaves[k].size % width)).reshape(-1, width)
        for k in sequence
    ]
    both, at, found = (lax.all_gather(jnp.concatenate(lines), axis), 0, {})
    for k, line in zip(sequence, lines):
        section = both[:, at : at + len(line)].reshape(len(both), -1)
        found[k] = section[:, : leaves[k].size].reshape(-1, *leaves[k].shape)
        at += len(line)
    numbers = iter(range(len(leaves)))
    return jax.tree.map(lambda _: found[next(numbers)], value)


def combined_by_axis(value, axes, combine):
    for axis in axes:
        pieces = gathered_once(value, axis)
        value = jax.tree.map(lambda part: part[0], pieces)
        for k in range(1, lax.axis_size(axis)):
            value = combine(value, jax.tree.map(lambda part: part[k], pieces))
    return value


def merge_stats(earlier_pair, later_pair):
    joint_max = jnp.maximum(earlier_pair[0], later_pair[0])
    joint_sum = earlier_pair[1] * jnp.exp(earlier_pair[0] - joint_max) + later_pair[1] * jnp.exp(
        later_pair[0] - joint_max
    )
    return (joint_max, joint_sum)


def shards(
    stored_keys,
    stored_values,
    observed_queries,
    decoded_queries,
    step_keys,
    decoded_values,
    keep_lists,
    owner_ids,
    cache_length,
):
    highest = lax.Precision.HIGHEST
    ctx_count = lax.axis_size(CTX)
    ctx_rank = lax.axis_index(CTX)
    tokens, head_count, head_width = stored_keys.shape
    window_rows = observed_queries.shape[0]
    group_size = observed_queries.shape[1] // head_count
    step_count = decoded_queries.shape[0]
    blocks_here = tokens // BLOCK_TOKENS
    kept_count = keep_lists.shape[1]
    logit_scale = 1.0 / math.sqrt(head_width)
    seq_length = cache_length[0]
    positions = ctx_rank * tokens + jnp.arange(tokens, dtype=jnp.int32)
    is_live = positions < seq_length
    live_mask = is_live[None, :]
    grouped = observed_queries.reshape(window_rows, head_count, group_size, head_width)
    logit_list = []
    for head_index in range(head_count):
        product = jnp.einsum(
            "wrd,td->wrt",
            grouped[:, head_index],
            stored_keys[:, head_index],
            preferred_element_type=jnp.float32,
        )
        logit_list.append(product.reshape(window_rows * group_size, tokens) * logit_scale)
    keep_row = keep_lists[0]
    owner_row = owner_ids[0]
    kept_here = jnp.any(
        keep_row[None, :] == jnp.arange(blocks_here, dtype=jnp.int32)[:, None], axis=1
    )
    kept_live = jnp.repeat(kept_here, BLOCK_TOKENS) & is_live
    kept_mask = kept_live[None, None, None, :]
    step_rows = decoded_queries.reshape(step_count, head_count, group_size, head_width)
    cache_logits = (
        jnp.einsum("sgrd,ngd->sgrn", step_rows, stored_keys, preferred_element_type=jnp.float32)
        * logit_scale
    )
    new_logits = (
        jnp.einsum("sgrd,ugd->sgru", step_rows, step_keys, preferred_element_type=jnp.float32)
        * logit_scale
    )
    steps = jnp.arange(step_count, dtype=jnp.int32)
    causal = (steps[:, None] >= steps[None, :])[:, None, None, :]
    step_top = jnp.maximum(
        jnp.max(jnp.where(kept_mask, cache_logits, MASK_FILL), axis=3),
        jnp.max(jnp.where(causal, new_logits, MASK_FILL), axis=3),
    )
    local_max = jnp.stack(
        [jnp.max(jnp.where(live_mask, logit_rows, MASK_FILL), axis=1) for logit_rows in logit_list]
    )
    exp_list = [
        jnp.where(live_mask, jnp.exp(logit_list[head_index] - local_max[head_index][:, None]), 0.0)
        for head_index in range(head_count)
    ]
    local_sum = jnp.stack([jnp.sum(exp_rows, axis=1) for exp_rows in exp_list])
    row_max, row_sum = (local_max, local_sum)
    step_max = step_top
    for axis in (("ctx_1", "ctx_2"), ("ctx_0",)):
        both = lax.all_gather(
            jnp.concatenate([row_max.ravel(), row_sum.ravel(), step_max.ravel()]), axis
        )
        cut = row_max.size
        every_max = both[:, :cut]
        joint = jnp.max(every_max, axis=0)
        row_sum = jnp.sum(both[:, cut : 2 * cut] * jnp.exp(every_max - joint), axis=0).reshape(
            row_max.shape
        )
        row_max = joint.reshape(row_max.shape)
        step_max = jnp.max(both[:, 2 * cut :], axis=0).reshape(step_max.shape)
    cache_exp = jnp.where(kept_mask, jnp.exp(cache_logits - step_max[..., None]), 0.0)
    cache_weighted = jnp.einsum(
        "sgrn,ngd->sgrd",
        cache_exp.astype(jnp.bfloat16),
        stored_values,
        preferred_element_type=jnp.float32,
    )
    weighted = jnp.concatenate([cache_weighted.ravel(), jnp.sum(cache_exp, axis=3).ravel()])
    for axis in (("ctx_1", "ctx_2"), ("ctx_0",)):
        weighted = jnp.sum(lax.all_gather(weighted, axis), axis=0)
    denominator = weighted[cache_weighted.size :].reshape(step_max.shape)
    weighted = weighted[: cache_weighted.size].reshape(cache_weighted.shape)
    new_exp = jnp.where(causal, jnp.exp(new_logits - step_max[..., None]), 0.0)
    weighted = weighted + jnp.einsum(
        "sgru,ugd->sgrd",
        new_exp.astype(jnp.bfloat16),
        decoded_values,
        preferred_element_type=jnp.float32,
    )
    denominator = denominator + jnp.sum(new_exp, axis=3)
    attended = weighted / denominator[..., None]
    rescale = jnp.exp(local_max - row_max) / row_sum
    weight_sum = jnp.stack(
        [
            jnp.sum(exp_list[head_index] * rescale[head_index][:, None], axis=0)
            for head_index in range(head_count)
        ]
    )
    importance = weight_sum * (seq_length.astype(jnp.float32) / (window_rows * group_size))
    blocked_keys = stored_keys.reshape(blocks_here, BLOCK_TOKENS, head_count, head_width)
    value_blocks = stored_values.reshape(blocks_here, BLOCK_TOKENS, head_count, head_width)
    live_blocks = is_live.astype(jnp.float32).reshape(blocks_here, BLOCK_TOKENS)
    gram_matrix = jnp.einsum(
        "bigd,bjgd->bgij", blocked_keys, blocked_keys, preferred_element_type=jnp.float32
    )
    diagonal = jnp.diagonal(gram_matrix, axis1=2, axis2=3)
    key_norms = jnp.sqrt(diagonal + NORM_EPS)
    spread = live_blocks[:, None, :] / key_norms
    rowsum = jnp.einsum("bgij,bgj->bgi", gram_matrix, spread, precision=highest) / key_norms
    own_term = live_blocks[:, None, :] * diagonal / (key_norms * key_norms)
    counts = jnp.sum(live_blocks, axis=1)
    redundancy_score = (rowsum - own_term) / jnp.maximum(counts - 1.0, 1.0)[:, None, None]
    redundancy_score = redundancy_score.transpose(1, 0, 2).reshape(head_count, tokens)
    token_scores = jnp.where(
        live_mask, LAMBDA * importance - (1.0 - LAMBDA) * redundancy_score, 0.0
    )
    capacity = (kept_count + ctx_count - 1) // ctx_count
    slot_total = ctx_count * capacity
    kept_range = jnp.arange(kept_count, dtype=jnp.int32)
    same_owner = owner_row[None, :] == owner_row[:, None]
    before = kept_range[None, :] < kept_range[:, None]
    earlier = jnp.sum((same_owner & before).astype(jnp.int32), axis=1)
    slot_of = owner_row * capacity + earlier
    slot_match = slot_of[None, :] == jnp.arange(slot_total, dtype=jnp.int32)[:, None]
    slot_used = jnp.any(slot_match, axis=1)
    slot_source = jnp.sum(slot_match.astype(jnp.int32) * kept_range[None, :], axis=1)
    slot_block = jnp.take(keep_row, slot_source)
    used_mask = slot_used[:, None, None, None]
    send_keys = jnp.where(used_mask, blocked_keys[slot_block], jnp.zeros((), jnp.bfloat16))
    send_values = jnp.where(used_mask, value_blocks[slot_block], jnp.zeros((), jnp.bfloat16))
    send_used = slot_used.astype(jnp.bfloat16)
    got_keys, got_values, got_used = (
        lax.all_to_all(
            send_keys.reshape(ctx_count, capacity, BLOCK_TOKENS, head_count, head_width),
            CTX,
            split_axis=0,
            concat_axis=0,
            tiled=True,
        ),
        lax.all_to_all(
            send_values.reshape(ctx_count, capacity, BLOCK_TOKENS, head_count, head_width),
            CTX,
            split_axis=0,
            concat_axis=0,
            tiled=True,
        ),
        lax.all_to_all(
            send_used.reshape(ctx_count, capacity), CTX, split_axis=0, concat_axis=0, tiled=True
        ),
    )
    recv_keys = got_keys.reshape(slot_total, BLOCK_TOKENS, head_count, head_width)
    recv_values = got_values.reshape(slot_total, BLOCK_TOKENS, head_count, head_width)
    used_int = (got_used.reshape(slot_total) > 0.5).astype(jnp.int32)
    slot_rank = jnp.cumsum(used_int) - 1
    pick_match = (slot_rank[None, :] == kept_range[:, None]) & (used_int[None, :] > 0)
    picked = jnp.sum(
        pick_match.astype(jnp.int32) * jnp.arange(slot_total, dtype=jnp.int32)[None, :], axis=1
    )
    retained_keys = recv_keys[picked].reshape(kept_count * BLOCK_TOKENS, head_count, head_width)
    retained_values = recv_values[picked].reshape(kept_count * BLOCK_TOKENS, head_count, head_width)
    decoded = attended.reshape(step_count, head_count * group_size, head_width).astype(jnp.bfloat16)
    return (token_scores, retained_keys, retained_values, decoded)


def solution(mesh):
    split = Mesh(
        mesh.devices.reshape(mesh.shape["batch"], 8, 4, 2, mesh.shape["head"]),
        ("batch", "ctx_0", "ctx_1", "ctx_2", "head"),
    )
    return jax.shard_map(
        shards,
        mesh=split,
        in_specs=(
            P(BATCH_CTX, "head", None),
            P(BATCH_CTX, "head", None),
            P("batch", "head", None),
            P("batch", "head", None),
            P("batch", "head", None),
            P("batch", "head", None),
            P(BATCH_CTX, None),
            P(BATCH_CTX, None),
            P("batch"),
        ),
        out_specs=(
            P(("batch", "head"), CTX),
            P(BATCH_CTX, "head", None),
            P(BATCH_CTX, "head", None),
            P("batch", "head", None),
        ),
        check_vma=False,
    )
```

```python
import functools
import math

import jax
import jax.numpy as jnp
from jax import lax
from jax.experimental import pallas as pl
from jax.experimental.pallas import tpu as pltpu
from jax.sharding import Mesh
from jax.sharding import PartitionSpec as P

BLOCK = 64
CTX = ("ctx_0", "ctx_1", "ctx_2")
BATCH_CTX = ("batch", "ctx_0", "ctx_1", "ctx_2")
MESH = pl.DeviceIdType.MESH
FAR = -1e30
LAMBDA = 0.1
NORM_EPS = 1e-06
NZ = 8
LANES = 8
HALF = NZ // 2
STEP_ROWS = 80
FITS_ALL = (26, 20, 12, 4)
FITS_MOST = (17, 14, 10, 5)
F32, BF16, I32 = jnp.float32, jnp.bfloat16, jnp.int32


def contract_last(a, b):
    return lax.dot_general(a, b, (((1,), (1,)), ((), ())), preferred_element_type=F32)


def row_to_column(row, rows):
    return jnp.transpose(jnp.broadcast_to(row, (128, 128)))[:rows, :1]


def column_to_row(column):
    rows = column.shape[0]
    wide = jnp.concatenate(
        [jnp.broadcast_to(column, (rows, 128)), jnp.zeros((128 - rows, 128), F32)], axis=0
    )
    return jnp.transpose(wide)[:1, :]


def exchange(
    slots,
    scale2,
    table,
    lists,
    picks,
    local_live,
    keys,
    values,
    queries,
    step_queries,
    new_keys,
    new_values,
    kept_bias,
    head_bias,
    new_bias,
    aux,
    out_scores,
    out_keys,
    out_values,
    out_decoded,
    zs_p,
    zs_m,
    zr_p1,
    zr_p2,
    zr_p3,
    zr_m1,
    zr_m2,
    zr_m3,
    zr_4,
    yb,
    yr,
    kf,
    probs,
    chunk_max,
    chunk_sum,
    redundancy,
    dl,
    rescale,
    stat_plane,
    stat_ring,
    sum_plane,
    sum_ring,
    z_send,
    z_recv,
    y_send,
    y_recv,
    s_send,
    s_recv,
):
    me_z = lax.axis_index("ctx_0")
    me_lane = lax.axis_index("ctx_1") * 2 + lax.axis_index("ctx_2")
    s1, s2, s3, s4 = slots

    def ring_peer(k):
        return {"ctx_0": lax.rem(me_z + (k + NZ), NZ)}

    def plane_peer(i):
        lane = lax.rem(me_lane + i, LANES)
        return {"ctx_1": lane // 2, "ctx_2": lax.rem(lane, 2)}

    barrier = pltpu.get_barrier_semaphore()
    for i in range(1, LANES):
        pl.semaphore_signal(barrier, inc=1, device_id=plane_peer(i), device_id_type=MESH)
    for k in range(1, NZ):
        pl.semaphore_signal(barrier, inc=1, device_id=ring_peer(k), device_id_type=MESH)

    def pack_lists(slot, carry):
        for way, dst in ((0, zs_p), (1, zs_m)):
            at = lists[way, slot]
            dst[slot, 0] = keys[at]
            dst[slot, 1] = values[at]
        return carry

    lax.fori_loop(0, s1, pack_lists, 0)

    def own_slot(i):
        at = table[0, lax.rem(me_lane + i, LANES)]
        return keys[at], values[at]

    for i in range(1, LANES):
        yb[0, i, 0], yb[0, i, 1] = own_slot(i)
    here = me_z * LANES + me_lane
    yr[here, 0], yr[here, 1] = own_slot(0)

    pl.semaphore_wait(barrier, LANES - 1 + NZ - 1)

    segments = ((0, s4), (s4, s3), (s3, s2), (s2, s1))
    ring = (
        (zs_p, zr_p1, zr_p2, zr_p3),
        (zs_m, zr_m1, zr_m2, zr_m3),
    )
    ring_copies = {}

    def ring_start(way, q, hop):
        a, b = segments[q]
        if a == b:
            return
        src = ring[way][hop - 1].at[pl.ds(a, b - a)]
        if hop < HALF:
            dst = ring[way][hop].at[pl.ds(a, b - a)]
        else:
            dst = zr_4.at[pl.ds(way * s4 + a, b - a)]
        number = q * HALF + hop - 1
        copy = pltpu.make_async_remote_copy(
            src_ref=src,
            dst_ref=dst,
            send_sem=z_send.at[way, number],
            recv_sem=z_recv.at[way, number],
            device_id=ring_peer(1 if way == 0 else -1),
            device_id_type=MESH,
        )
        copy.start()
        ring_copies[way, q, hop] = copy

    def ring_arrived(way, q, hop):
        if (way, q, hop) in ring_copies:
            ring_copies[way, q, hop].wait_recv()

    def hand_on(q, hop):
        for way in range(2):
            ring_arrived(way, q, hop)
            ring_start(way, q, hop + 1)

    arrivals = {1: zr_p1, 2: zr_p2, 3: zr_p3, 4: zr_4, 5: zr_m3, 6: zr_m2, 7: zr_m1}
    plane_copies = {}
    order = (0, 1, 7, 2, 6, 3, 5, 4)
    depth = yb.shape[0]

    def plane_pack(b):
        at = order.index(b)
        if at >= depth:
            for i in range(1, LANES):
                plane_copies[order[at - depth], i].wait_send()
        source = lax.rem(me_z + (NZ - b), NZ) * LANES + me_lane
        got = arrivals[b]
        for i in range(LANES):
            slot = table[b, lax.rem(me_lane + i, LANES)]
            if i == 0:
                yr[source] = got[slot]
            else:
                yb[at % depth, i] = got[slot]

    def plane_start(b):
        at = order.index(b)
        source = lax.rem(me_z + (NZ - b), NZ) * LANES + me_lane
        for i in range(1, LANES):
            copy = pltpu.make_async_remote_copy(
                src_ref=yb.at[at % depth, i],
                dst_ref=yr.at[source],
                send_sem=y_send.at[b, i],
                recv_sem=y_recv.at[b, i],
                device_id=plane_peer(i),
                device_id_type=MESH,
            )
            copy.start()
            plane_copies[b, i] = copy

    def share(buffer, number, at, peer, count):
        copies = []
        for i in range(1, count):
            copy = pltpu.make_async_remote_copy(
                src_ref=buffer.at[at],
                dst_ref=buffer.at[at],
                send_sem=s_send.at[number, i],
                recv_sem=s_recv.at[number, i],
                device_id=peer(i),
                device_id_type=MESH,
            )
            copy.start()
            copies.append(copy)
        return copies

    def settle(copies):
        for copy in copies:
            copy.wait()

    for q in range(HALF):
        for way in range(2):
            ring_start(way, q, 1)
    plane_start(0)

    def widen(c, carry):
        kf[pl.ds(pl.multiple_of(c * 256, 256), 256), :] = keys[c].astype(F32)
        return carry

    lax.fori_loop(0, 32, widen, 0)
    live_here = local_live[0]
    rows = lax.broadcasted_iota(I32, (256, 256), 0)
    columns = lax.broadcasted_iota(I32, (256, 256), 1)

    def score(i, carry):
        g, c = i // 8, lax.rem(i, 8)
        chunk = kf[pl.ds(c * 1024 + g, 256, stride=4), :].astype(BF16)
        live = lax.broadcasted_iota(I32, (256, 128), 0) + c * 256 < live_here
        bias = jnp.where(live, 0.0, FAR)
        logits = contract_last(chunk, queries[g]) + jnp.concatenate([bias] * 5, axis=1)
        largest = jnp.max(logits, axis=0, keepdims=True)
        weights = jnp.exp2((logits - largest) * scale2)
        chunk_max[pl.ds(i, 1), :] = largest
        chunk_sum[pl.ds(i, 1), :] = jnp.sum(weights, axis=0, keepdims=True)
        probs[i] = weights.astype(BF16)
        gram = contract_last(chunk, chunk)
        on_diagonal = jnp.where(rows == columns, gram, 0.0)
        across = jnp.sum(on_diagonal, axis=0, keepdims=True)
        down = jnp.sum(on_diagonal, axis=1, keepdims=True)
        spread = jnp.where(live[:, :1], 1.0, 0.0) / jnp.sqrt(down + NORM_EPS)
        norm = jnp.sqrt(across + NORM_EPS)
        together = jnp.where(rows // BLOCK == columns // BLOCK, gram, 0.0)
        row_sum = jnp.sum(together * spread, axis=0, keepdims=True) / norm
        own = aux[pl.ds(c, 1), :] * across / (norm * norm)
        redundancy[pl.ds(i, 1), :] = (row_sum - own) / aux[pl.ds(c + 8, 1), :]
        return carry

    lax.fori_loop(0, 32, score, 0)

    def decode_logits(c, top):
        chunk = keys[pl.ds(c * 4, 4)].reshape(1024, 128)
        found = contract_last(step_queries[...], chunk)
        found = found + jnp.concatenate([head_bias[...]] * 8, axis=1) + kept_bias[pl.ds(c, 1), :]
        dl[c] = found
        for part in range(8):
            top = jnp.maximum(top, found[:, part * 128 : (part + 1) * 128])
        return top

    new_logits = contract_last(step_queries[...], new_keys[...]) + new_bias[...]
    top = lax.fori_loop(0, 8, decode_logits, new_logits)
    step_top = column_to_row(jnp.max(top, axis=1, keepdims=True))

    maxima, sums = [], []
    for g in range(4):
        part_max = chunk_max[g * 8 : g * 8 + 8, :]
        largest = jnp.max(part_max, axis=0, keepdims=True)
        maxima.append(largest)
        sums.append(
            jnp.sum(
                chunk_sum[g * 8 : g * 8 + 8, :] * jnp.exp2((part_max - largest) * scale2),
                axis=0,
                keepdims=True,
            )
        )
    stat_plane[me_lane, :, :640] = jnp.concatenate(maxima + sums, axis=0)
    stat_plane[me_lane, :, 640:] = jnp.broadcast_to(step_top, (8, 128))
    stats = share(stat_plane, 0, me_lane, plane_peer, LANES)
    hand_on(0, 1)

    def merged(buffer, count):
        largest = buffer[0, :4, :640]
        step_max = buffer[0, :, 640:]
        for k in range(1, count):
            largest = jnp.maximum(largest, buffer[k, :4, :640])
            step_max = jnp.maximum(step_max, buffer[k, :, 640:])
        total = jnp.zeros((4, 640), F32)
        for k in range(count):
            total = total + buffer[k, 4:, :640] * jnp.exp2(
                (buffer[k, :4, :640] - largest) * scale2
            )
        return largest, total, step_max

    settle(stats)
    largest, total, step_max = merged(stat_plane, LANES)
    stat_ring[me_z, :, :640] = jnp.concatenate([largest, total], axis=0)
    stat_ring[me_z, :, 640:] = step_max
    stats = share(stat_ring, 1, me_z, ring_peer, NZ)
    hand_on(1, 1)
    hand_on(2, 1)
    for way in range(2):
        ring_arrived(way, 3, 1)
    plane_pack(1)
    plane_pack(7)
    plane_start(1)
    plane_start(7)
    hand_on(0, 2)

    settle(stats)
    row_max, row_total, step_max = merged(stat_ring, NZ)
    step_column = row_to_column(step_max[:1, :], STEP_ROWS)

    def decode_sum(c, carry):
        weighted, total = carry
        part = jnp.exp2((dl[c] - step_column) * scale2)
        for piece in range(8):
            total = total + part[:, piece * 128 : (piece + 1) * 128]
        chunk = values[pl.ds(c * 4, 4)].reshape(1024, 128)
        weighted = weighted + jnp.dot(part.astype(BF16), chunk, preferred_element_type=F32)
        return weighted, total

    nothing = jnp.zeros((STEP_ROWS, 128), F32)
    weighted, total = lax.fori_loop(0, 8, decode_sum, (nothing, nothing))
    sum_plane[me_lane, :STEP_ROWS, :] = weighted
    sum_plane[me_lane, STEP_ROWS:, :] = jnp.broadcast_to(
        column_to_row(jnp.sum(total, axis=1, keepdims=True)), (8, 128)
    )
    sums = share(sum_plane, 2, me_lane, plane_peer, LANES)
    hand_on(1, 2)
    for way in range(2):
        ring_arrived(way, 2, 2)
    plane_pack(2)
    plane_pack(6)
    plane_start(2)
    plane_start(6)
    hand_on(0, 3)

    settle(sums)
    total = sum_plane[0]
    for k in range(1, LANES):
        total = total + sum_plane[k]
    sum_ring[me_z] = total
    sums = share(sum_ring, 3, me_z, ring_peer, NZ)

    for g in range(4):
        factor = (
            jnp.exp2((chunk_max[g * 8 : g * 8 + 8, :] - row_max[g : g + 1]) * scale2)
            / row_total[g : g + 1]
        )
        high = factor.astype(BF16)
        low = (factor - high.astype(F32)).astype(BF16)
        rescale[g] = jnp.concatenate([high.astype(F32), low.astype(F32)], axis=0).astype(BF16)

    def importance(i, carry):
        g, c = i // 8, lax.rem(i, 8)
        found = contract_last(rescale[g], probs[i])
        wanted = lax.rem(lax.broadcasted_iota(I32, (16, 256), 0), 8) == c
        found = jnp.sum(jnp.where(wanted, found, 0.0), axis=0, keepdims=True)
        value = (LAMBDA * aux[16:17, :]) * found - (1.0 - LAMBDA) * redundancy[pl.ds(i, 1), :]
        redundancy[pl.ds(i, 1), :] = jnp.where(aux[pl.ds(c, 1), :] > 0.5, value, 0.0)
        return carry

    lax.fori_loop(0, 32, importance, 0)
    for g in range(4):
        for c in range(8):
            out_scores[g : g + 1, c * 256 : (c + 1) * 256] = redundancy[g * 8 + c : g * 8 + c + 1, :]

    for way in range(2):
        ring_arrived(way, 1, 3)
    plane_pack(3)
    plane_pack(5)
    plane_start(3)
    plane_start(5)

    settle(sums)
    total = sum_ring[0]
    for k in range(1, NZ):
        total = total + sum_ring[k]
    fresh = jnp.exp2((new_logits - step_column) * scale2)
    weighted = total[:STEP_ROWS] + jnp.dot(
        fresh.astype(BF16), new_values[...], preferred_element_type=F32
    )
    bottom = row_to_column(total[STEP_ROWS : STEP_ROWS + 1, :], STEP_ROWS)
    bottom = bottom + jnp.sum(fresh, axis=1, keepdims=True)
    out_decoded[...] = (weighted / bottom).astype(BF16)

    for way in range(2):
        ring_arrived(way, 0, 4)
    plane_pack(4)
    plane_start(4)

    for b in order:
        for i in range(1, LANES):
            plane_copies[b, i].wait_recv()

    def unpack(j, carry):
        at = picks[j]
        out_keys[j] = yr[at, 0]
        out_values[j] = yr[at, 1]
        return carry

    lax.fori_loop(0, out_keys.shape[0], unpack, 0)
    for b in order[-depth:]:
        for i in range(1, LANES):
            plane_copies[b, i].wait_send()
    for copy in ring_copies.values():
        copy.wait_send()


def build(slots, collective_id, scale2, keep):
    s1, s2, s3, s4 = slots
    slot = (2, 256, 128)

    def buffers(count):
        return pltpu.VMEM((count, *slot), BF16)

    vmem, smem = pl.BlockSpec(memory_space=pltpu.VMEM), pl.BlockSpec(memory_space=pltpu.SMEM)
    return pl.pallas_call(
        functools.partial(exchange, slots, scale2),
        out_shape=(
            jax.ShapeDtypeStruct((4, 2048), F32),
            jax.ShapeDtypeStruct((keep, 256, 128), BF16),
            jax.ShapeDtypeStruct((keep, 256, 128), BF16),
            jax.ShapeDtypeStruct((STEP_ROWS, 128), BF16),
        ),
        in_specs=[smem] * 4 + [vmem] * 10,
        out_specs=(vmem,) * 4,
        scratch_shapes=[
            buffers(s1),
            buffers(s1),
            buffers(s1),
            buffers(s2),
            buffers(s3),
            buffers(s1),
            buffers(s2),
            buffers(s3),
            buffers(2 * s4),
            pltpu.VMEM((4, LANES, *slot), BF16),
            buffers(NZ * LANES),
            pltpu.VMEM((8192, 128), F32),
            pltpu.VMEM((32, 256, 640), BF16),
            pltpu.VMEM((32, 640), F32),
            pltpu.VMEM((32, 640), F32),
            pltpu.VMEM((32, 256), F32),
            pltpu.VMEM((8, STEP_ROWS, 1024), F32),
            pltpu.VMEM((4, 16, 640), BF16),
            pltpu.VMEM((LANES, 8, 768), F32),
            pltpu.VMEM((NZ, 8, 768), F32),
            pltpu.VMEM((LANES, STEP_ROWS + 8, 128), F32),
            pltpu.VMEM((NZ, STEP_ROWS + 8, 128), F32),
            pltpu.SemaphoreType.DMA((2, 16)),
            pltpu.SemaphoreType.DMA((2, 16)),
            pltpu.SemaphoreType.DMA((NZ, LANES)),
            pltpu.SemaphoreType.DMA((NZ, LANES)),
            pltpu.SemaphoreType.DMA((4, 8)),
            pltpu.SemaphoreType.DMA((4, 8)),
        ],
        compiler_params=pltpu.CompilerParams(
            collective_id=collective_id,
            has_side_effects=True,
            vmem_limit_bytes=67_043_328,
        ),
        name="exchange_%d" % s1,
    )


def send_plan(keep_row, owner_row, me_z, me_lane):
    owners = jnp.arange(NZ * LANES, dtype=I32)
    match = owner_row[None, :] == owners[:, None]
    has = jnp.any(match, axis=1).astype(I32).reshape(NZ, LANES)
    block = jnp.sum(jnp.where(match, keep_row[None, :], 0), axis=1).reshape(NZ, LANES)
    turn = (lax.broadcasted_iota(I32, (NZ, NZ), 0) + me_z) % NZ == lax.broadcasted_iota(
        I32, (NZ, NZ), 1
    )
    has = jnp.sum(jnp.where(turn[:, :, None], has[None], 0), axis=1)
    block = jnp.sum(jnp.where(turn[:, :, None], block[None], 0), axis=1)
    lower = (
        lax.broadcasted_iota(I32, (LANES, LANES), 0) < lax.broadcasted_iota(I32, (LANES, LANES), 1)
    )
    rank = jnp.sum(jnp.where(lower[None], has[:, :, None], 0), axis=1)
    count = jnp.sum(has, axis=1)
    n4 = count[HALF]
    ahead = count[1] + count[2] + count[3]
    behind = count[7] + count[6] + count[5]
    first = jnp.clip((n4 + behind - ahead + 1) // 2, jnp.maximum(n4 - 4, 0), jnp.minimum(n4, 4))
    tails_p = [first]
    tails_m = [n4 - first]
    for k in (3, 2, 1):
        tails_p.append(tails_p[-1] + count[k])
        tails_m.append(tails_m[-1] + count[NZ - k])
    tails = jnp.maximum(jnp.stack(tails_p[::-1]), jnp.stack(tails_m[::-1]))
    start = jnp.stack(
        [
            jnp.zeros((), I32),
            tails_p[2],
            tails_p[1],
            tails_p[0],
            jnp.zeros((), I32),
            tails_m[0],
            tails_m[1],
            tails_m[2],
        ]
    )
    position = start[:, None] + rank
    far = lax.broadcasted_iota(I32, (NZ, LANES), 0) == HALF
    k_of = lax.broadcasted_iota(I32, (NZ, LANES), 0)
    over = far & (rank >= first)
    position = jnp.where(over, rank - first, position)
    way = (k_of > HALF) | over
    used = (has > 0) & (k_of > 0)
    return has, block, position, way, used, tails


def shards(
    stored_keys,
    stored_values,
    observed_queries,
    decoded_queries,
    step_keys,
    decoded_values,
    keep_lists,
    owner_ids,
    cache_length,
):
    tokens, head_count, width = stored_keys.shape
    window = observed_queries.shape[0]
    group = observed_queries.shape[1] // head_count
    step_count = decoded_queries.shape[0]
    keep = keep_lists.shape[1]
    scale2 = math.log2(math.e) / math.sqrt(width)
    me_z = lax.axis_index("ctx_0")
    me_lane = lax.axis_index("ctx_1") * 2 + lax.axis_index("ctx_2")
    rank = me_z * LANES + me_lane
    keep_row, owner_row = keep_lists[0], owner_ids[0]

    has, block, position, way, used, tails = send_plan(keep_row, owner_row, me_z, me_lane)
    slot_numbers = jnp.arange(FITS_ALL[0], dtype=I32)
    lists = jnp.stack(
        [
            jnp.sum(
                jnp.where(
                    (used & (way == bool(w)))[None] & (position[None] == slot_numbers[:, None, None]),
                    block[None],
                    0,
                ),
                axis=(1, 2),
            )
            for w in range(2)
        ]
    )
    coded = jnp.where(has > 0, position + 1 + jnp.where((way & (position >= 0)), 32, 0), 0)
    back = (lax.broadcasted_iota(I32, (NZ, NZ), 0) + (NZ - me_z)) % NZ == lax.broadcasted_iota(
        I32, (NZ, NZ), 1
    )
    coded = jnp.sum(jnp.where(back[:, :, None], coded[None], 0), axis=1)
    row = jnp.concatenate([coded, jnp.broadcast_to(tails[None], (NZ, 4))], axis=1)
    row = jnp.broadcast_to(row[None, :, None, :], (2, NZ, LANES, 12)).reshape(2 * NZ * LANES, 12)
    got = lax.all_to_all(row, BATCH_CTX, 0, 0, tiled=True)
    most = jnp.max(got[:, LANES:], axis=0)
    mine = lax.dynamic_slice(got, (lax.axis_index("batch") * (NZ * LANES), 0), (NZ * LANES, LANES))
    valid = lax.dynamic_slice(mine, (0, me_lane), (NZ * LANES, 1))[:, 0] > 0
    before = jnp.arange(NZ * LANES)[:, None] < jnp.arange(NZ * LANES)[None, :]
    order = jnp.sum((before & valid[:, None]).astype(I32), axis=0)
    chosen = valid[None, :] & (order[None, :] == jnp.arange(keep, dtype=I32)[:, None])
    picks = jnp.sum(jnp.where(chosen, jnp.arange(NZ * LANES, dtype=I32)[None, :], 0), axis=1)
    my_ring = lax.dynamic_slice(
        mine.reshape(NZ, LANES, LANES), (0, me_lane, 0), (NZ, 1, LANES)
    )[:, 0]
    steps_back = (me_z + NZ - lax.broadcasted_iota(I32, (NZ, NZ), 0)) % NZ == lax.broadcasted_iota(
        I32, (NZ, NZ), 1
    )
    ring_rows = jnp.sum(jnp.where(steps_back[:, :, None], my_ring[None], 0), axis=1)

    seq = cache_length[0]
    base = rank * tokens
    local_live = (seq - base).reshape(1)
    at = base + jnp.arange(tokens, dtype=I32)
    live = (at < seq).astype(F32).reshape(8, 256)
    in_block = jnp.clip(seq - at // BLOCK * BLOCK, 0, BLOCK).astype(F32).reshape(8, 256)
    factor = jnp.broadcast_to(
        (seq.astype(F32) / (window * group)).reshape(1, 1), (8, 256)
    )
    aux = jnp.concatenate([live, jnp.maximum(in_block - 1.0, 1.0), factor], axis=0)
    blocks = tokens // BLOCK
    wide = jnp.arange(tokens * head_count, dtype=I32)
    kept = jnp.any(keep_row[None, :] == (wide // (BLOCK * head_count))[:, None], axis=1)
    kept_bias = jnp.where(kept & (base + wide // head_count < seq), 0.0, FAR).reshape(8, 1024)
    row_of = jnp.arange(STEP_ROWS, dtype=I32)[:, None]
    lane_of = jnp.arange(128, dtype=I32)[None, :]
    row_head, row_step = row_of // (step_count * group), row_of % (step_count * group) // group
    same_head = lane_of % head_count == row_head
    head_bias = jnp.where(same_head, 0.0, FAR).astype(F32)
    new_bias = jnp.where(
        same_head & (lane_of // head_count <= row_step) & (lane_of < step_count * head_count),
        0.0,
        FAR,
    ).astype(F32)

    def by_head(q):
        n = q.shape[0]
        q = q.reshape(n, head_count, group, width).transpose(1, 0, 2, 3)
        return q.reshape(head_count, n * group, width)

    queries = by_head(observed_queries)
    step_queries = by_head(decoded_queries).reshape(STEP_ROWS, width)

    def padded(rows):
        flat = rows.reshape(step_count * head_count, width)
        return jnp.pad(flat, ((0, 128 - step_count * head_count), (0, 0)))

    new_keys, new_values = padded(step_keys), padded(decoded_values)
    key_blocks = stored_keys.reshape(blocks, BLOCK * head_count, width)
    value_blocks = stored_values.reshape(blocks, BLOCK * head_count, width)

    def run(slots, collective_id):
        def call():
            second = ring_rows > 32
            place = jnp.where(second, ring_rows - 33, jnp.maximum(ring_rows - 1, 0))
            is_far = lax.broadcasted_iota(I32, (NZ, LANES), 0) == HALF
            place = place + jnp.where(second & is_far, slots[3], 0)
            is_own = lax.broadcasted_iota(I32, (NZ, LANES), 0) == 0
            own = lax.broadcast_in_dim(block[0], (NZ, LANES), (1,))
            table = jnp.where(is_own, own, place)
            return build(slots, collective_id, scale2, keep)(
                table,
                lists,
                picks,
                local_live,
                key_blocks,
                value_blocks,
                queries,
                step_queries,
                new_keys,
                new_values,
                kept_bias,
                head_bias,
                new_bias,
                aux,
            )

        return call

    fits = jnp.all(most <= jnp.array(FITS_MOST, I32))
    scores, kept_keys, kept_values, decoded = lax.cond(
        fits, run(FITS_MOST, 0), run(FITS_ALL, 1)
    )
    decoded = (
        decoded.reshape(head_count, step_count, group, width)
        .transpose(1, 0, 2, 3)
        .reshape(step_count, head_count * group, width)
    )
    shape = (keep * BLOCK, head_count, width)
    return scores, kept_keys.reshape(shape), kept_values.reshape(shape), decoded


def solution(mesh):
    split = Mesh(
        mesh.devices.reshape(mesh.shape["batch"], 8, 4, 2, mesh.shape["head"]),
        ("batch", "ctx_0", "ctx_1", "ctx_2", "head"),
    )
    return jax.shard_map(
        shards,
        mesh=split,
        in_specs=(
            P(BATCH_CTX, "head", None),
            P(BATCH_CTX, "head", None),
            P("batch", "head", None),
            P("batch", "head", None),
            P("batch", "head", None),
            P("batch", "head", None),
            P(BATCH_CTX, None),
            P(BATCH_CTX, None),
            P("batch"),
        ),
        out_specs=(
            P(("batch", "head"), CTX),
            P(BATCH_CTX, "head", None),
            P(BATCH_CTX, "head", None),
            P("batch", "head", None),
        ),
        check_vma=False,
    )
```

```python
import functools
import math

import jax
import jax.numpy as jnp
from jax import lax
from jax.experimental import pallas as pl
from jax.experimental.pallas import tpu as pltpu
from jax.sharding import Mesh
from jax.sharding import PartitionSpec as P

BLOCK = 64
CTX = ("ctx_0", "ctx_1", "ctx_2")
BATCH_CTX = ("batch", "ctx_0", "ctx_1", "ctx_2")
MESH = pl.DeviceIdType.MESH
FAR = -1e30
LAMBDA = 0.1
NORM_EPS = 1e-06
NZ = 8
LANES = 8
HALF = NZ // 2
HEADS = 4
GROUP = 5
STEPS = 4
HEAD_ROWS = HEADS * GROUP
STEP_ROWS = STEPS * HEAD_ROWS
WINDOW = 128
KEEP = 26
BLOCKS = 32
SECOND = 32
FITS_ALL = (26, 20, 12, 4)
FITS_MOST = (17, 13, 10, 4)
F32, BF16, I32 = jnp.float32, jnp.bfloat16, jnp.int32


def contract_last(a, b):
    return lax.dot_general(a, b, (((1,), (1,)), ((), ())), preferred_element_type=F32)


def row_to_column(row, rows):
    return jnp.transpose(jnp.broadcast_to(row, (128, 128)))[:rows, :1]


def column_to_row(column):
    rows = column.shape[0]
    wide = jnp.concatenate(
        [jnp.broadcast_to(column, (rows, 128)), jnp.zeros((128 - rows, 128), F32)], axis=0
    )
    return jnp.transpose(wide)[:1, :]


def plan(keep, owner, lists, own, kept, meta, block_of):
    me_z = lax.axis_index("ctx_0")
    for o in range(NZ * LANES):
        block_of[o] = -1
    for b in range(BLOCKS):
        kept[b] = 0
    for slot in range(SECOND):
        lists[0, slot] = 0
        lists[1, slot] = 0

    def place(j, carry):
        block_of[owner[0, j]] = keep[0, j]
        kept[keep[0, j]] = 1
        return carry

    lax.fori_loop(0, KEEP, place, 0)
    planes = [lax.rem(me_z + k, NZ) for k in range(NZ)]
    blocks = [[block_of[planes[k] * LANES + i] for i in range(LANES)] for k in range(NZ)]
    has = [[(b >= 0).astype(I32) for b in row] for row in blocks]
    count = [sum(row[1:], row[0]) for row in has]
    n4 = count[HALF]
    ahead, behind = count[1] + count[2] + count[3], count[7] + count[6] + count[5]
    first = lax.max(n4 - 4, lax.min(lax.min(n4, 4), lax.max(0, (n4 + behind - ahead + 1) >> 1)))
    first = lax.max(first, 0)
    second = n4 - first
    tails_p = [first, first + count[3], first + count[3] + count[2], first + ahead]
    tails_m = [second, second + count[5], second + count[5] + count[6], second + behind]
    start = [0, tails_p[2], tails_p[1], tails_p[0], 0, tails_m[0], tails_m[1], tails_m[2]]
    needs = [lax.max(p, m) for p, m in zip(tails_p[::-1], tails_m[::-1])]
    for k in range(NZ):
        rank = start[k] + jnp.zeros((), I32)
        for i in range(LANES):
            if k == HALF:
                way = (rank >= first).astype(I32)
                slot = rank - way * first
            else:
                way = jnp.full((), int(k > HALF), I32)
                slot = rank
            there = has[k][i]
            meta[planes[k], i] = there * (slot + 1 + way * SECOND)
            if k == 0:
                own[i] = lax.max(blocks[k][i], 0)
            else:

                @pl.when(there > 0)
                def _(way=way, slot=slot, block=blocks[k][i]):
                    lists[way, slot] = block

            rank = rank + there
        for n in range(4):
            meta[k, LANES + n] = needs[n]


def exchange(
    slots,
    scale2,
    lists,
    own,
    kept,
    length,
    meta,
    keys,
    values,
    queries,
    step_queries,
    new_keys,
    new_values,
    out_scores,
    out_decoded,
    out_meta,
    out_needs,
    yr_k,
    yr_v,
    zs_p,
    zs_m,
    zr_p1,
    zr_p2,
    zr_p3,
    zr_m1,
    zr_m2,
    zr_m3,
    zr_4,
    yb,
    kf,
    probs,
    chunk_max,
    chunk_sum,
    redundancy,
    dl,
    rescale,
    meta_ring,
    needs_pair,
    table,
    stat_plane,
    stat_ring,
    sum_plane,
    sum_ring,
    z_send,
    z_recv,
    y_send,
    y_recv,
    s_send,
    s_recv,
    t_sem,
):
    me_b = lax.axis_index("batch")
    me_z = lax.axis_index("ctx_0")
    me_lane = lax.axis_index("ctx_1") * 2 + lax.axis_index("ctx_2")
    s1, s2, s3, s4 = slots
    stores = (keys, values)
    results = (yr_k, yr_v)

    def ring_peer(k):
        return {"ctx_0": lax.rem(me_z + (k + NZ), NZ)}

    def plane_peer(i):
        lane = lax.rem(me_lane + i, LANES)
        return {"ctx_1": lane // 2, "ctx_2": lax.rem(lane, 2)}

    def pair_peer(i):
        return {"batch": 1 - me_b}

    barrier = pltpu.get_barrier_semaphore()
    for i in range(1, LANES):
        pl.semaphore_signal(barrier, inc=1, device_id=plane_peer(i), device_id_type=MESH)
    for k in range(1, NZ):
        pl.semaphore_signal(barrier, inc=1, device_id=ring_peer(k), device_id_type=MESH)
    pl.semaphore_signal(barrier, inc=1, device_id=pair_peer(0), device_id_type=MESH)

    def pack_lists(slot, carry):
        for way, dst in ((0, zs_p), (1, zs_m)):
            at = lists[way, slot]
            for kind in range(2):
                dst[kind][slot] = stores[kind][at]
        return carry

    lax.fori_loop(0, s1, pack_lists, 0)
    for i in range(LANES):
        at = own[lax.rem(me_lane + i, LANES)]
        for kind in range(2):
            yb[kind, 0, i] = stores[kind][at]
    meta_ring[me_z] = meta[me_z]

    pl.semaphore_wait(barrier, LANES - 1 + NZ - 1 + 1)

    def share(source, buffer, number, at, peer, count):
        copies = []
        for i in range(1, count):
            copy = pltpu.make_async_remote_copy(
                src_ref=source(i),
                dst_ref=buffer.at[at],
                send_sem=s_send.at[number, i],
                recv_sem=s_recv.at[number, i],
                device_id=peer(i),
                device_id_type=MESH,
            )
            copy.start()
            copies.append(copy)
        return copies

    def settle(copies):
        for copy in copies:
            copy.wait()

    metas = share(
        lambda k: meta.at[lax.rem(me_z + k, NZ)], meta_ring, 4, me_z, ring_peer, NZ
    )

    segments = ((0, s4), (s4, s3), (s3, s2), (s2, s1))
    ring = ((zs_p, zr_p1, zr_p2, zr_p3), (zs_m, zr_m1, zr_m2, zr_m3))
    ring_copies = {}

    def ring_start(kind, way, q, hop):
        a, b = segments[q]
        if a == b:
            return
        src = ring[way][hop - 1][kind].at[pl.ds(a, b - a)]
        if hop < HALF:
            dst = ring[way][hop][kind].at[pl.ds(a, b - a)]
        else:
            dst = zr_4[kind].at[pl.ds(way * s4 + a, b - a)]
        number = q * HALF + hop - 1
        copy = pltpu.make_async_remote_copy(
            src_ref=src,
            dst_ref=dst,
            send_sem=z_send.at[kind, way, number],
            recv_sem=z_recv.at[kind, way, number],
            device_id=ring_peer(1 if way == 0 else -1),
            device_id_type=MESH,
        )
        copy.start()
        ring_copies[kind, way, q, hop] = copy

    def arrived(kind, q, hop):
        for way in range(2):
            if (kind, way, q, hop) in ring_copies:
                ring_copies[kind, way, q, hop].wait_recv()

    def hand_on(kind, hop):
        for q in range(HALF - hop):
            for way in range(2):
                if (kind, way, q, hop) in ring_copies:
                    ring_copies[kind, way, q, hop].wait_recv()
                ring_start(kind, way, q, hop + 1)
        arrived(kind, HALF - hop, hop)

    arrivals = {1: zr_p1, 2: zr_p2, 3: zr_p3, 4: zr_4, 5: zr_m3, 6: zr_m2, 7: zr_m1}
    plane_copies = {}

    def plane_pack(kind, b):
        source = lax.rem(me_z + (NZ - b), NZ)
        got = arrivals[b][kind]
        for i in range(LANES):
            code = table[source, 0, lax.rem(me_lane + i, LANES)]
            is_second = (code > SECOND).astype(I32)
            slot = lax.max(code - 1 - is_second * SECOND, 0)
            if b == HALF:
                slot = lax.min(slot, s4 - 1) + is_second * s4
            else:
                slot = lax.min(slot, got.shape[0] - 1)
            yb[kind, b, i] = got[slot]

    def plane_start(kind, b):
        source = lax.rem(me_z + (NZ - b), NZ) * LANES + me_lane
        for i in range(1, LANES):
            copy = pltpu.make_async_remote_copy(
                src_ref=yb.at[kind, b, i],
                dst_ref=results[kind].at[source],
                send_sem=y_send.at[kind, b, i],
                recv_sem=y_recv.at[kind, b, i],
                device_id=plane_peer(i),
                device_id_type=MESH,
            )
            copy.start()
            plane_copies[kind, b, i] = copy
        copy = pltpu.make_async_copy(
            yb.at[kind, b, 0], results[kind].at[source], y_send.at[kind, b, 0]
        )
        copy.start()
        plane_copies[kind, b, 0] = copy

    def across(kind, *batches):
        for b in batches:
            plane_pack(kind, b)
        for b in batches:
            plane_start(kind, b)

    for kind in range(2):
        for q in range(HALF):
            for way in range(2):
                ring_start(kind, way, q, 1)
    plane_start(0, 0)
    plane_start(1, 0)

    def widen(c, carry):
        kf[pl.ds(pl.multiple_of(c * 256, 256), 256), :] = keys[c].astype(F32)
        return carry

    lax.fori_loop(0, BLOCKS, widen, 0)
    live_here = length[0] - (me_z * LANES + me_lane) * (BLOCKS * BLOCK)
    rows = lax.broadcasted_iota(I32, (256, 256), 0)
    columns = lax.broadcasted_iota(I32, (256, 256), 1)
    lane_256 = lax.broadcasted_iota(I32, (1, 256), 1)

    def score(i, carry):
        g, c = i // 8, lax.rem(i, 8)
        chunk = kf[pl.ds(c * 1024 + g, 256, stride=4), :].astype(BF16)
        live = lax.broadcasted_iota(I32, (256, 128), 0) + c * 256 < live_here
        bias = jnp.where(live, 0.0, FAR)
        logits = contract_last(chunk, queries[g]) + jnp.concatenate([bias] * 5, axis=1)
        largest = jnp.max(logits, axis=0, keepdims=True)
        weights = jnp.exp2((logits - largest) * scale2)
        chunk_max[pl.ds(i, 1), :] = largest
        chunk_sum[pl.ds(i, 1), :] = jnp.sum(weights, axis=0, keepdims=True)
        probs[i] = weights.astype(BF16)
        gram = contract_last(chunk, chunk)
        on_diagonal = jnp.where(rows == columns, gram, 0.0)
        squares = jnp.sum(on_diagonal, axis=0, keepdims=True)
        down = jnp.sum(on_diagonal, axis=1, keepdims=True)
        spread = jnp.where(live[:, :1], 1.0, 0.0) / jnp.sqrt(down + NORM_EPS)
        norm = jnp.sqrt(squares + NORM_EPS)
        together = jnp.where(rows // BLOCK == columns // BLOCK, gram, 0.0)
        row_sum = jnp.sum(together * spread, axis=0, keepdims=True) / norm
        live_lanes = jnp.where(lane_256 + c * 256 < live_here, 1.0, 0.0)
        own_term = live_lanes * squares / (norm * norm)
        in_block = jnp.clip(live_here - c * 256 - lane_256 // BLOCK * BLOCK, 0, BLOCK).astype(F32)
        redundancy[pl.ds(i, 1), :] = (row_sum - own_term) / jnp.maximum(in_block - 1.0, 1.0)
        return carry

    lax.fori_loop(0, HEADS * 8, score, 0)

    row_of = lax.broadcasted_iota(I32, (STEP_ROWS, 128), 0)
    lane_of = lax.broadcasted_iota(I32, (STEP_ROWS, 128), 1)
    row_step = row_of % STEPS
    row_head = jnp.zeros((STEP_ROWS, 128), I32)
    for g in range(1, HEADS):
        row_head = row_head + (row_of >= g * GROUP * STEPS).astype(I32)
    same_head = lane_of % HEADS == row_head
    head_bias = jnp.concatenate([jnp.where(same_head, 0.0, FAR)] * 8, axis=1)
    may_see = same_head & (lane_of // HEADS <= row_step) & (lane_of < STEPS * HEADS)
    new_bias = jnp.where(may_see, 0.0, FAR)

    def padded(ref):
        return jnp.concatenate([ref[...], jnp.zeros((128 - STEPS * HEADS, 128), BF16)], axis=0)

    def decode_logits(c, top):
        chunk = keys[pl.ds(c * 4, 4)].reshape(1024, 128)
        kept_part = jnp.concatenate(
            [
                jnp.where(jnp.full((1, 256), kept[c * 4 + part], I32) > 0, 0.0, FAR)
                for part in range(4)
            ],
            axis=1,
        )
        token = lax.broadcasted_iota(I32, (1, 1024), 1) // HEADS + c * 256
        bias = kept_part + jnp.where(token < live_here, 0.0, FAR)
        found = contract_last(step_queries[...], chunk) + head_bias + bias
        dl[c] = found
        for part in range(8):
            top = jnp.maximum(top, found[:, part * 128 : (part + 1) * 128])
        return top

    new_logits = contract_last(step_queries[...], padded(new_keys)) + new_bias
    top = lax.fori_loop(0, 8, decode_logits, new_logits)
    step_top = column_to_row(jnp.max(top, axis=1, keepdims=True))

    maxima, sums = [], []
    for g in range(HEADS):
        part_max = chunk_max[g * 8 : g * 8 + 8, :]
        largest = jnp.max(part_max, axis=0, keepdims=True)
        maxima.append(largest)
        sums.append(
            jnp.sum(
                chunk_sum[g * 8 : g * 8 + 8, :] * jnp.exp2((part_max - largest) * scale2),
                axis=0,
                keepdims=True,
            )
        )
    stat_plane[me_lane, :, :640] = jnp.concatenate(maxima + sums, axis=0)
    stat_plane[me_lane, :, 640:] = jnp.broadcast_to(step_top, (8, 128))

    settle(metas)
    to_scalars = pltpu.make_async_copy(meta_ring, table, t_sem)
    to_scalars.start()
    to_scalars.wait()
    out_meta[me_lane] = meta_ring[...]
    stats = share(lambda i: stat_plane.at[me_lane], stat_plane, 0, me_lane, plane_peer, LANES)
    metas = share(lambda i: meta_ring, out_meta, 5, me_lane, plane_peer, LANES)

    def merged(buffer, count):
        largest = buffer[0, :4, :640]
        step_max = buffer[0, :, 640:]
        for k in range(1, count):
            largest = jnp.maximum(largest, buffer[k, :4, :640])
            step_max = jnp.maximum(step_max, buffer[k, :, 640:])
        total = jnp.zeros((4, 640), F32)
        for k in range(count):
            total = total + buffer[k, 4:, :640] * jnp.exp2(
                (buffer[k, :4, :640] - largest) * scale2
            )
        return largest, total, step_max

    settle(stats)
    largest, total, step_max = merged(stat_plane, LANES)
    stat_ring[me_z, :, :640] = jnp.concatenate([largest, total], axis=0)
    stat_ring[me_z, :, 640:] = step_max
    stats = share(lambda k: stat_ring.at[me_z], stat_ring, 1, me_z, ring_peer, NZ)
    hand_on(0, 1)
    across(0, 1, 7)
    settle(metas)
    most = out_meta[0, 0]
    for lane in range(LANES):
        for z in range(NZ):
            most = jnp.maximum(most, out_meta[lane, z])
    needs_pair[me_b] = most
    pair = share(lambda i: needs_pair.at[me_b], needs_pair, 6, me_b, pair_peer, 2)
    hand_on(1, 1)
    across(1, 1, 7)

    settle(stats)
    row_max, row_total, step_max = merged(stat_ring, NZ)
    step_column = row_to_column(step_max[:1, :], STEP_ROWS)

    def decode_sum(c, carry):
        weighted, total = carry
        part = jnp.exp2((dl[c] - step_column) * scale2)
        for piece in range(8):
            total = total + part[:, piece * 128 : (piece + 1) * 128]
        chunk = values[pl.ds(c * 4, 4)].reshape(1024, 128)
        weighted = weighted + jnp.dot(part.astype(BF16), chunk, preferred_element_type=F32)
        return weighted, total

    nothing = jnp.zeros((STEP_ROWS, 128), F32)
    weighted, total = lax.fori_loop(0, 8, decode_sum, (nothing, nothing))
    sum_plane[me_lane, :STEP_ROWS, :] = weighted
    sum_plane[me_lane, STEP_ROWS:, :] = jnp.broadcast_to(
        column_to_row(jnp.sum(total, axis=1, keepdims=True)), (8, 128)
    )
    sums = share(lambda i: sum_plane.at[me_lane], sum_plane, 2, me_lane, plane_peer, LANES)
    hand_on(0, 2)
    across(0, 2, 6)
    settle(sums)
    total = sum_plane[0]
    for k in range(1, LANES):
        total = total + sum_plane[k]
    sum_ring[me_z] = total
    sums = share(lambda k: sum_ring.at[me_z], sum_ring, 3, me_z, ring_peer, NZ)
    hand_on(1, 2)
    across(1, 2, 6)

    for g in range(HEADS):
        factor = (
            jnp.exp2((chunk_max[g * 8 : g * 8 + 8, :] - row_max[g : g + 1]) * scale2)
            / row_total[g : g + 1]
        )
        high = factor.astype(BF16)
        low = (factor - high.astype(F32)).astype(BF16)
        rescale[g] = jnp.concatenate([high.astype(F32), low.astype(F32)], axis=0).astype(BF16)
    share_of_row = jnp.full((1, 256), length[0], I32).astype(F32) / (WINDOW * GROUP)

    def importance(i, carry):
        g, c = i // 8, lax.rem(i, 8)
        found = contract_last(rescale[g], probs[i])
        wanted = lax.rem(lax.broadcasted_iota(I32, (16, 256), 0), 8) == c
        found = jnp.sum(jnp.where(wanted, found, 0.0), axis=0, keepdims=True)
        value = (LAMBDA * share_of_row) * found - (1.0 - LAMBDA) * redundancy[pl.ds(i, 1), :]
        live = lane_256 + c * 256 < live_here
        redundancy[pl.ds(i, 1), :] = jnp.where(live, value, 0.0)
        return carry

    lax.fori_loop(0, HEADS * 8, importance, 0)
    for g in range(HEADS):
        for c in range(8):
            out_scores[g : g + 1, c * 256 : (c + 1) * 256] = redundancy[g * 8 + c : g * 8 + c + 1, :]
    settle(pair)
    out_needs[...] = jnp.maximum(needs_pair[0], needs_pair[1])

    hand_on(0, 3)
    across(0, 3, 5)
    hand_on(1, 3)
    across(1, 3, 5)

    settle(sums)
    total = sum_ring[0]
    for k in range(1, NZ):
        total = total + sum_ring[k]
    fresh = jnp.exp2((new_logits - step_column) * scale2)
    weighted = total[:STEP_ROWS] + jnp.dot(
        fresh.astype(BF16), padded(new_values), preferred_element_type=F32
    )
    bottom = row_to_column(total[STEP_ROWS : STEP_ROWS + 1, :], STEP_ROWS)
    bottom = bottom + jnp.sum(fresh, axis=1, keepdims=True)
    out_decoded[...] = (weighted / bottom).astype(BF16)

    for kind in range(2):
        arrived(kind, 0, HALF)
        across(kind, HALF)

    for (kind, b, i), copy in plane_copies.items():
        copy.wait()
    for copy in ring_copies.values():
        copy.wait_send()


VMEM, SMEM = pl.BlockSpec(memory_space=pltpu.VMEM), pl.BlockSpec(memory_space=pltpu.SMEM)
ANY = pl.BlockSpec(memory_space=pl.ANY)


def run_plan(keep, owner):
    return pl.pallas_call(
        plan,
        out_shape=(
            jax.ShapeDtypeStruct((2, SECOND), I32),
            jax.ShapeDtypeStruct((LANES,), I32),
            jax.ShapeDtypeStruct((BLOCKS,), I32),
            jax.ShapeDtypeStruct((NZ, 128), I32),
        ),
        in_specs=[SMEM] * 2,
        out_specs=(SMEM,) * 4,
        scratch_shapes=[pltpu.SMEM((NZ * LANES,), I32)],
        name="plan",
    )(keep, owner)


def run_exchange(slots, collective_id, scale2, operands):
    s1, s2, s3, s4 = slots
    block = (BLOCKS * 8, 128)

    def buffers(count):
        return (pltpu.VMEM((count, *block), BF16),) * 2

    return pl.pallas_call(
        functools.partial(exchange, slots, scale2),
        out_shape=(
            jax.ShapeDtypeStruct((HEADS, BLOCKS * BLOCK), F32),
            jax.ShapeDtypeStruct((STEP_ROWS, 128), BF16),
            jax.ShapeDtypeStruct((LANES, NZ, 1, 128), I32),
            jax.ShapeDtypeStruct((1, 128), I32),
            jax.ShapeDtypeStruct((NZ * LANES, *block), BF16),
            jax.ShapeDtypeStruct((NZ * LANES, *block), BF16),
        ),
        in_specs=[SMEM] * 4 + [VMEM] * 7,
        out_specs=(VMEM,) * 4 + (ANY,) * 2,
        scratch_shapes=[
            buffers(s1),
            buffers(s1),
            buffers(s1),
            buffers(s2),
            buffers(s3),
            buffers(s1),
            buffers(s2),
            buffers(s3),
            buffers(2 * s4),
            pltpu.VMEM((2, NZ, LANES, *block), BF16),
            pltpu.VMEM((BLOCKS * 256, 128), F32),
            pltpu.VMEM((HEADS * 8, 256, WINDOW * GROUP), BF16),
            pltpu.VMEM((HEADS * 8, WINDOW * GROUP), F32),
            pltpu.VMEM((HEADS * 8, WINDOW * GROUP), F32),
            pltpu.VMEM((HEADS * 8, 256), F32),
            pltpu.VMEM((8, STEP_ROWS, 1024), F32),
            pltpu.VMEM((HEADS, 16, WINDOW * GROUP), BF16),
            pltpu.VMEM((NZ, 1, 128), I32),
            pltpu.VMEM((2, 1, 128), I32),
            pltpu.SMEM((NZ, 1, 128), I32),
            pltpu.VMEM((LANES, 8, 768), F32),
            pltpu.VMEM((NZ, 8, 768), F32),
            pltpu.VMEM((LANES, STEP_ROWS + 8, 128), F32),
            pltpu.VMEM((NZ, STEP_ROWS + 8, 128), F32),
            pltpu.SemaphoreType.DMA((2, 2, 16)),
            pltpu.SemaphoreType.DMA((2, 2, 16)),
            pltpu.SemaphoreType.DMA((2, NZ, LANES)),
            pltpu.SemaphoreType.DMA((2, NZ, LANES)),
            pltpu.SemaphoreType.DMA((8, 8)),
            pltpu.SemaphoreType.DMA((8, 8)),
            pltpu.SemaphoreType.DMA,
        ],
        compiler_params=pltpu.CompilerParams(
            collective_id=collective_id,
            has_side_effects=True,
            vmem_limit_bytes=67_043_328,
        ),
        name="exchange_%d" % s1,
    )(*operands)


def unpack(meta, came_k, came_v, out_k, out_v, picks, sems):
    me_lane = lax.axis_index("ctx_1") * 2 + lax.axis_index("ctx_2")

    def choose(source, found):
        z, lane = source // LANES, lax.rem(source, LANES)
        picks[found] = source
        return found + (meta[lane * NZ + z, me_lane] > 0).astype(I32)

    lax.fori_loop(0, NZ * LANES, choose, 0)

    def copies(j):
        at = picks[j]
        return (
            pltpu.make_async_copy(came_k.at[at], out_k.at[j], sems.at[0, j]),
            pltpu.make_async_copy(came_v.at[at], out_v.at[j], sems.at[1, j]),
        )

    def start(j, carry):
        for copy in copies(j):
            copy.start()
        return carry

    def wait(j, carry):
        for copy in copies(j):
            copy.wait()
        return carry

    lax.fori_loop(0, KEEP, start, 0)
    lax.fori_loop(0, KEEP, wait, 0)


def run_unpack(meta, came_k, came_v):
    shape = jax.ShapeDtypeStruct((KEEP, *came_k.shape[1:]), BF16)
    return pl.pallas_call(
        unpack,
        out_shape=(shape, shape),
        in_specs=[SMEM, ANY, ANY],
        out_specs=(VMEM, VMEM),
        scratch_shapes=[
            pltpu.SMEM((NZ * LANES + 1,), I32),
            pltpu.SemaphoreType.DMA((2, KEEP)),
        ],
        name="unpack",
    )(meta.reshape(NZ * LANES, 128), came_k, came_v)


def shards(
    stored_keys,
    stored_values,
    observed_queries,
    decoded_queries,
    step_keys,
    decoded_values,
    keep_lists,
    owner_ids,
    cache_length,
):
    tokens, head_count, width = stored_keys.shape
    scale2 = math.log2(math.e) / math.sqrt(width)
    lists, own, kept, meta = run_plan(keep_lists, owner_ids)
    operands = (
        lists,
        own,
        kept,
        cache_length,
        meta.reshape(NZ, 1, 128),
        stored_keys.reshape(BLOCKS, BLOCK * head_count, width),
        stored_values.reshape(BLOCKS, BLOCK * head_count, width),
        observed_queries.transpose(1, 0, 2).reshape(HEADS, GROUP * WINDOW, width),
        decoded_queries.transpose(1, 0, 2).reshape(STEP_ROWS, width),
        step_keys.reshape(STEPS * HEADS, width),
        decoded_values.reshape(STEPS * HEADS, width),
    )
    scores, decoded, came, needs, came_k, came_v = run_exchange(FITS_MOST, 0, scale2, operands)
    fits = jnp.all(needs[0, LANES : LANES + 4] <= jnp.array(FITS_MOST, I32))

    def done():
        return run_unpack(came, came_k, came_v)

    def again():
        _, _, came, _, came_k, came_v = run_exchange(FITS_ALL, 1, scale2, operands)
        return run_unpack(came, came_k, came_v)

    kept_keys, kept_values = lax.cond(fits, done, again)
    decoded = decoded.reshape(HEAD_ROWS, STEPS, width).transpose(1, 0, 2)
    shape = (KEEP * BLOCK, head_count, width)
    return scores, kept_keys.reshape(shape), kept_values.reshape(shape), decoded


def solution(mesh):
    split = Mesh(
        mesh.devices.reshape(mesh.shape["batch"], 8, 4, 2, mesh.shape["head"]),
        ("batch", "ctx_0", "ctx_1", "ctx_2", "head"),
    )
    return jax.shard_map(
        shards,
        mesh=split,
        in_specs=(
            P(BATCH_CTX, "head", None),
            P(BATCH_CTX, "head", None),
            P("batch", "head", None),
            P("batch", "head", None),
            P("batch", "head", None),
            P("batch", "head", None),
            P(BATCH_CTX, None),
            P(BATCH_CTX, None),
            P("batch"),
        ),
        out_specs=(
            P(("batch", "head"), CTX),
            P(BATCH_CTX, "head", None),
            P(BATCH_CTX, "head", None),
            P("batch", "head", None),
        ),
        check_vma=False,
    )
```

```python
import functools
import math

import jax
import jax.numpy as jnp
from jax import lax
from jax.experimental import pallas as pl
from jax.experimental.pallas import tpu as pltpu
from jax.sharding import Mesh
from jax.sharding import PartitionSpec as P

BLOCK = 64
CTX = ("ctx_0", "ctx_1", "ctx_2")
BATCH_CTX = ("batch", "ctx_0", "ctx_1", "ctx_2")
MESH = pl.DeviceIdType.MESH
FAR = -1e30
LAMBDA = 0.1
NORM_EPS = 1e-06
NZ = 8
LANES = 8
HALF = NZ // 2
HEADS = 4
GROUP = 5
STEPS = 4
HEAD_ROWS = HEADS * GROUP
STEP_ROWS = STEPS * HEAD_ROWS
WINDOW = 128
KEEP = 26
PARTS = 4
BLOCKS = 32
SECOND = 32
FITS_ALL = (26, 20, 12, 4)
FITS_MOST = (17, 13, 10, 4)
F32, BF16, I32 = jnp.float32, jnp.bfloat16, jnp.int32


def contract_last(a, b):
    return lax.dot_general(a, b, (((1,), (1,)), ((), ())), preferred_element_type=F32)


def row_to_column(row, rows):
    return jnp.transpose(jnp.broadcast_to(row, (128, 128)))[:rows, :1]


def column_to_row(column):
    rows = column.shape[0]
    wide = jnp.concatenate(
        [jnp.broadcast_to(column, (rows, 128)), jnp.zeros((128 - rows, 128), F32)], axis=0
    )
    return jnp.transpose(wide)[:1, :]


def plan(keep, owner, lists, own, kept, meta, block_of):
    me_z = lax.axis_index("ctx_0")
    for o in range(NZ * LANES):
        block_of[o] = -1
    for b in range(BLOCKS):
        kept[b] = 0
    for slot in range(SECOND):
        lists[0, slot] = 0
        lists[1, slot] = 0

    def place(j, carry):
        block_of[owner[0, j]] = keep[0, j]
        kept[keep[0, j]] = 1
        return carry

    lax.fori_loop(0, KEEP, place, 0)
    planes = [lax.rem(me_z + k, NZ) for k in range(NZ)]
    blocks = [[block_of[planes[k] * LANES + i] for i in range(LANES)] for k in range(NZ)]
    has = [[(b >= 0).astype(I32) for b in row] for row in blocks]
    count = [sum(row[1:], row[0]) for row in has]
    n4 = count[HALF]
    ahead, behind = count[1] + count[2] + count[3], count[7] + count[6] + count[5]
    first = lax.max(n4 - 4, lax.min(lax.min(n4, 4), lax.max(0, (n4 + behind - ahead + 1) >> 1)))
    first = lax.max(first, 0)
    second = n4 - first
    tails_p = [first, first + count[3], first + count[3] + count[2], first + ahead]
    tails_m = [second, second + count[5], second + count[5] + count[6], second + behind]
    start = [0, tails_p[2], tails_p[1], tails_p[0], 0, tails_m[0], tails_m[1], tails_m[2]]
    needs = [lax.max(p, m) for p, m in zip(tails_p[::-1], tails_m[::-1])]
    for k in range(NZ):
        rank = start[k] + jnp.zeros((), I32)
        for i in range(LANES):
            if k == HALF:
                way = (rank >= first).astype(I32)
                slot = rank - way * first
            else:
                way = jnp.full((), int(k > HALF), I32)
                slot = rank
            there = has[k][i]
            meta[planes[k], i] = there * (slot + 1 + way * SECOND)
            if k == 0:
                own[i] = lax.max(blocks[k][i], 0)
            else:

                @pl.when(there > 0)
                def _(way=way, slot=slot, block=blocks[k][i]):
                    lists[way, slot] = block

            rank = rank + there
        for n in range(4):
            meta[k, LANES + n] = needs[n]


def exchange(
    slots,
    scale2,
    lists,
    own,
    kept,
    length,
    meta,
    keys_in,
    values_in,
    queries,
    step_queries,
    new_keys,
    new_values,
    out_scores,
    out_decoded,
    out_meta,
    out_over,
    yr_k,
    yr_v,
    keys,
    values,
    in_sem,
    zs_p,
    zs_m,
    zr_p1,
    zr_p2,
    zr_p3,
    zr_m1,
    zr_m2,
    zr_m3,
    zr_4,
    yb,
    kf,
    probs,
    chunk_max,
    chunk_sum,
    redundancy,
    dl,
    rescale,
    meta_ring,
    needs_pair,
    table,
    stat_out,
    stat_plane,
    stat_ring,
    stat_all,
    sum_out,
    sum_plane,
    sum_ring,
    sum_all,
    z_send,
    z_recv,
    y_send,
    y_recv,
    s_send,
    s_recv,
    t_sem,
):
    me_b = lax.axis_index("batch")
    me_z = lax.axis_index("ctx_0")
    me_lane = lax.axis_index("ctx_1") * 2 + lax.axis_index("ctx_2")
    s1, s2, s3, s4 = slots
    halves = PARTS // 2
    rows_part = keys.shape[1] // halves

    def part_of(pair, part):
        return pair[part // halves], pl.ds(part % halves * rows_part, rows_part)

    def ring_peer(k):
        return {"ctx_0": lax.rem(me_z + (k + NZ), NZ)}

    def plane_peer(i):
        lane = lax.rem(me_lane + i, LANES)
        return {"ctx_1": lane // 2, "ctx_2": lax.rem(lane, 2)}

    def pair_peer(i):
        return {"batch": 1 - me_b}

    loads = [
        pltpu.make_async_copy(source, store, in_sem.at[kind])
        for kind, (source, store) in enumerate(((keys_in, keys), (values_in, values)))
    ]
    for load in loads:
        load.start()

    barrier = pltpu.get_barrier_semaphore()
    for i in range(1, LANES):
        pl.semaphore_signal(barrier, inc=1, device_id=plane_peer(i), device_id_type=MESH)
    for k in range(1, NZ):
        pl.semaphore_signal(barrier, inc=1, device_id=ring_peer(k), device_id_type=MESH)
    pl.semaphore_signal(barrier, inc=1, device_id=pair_peer(0), device_id_type=MESH)

    def pack(part):
        store, rows = part_of((keys, values), part)

        def fill(slot, carry):
            for way, dst in ((0, zs_p), (1, zs_m)):
                dst[part][slot] = store[lists[way, slot], rows]
            return carry

        lax.fori_loop(0, s1, fill, 0)

    def pack_own(part):
        store, rows = part_of((keys, values), part)
        for i in range(LANES):
            yb[part, 0, i] = store[own[lax.rem(me_lane + i, LANES)], rows]

    loads[0].wait()
    for part in range(halves):
        pack(part)
    meta_ring[me_z] = meta[me_z]
    pl.semaphore_wait(barrier, LANES - 1 + NZ - 1 + 1)

    def share(source, buffer, number, at, peer, count):
        copies = []
        for i in range(1, count):
            copy = pltpu.make_async_remote_copy(
                src_ref=source(i),
                dst_ref=buffer.at[at],
                send_sem=s_send.at[number, i],
                recv_sem=s_recv.at[number, i],
                device_id=peer(i),
                device_id_type=MESH,
            )
            copy.start()
            copies.append(copy)
        return copies

    def settle(copies):
        for copy in copies:
            copy.wait()

    metas = share(
        lambda k: meta.at[lax.rem(me_z + k, NZ)], meta_ring, 4, me_z, ring_peer, NZ
    )

    segments = ((0, s4), (s4, s3), (s3, s2), (s2, s1))
    ring = ((zs_p, zr_p1, zr_p2, zr_p3), (zs_m, zr_m1, zr_m2, zr_m3))
    ring_copies = {}

    def ring_start(part, way, q, hop):
        a, b = segments[q]
        if a == b:
            return
        src = ring[way][hop - 1][part].at[pl.ds(a, b - a)]
        if hop < HALF:
            dst = ring[way][hop][part].at[pl.ds(a, b - a)]
        else:
            dst = zr_4[part].at[pl.ds(way * s4 + a, b - a)]
        number = q * HALF + hop - 1
        copy = pltpu.make_async_remote_copy(
            src_ref=src,
            dst_ref=dst,
            send_sem=z_send.at[part, way, number],
            recv_sem=z_recv.at[part, way, number],
            device_id=ring_peer(1 if way == 0 else -1),
            device_id_type=MESH,
        )
        copy.start()
        ring_copies[part, way, q, hop] = copy

    def arrived(part, q, hop):
        for way in range(2):
            if (part, way, q, hop) in ring_copies:
                ring_copies[part, way, q, hop].wait_recv()

    def hand_on(part, hop):
        for q in range(HALF - hop):
            for way in range(2):
                if (part, way, q, hop) in ring_copies:
                    ring_copies[part, way, q, hop].wait_recv()
                ring_start(part, way, q, hop + 1)
        arrived(part, HALF - hop, hop)

    arrivals = {1: zr_p1, 2: zr_p2, 3: zr_p3, 4: zr_4, 5: zr_m3, 6: zr_m2, 7: zr_m1}
    plane_copies = {}

    def plane_pack(part, b):
        source = lax.rem(me_z + (NZ - b), NZ)
        got = arrivals[b][part]
        for i in range(LANES):
            code = table[source, 0, lax.rem(me_lane + i, LANES)]
            is_second = (code > SECOND).astype(I32)
            slot = lax.max(code - 1 - is_second * SECOND, 0)
            if b == HALF:
                slot = lax.min(slot, s4 - 1) + is_second * s4
            else:
                slot = lax.min(slot, got.shape[0] - 1)
            yb[part, b, i] = got[slot]

    def plane_start(part, b):
        result, rows = part_of((yr_k, yr_v), part)
        source = lax.rem(me_z + (NZ - b), NZ) * LANES + me_lane
        for i in range(1, LANES):
            copy = pltpu.make_async_remote_copy(
                src_ref=yb.at[part, b, i],
                dst_ref=result.at[source, rows],
                send_sem=y_send.at[part, b, i],
                recv_sem=y_recv.at[part, b, i],
                device_id=plane_peer(i),
                device_id_type=MESH,
            )
            copy.start()
            plane_copies[part, b, i] = copy
        copy = pltpu.make_async_copy(
            yb.at[part, b, 0], result.at[source, rows], y_send.at[part, b, 0]
        )
        copy.start()
        plane_copies[part, b, 0] = copy

    def across(part, *batches):
        for b in batches:
            plane_pack(part, b)
        for b in batches:
            plane_start(part, b)

    def ring_first(part, *parts):
        for q in parts:
            for way in range(2):
                ring_start(part, way, q, 1)

    every = range(HALF)
    for part in range(halves):
        ring_first(part, *every)
    loads[1].wait()
    for part in range(halves, PARTS):
        pack(part)
    for part in range(halves, PARTS - 1):
        ring_first(part, *every)
    for part in range(PARTS):
        pack_own(part)
    for part in range(PARTS):
        plane_start(part, 0)

    def widen(c, carry):
        kf[pl.ds(pl.multiple_of(c * 256, 256), 256), :] = keys[c].astype(F32)
        return carry

    lax.fori_loop(0, BLOCKS, widen, 0)
    live_here = length[0] - (me_z * LANES + me_lane) * (BLOCKS * BLOCK)
    rows = lax.broadcasted_iota(I32, (256, 256), 0)
    columns = lax.broadcasted_iota(I32, (256, 256), 1)
    lane_256 = lax.broadcasted_iota(I32, (1, 256), 1)

    def score(i, carry):
        g, c = i // 8, lax.rem(i, 8)
        chunk = kf[pl.ds(c * 1024 + g, 256, stride=4), :].astype(BF16)
        live = lax.broadcasted_iota(I32, (256, 128), 0) + c * 256 < live_here
        bias = jnp.where(live, 0.0, FAR)
        logits = contract_last(chunk, queries[g]) + jnp.concatenate([bias] * 5, axis=1)
        largest = jnp.max(logits, axis=0, keepdims=True)
        weights = jnp.exp2((logits - largest) * scale2)
        chunk_max[pl.ds(i, 1), :] = largest
        chunk_sum[pl.ds(i, 1), :] = jnp.sum(weights, axis=0, keepdims=True)
        probs[i] = weights.astype(BF16)
        gram = contract_last(chunk, chunk)
        on_diagonal = jnp.where(rows == columns, gram, 0.0)
        squares = jnp.sum(on_diagonal, axis=0, keepdims=True)
        down = jnp.sum(on_diagonal, axis=1, keepdims=True)
        spread = jnp.where(live[:, :1], 1.0, 0.0) / jnp.sqrt(down + NORM_EPS)
        norm = jnp.sqrt(squares + NORM_EPS)
        together = jnp.where(rows // BLOCK == columns // BLOCK, gram, 0.0)
        row_sum = jnp.sum(together * spread, axis=0, keepdims=True) / norm
        live_lanes = jnp.where(lane_256 + c * 256 < live_here, 1.0, 0.0)
        own_term = live_lanes * squares / (norm * norm)
        in_block = jnp.clip(live_here - c * 256 - lane_256 // BLOCK * BLOCK, 0, BLOCK).astype(F32)
        redundancy[pl.ds(i, 1), :] = (row_sum - own_term) / jnp.maximum(in_block - 1.0, 1.0)
        return carry

    lax.fori_loop(0, HEADS * 8, score, 0)

    row_of = lax.broadcasted_iota(I32, (STEP_ROWS, 128), 0)
    lane_of = lax.broadcasted_iota(I32, (STEP_ROWS, 128), 1)
    row_step = row_of % STEPS
    row_head = jnp.zeros((STEP_ROWS, 128), I32)
    for g in range(1, HEADS):
        row_head = row_head + (row_of >= g * GROUP * STEPS).astype(I32)
    same_head = lane_of % HEADS == row_head
    head_bias = jnp.concatenate([jnp.where(same_head, 0.0, FAR)] * 8, axis=1)
    may_see = same_head & (lane_of // HEADS <= row_step) & (lane_of < STEPS * HEADS)
    new_bias = jnp.where(may_see, 0.0, FAR)

    def padded(ref):
        return jnp.concatenate([ref[...], jnp.zeros((128 - STEPS * HEADS, 128), BF16)], axis=0)

    def decode_logits(c, top):
        chunk = keys[pl.ds(c * 4, 4)].reshape(1024, 128)
        kept_part = jnp.concatenate(
            [
                jnp.where(jnp.full((1, 256), kept[c * 4 + part], I32) > 0, 0.0, FAR)
                for part in range(4)
            ],
            axis=1,
        )
        token = lax.broadcasted_iota(I32, (1, 1024), 1) // HEADS + c * 256
        bias = kept_part + jnp.where(token < live_here, 0.0, FAR)
        found = contract_last(step_queries[...], chunk) + head_bias + bias
        dl[c] = found
        for part in range(8):
            top = jnp.maximum(top, found[:, part * 128 : (part + 1) * 128])
        return top

    new_logits = contract_last(step_queries[...], padded(new_keys)) + new_bias
    top = lax.fori_loop(0, 8, decode_logits, new_logits)
    step_top = column_to_row(jnp.max(top, axis=1, keepdims=True))

    maxima, sums = [], []
    for g in range(HEADS):
        part_max = chunk_max[g * 8 : g * 8 + 8, :]
        largest = jnp.max(part_max, axis=0, keepdims=True)
        maxima.append(largest)
        sums.append(
            jnp.sum(
                chunk_sum[g * 8 : g * 8 + 8, :] * jnp.exp2((part_max - largest) * scale2),
                axis=0,
                keepdims=True,
            )
        )
    tiles = [
        tuple(found[g][:, t * 128 : (t + 1) * 128] for found in (maxima, sums))
        for g in range(HEADS)
        for t in range(GROUP)
    ] + [(step_top, jnp.zeros((1, 128), F32))]
    stat_out[...] = jnp.zeros_like(stat_out)
    for n, (tile_max, tile_sum) in enumerate(tiles):
        stat_out[n // 3, n % 3 : n % 3 + 1, :] = tile_max
        stat_out[n // 3, n % 3 + 3 : n % 3 + 4, :] = tile_sum
    stat_plane[me_lane] = stat_out[me_lane]

    def plane_slice(buffer):
        return lambda i: buffer.at[lax.rem(me_lane + i, LANES)]

    settle(metas)
    to_scalars = pltpu.make_async_copy(meta_ring, table, t_sem)
    to_scalars.start()
    to_scalars.wait()
    out_meta[me_lane] = meta_ring[...]
    stats = share(plane_slice(stat_out), stat_plane, 0, me_lane, plane_peer, LANES)
    metas = share(lambda i: meta_ring, out_meta, 5, me_lane, plane_peer, LANES)

    def merged(buffer):
        largest = buffer[0, 0:3, :]
        for k in range(1, 8):
            largest = jnp.maximum(largest, buffer[k, 0:3, :])
        total = jnp.zeros((3, 128), F32)
        for k in range(8):
            total = total + buffer[k, 3:6, :] * jnp.exp2((buffer[k, 0:3, :] - largest) * scale2)
        return largest, total

    settle(stats)
    largest, total = merged(stat_plane)
    stat_ring[me_z, 0:3, :] = largest
    stat_ring[me_z, 3:6, :] = total
    stats = share(lambda k: stat_ring.at[me_z], stat_ring, 1, me_z, ring_peer, NZ)
    ring_first(PARTS - 1, *every)
    for part in range(PARTS):
        hand_on(part, 1)
        across(part, 1, 7)
    settle(metas)
    most = out_meta[0, 0]
    for lane in range(LANES):
        for z in range(NZ):
            most = jnp.maximum(most, out_meta[lane, z])
    needs_pair[me_b] = most
    pair = share(lambda i: needs_pair.at[me_b], needs_pair, 6, me_b, pair_peer, 2)

    settle(stats)
    largest, total = merged(stat_ring)
    stat_all[me_lane, 0:3, :] = largest
    stat_all[me_lane, 3:6, :] = total
    stats = share(lambda i: stat_all.at[me_lane], stat_all, 7, me_lane, plane_peer, LANES)
    for part in range(PARTS // 2):
        hand_on(part, 2)
        across(part, 2, 6)

    settle(stats)

    def across_tiles(first, g):
        tiles = range(g * GROUP, (g + 1) * GROUP)
        return jnp.concatenate(
            [stat_all[n // 3, first + n % 3 : first + n % 3 + 1, :] for n in tiles], axis=1
        )

    row_max = [across_tiles(0, g) for g in range(HEADS)]
    row_total = [across_tiles(3, g) for g in range(HEADS)]
    step_column = row_to_column(stat_all[6, 2:3, :], STEP_ROWS)

    def decode_sum(c, carry):
        weighted, total = carry
        part = jnp.exp2((dl[c] - step_column) * scale2)
        for piece in range(8):
            total = total + part[:, piece * 128 : (piece + 1) * 128]
        chunk = values[pl.ds(c * 4, 4)].reshape(1024, 128)
        weighted = weighted + jnp.dot(part.astype(BF16), chunk, preferred_element_type=F32)
        return weighted, total

    nothing = jnp.zeros((STEP_ROWS, 128), F32)
    weighted, total = lax.fori_loop(0, 8, decode_sum, (nothing, nothing))
    bottom = column_to_row(jnp.sum(total, axis=1, keepdims=True))
    each = STEP_ROWS // LANES
    for lane in range(LANES):
        sum_out[lane, 0:each, :] = weighted[lane * each : (lane + 1) * each]
        sum_out[lane, each:16, :] = jnp.broadcast_to(bottom, (16 - each, 128))
    sum_plane[me_lane] = sum_out[me_lane]
    sums = share(plane_slice(sum_out), sum_plane, 2, me_lane, plane_peer, LANES)

    for g in range(HEADS):
        factor = (
            jnp.exp2((chunk_max[g * 8 : g * 8 + 8, :] - row_max[g]) * scale2)
            / row_total[g]
        )
        high = factor.astype(BF16)
        low = (factor - high.astype(F32)).astype(BF16)
        rescale[g] = jnp.concatenate([high.astype(F32), low.astype(F32)], axis=0).astype(BF16)
    share_of_row = jnp.full((1, 256), length[0], I32).astype(F32) / (WINDOW * GROUP)

    def importance(i, carry):
        g, c = i // 8, lax.rem(i, 8)
        found = contract_last(rescale[g], probs[i])
        wanted = lax.rem(lax.broadcasted_iota(I32, (16, 256), 0), 8) == c
        found = jnp.sum(jnp.where(wanted, found, 0.0), axis=0, keepdims=True)
        value = (LAMBDA * share_of_row) * found - (1.0 - LAMBDA) * redundancy[pl.ds(i, 1), :]
        live = lane_256 + c * 256 < live_here
        redundancy[pl.ds(i, 1), :] = jnp.where(live, value, 0.0)
        return carry

    for part in range(PARTS // 2, PARTS):
        hand_on(part, 2)
        across(part, 2, 6)
        piece = part - PARTS // 2
        lax.fori_loop(piece * 64 // PARTS, (piece + 1) * 64 // PARTS, importance, 0)

    def summed(buffer):
        total = buffer[0]
        for k in range(1, 8):
            total = total + buffer[k]
        return total

    settle(sums)
    sum_ring[me_z] = summed(sum_plane)
    sums = share(lambda k: sum_ring.at[me_z], sum_ring, 3, me_z, ring_peer, NZ)
    for part in range(PARTS):
        hand_on(part, 3)
        across(part, 3, 5)
    settle(sums)
    sum_all[me_lane] = summed(sum_ring)
    sums = share(lambda i: sum_all.at[me_lane], sum_all, 8, me_lane, plane_peer, LANES)
    for g in range(HEADS):
        for c in range(8):
            out_scores[g : g + 1, c * 256 : (c + 1) * 256] = redundancy[g * 8 + c : g * 8 + c + 1, :]
    settle(pair)
    over = jnp.maximum(needs_pair[0], needs_pair[1])
    lane = lax.broadcasted_iota(I32, (1, 128), 1)
    for n in range(4):
        over = jnp.where(lane == LANES + n, over - slots[n], over)
    over = jnp.where((lane >= LANES) & (lane < LANES + 4), over, -1)
    out_over[0] = jnp.max(over)

    for part in range(PARTS):
        arrived(part, 0, HALF)
        across(part, HALF)

    settle(sums)
    fresh = jnp.exp2((new_logits - step_column) * scale2)
    weighted = jnp.concatenate([sum_all[lane, 0:each, :] for lane in range(LANES)], axis=0)
    weighted = weighted + jnp.dot(
        fresh.astype(BF16), padded(new_values), preferred_element_type=F32
    )
    bottom = row_to_column(sum_all[0, each : each + 1, :], STEP_ROWS)
    bottom = bottom + jnp.sum(fresh, axis=1, keepdims=True)
    out_decoded[...] = (weighted / bottom).astype(BF16)

    for (part, b, i), copy in plane_copies.items():
        copy.wait()
    for copy in ring_copies.values():
        copy.wait_send()


VMEM, SMEM = pl.BlockSpec(memory_space=pltpu.VMEM), pl.BlockSpec(memory_space=pltpu.SMEM)
ANY = pl.BlockSpec(memory_space=pl.ANY)


def run_plan(keep, owner):
    return pl.pallas_call(
        plan,
        out_shape=(
            jax.ShapeDtypeStruct((2, SECOND), I32),
            jax.ShapeDtypeStruct((LANES,), I32),
            jax.ShapeDtypeStruct((BLOCKS,), I32),
            jax.ShapeDtypeStruct((NZ, 128), I32),
        ),
        in_specs=[SMEM] * 2,
        out_specs=(SMEM,) * 4,
        scratch_shapes=[pltpu.SMEM((NZ * LANES,), I32)],
        name="plan",
    )(keep, owner)


def run_exchange(slots, collective_id, scale2, operands):
    s1, s2, s3, s4 = slots
    block = (BLOCKS * 8, 128)

    slot = (block[0] * 2 // PARTS, 128)

    def buffers(count):
        return (pltpu.VMEM((count, *slot), BF16),) * PARTS

    return pl.pallas_call(
        functools.partial(exchange, slots, scale2),
        out_shape=(
            jax.ShapeDtypeStruct((HEADS, BLOCKS * BLOCK), F32),
            jax.ShapeDtypeStruct((STEP_ROWS, 128), BF16),
            jax.ShapeDtypeStruct((LANES, NZ, 1, 128), I32),
            jax.ShapeDtypeStruct((1,), I32),
            jax.ShapeDtypeStruct((NZ * LANES, *block), BF16),
            jax.ShapeDtypeStruct((NZ * LANES, *block), BF16),
        ),
        in_specs=[SMEM] * 4 + [VMEM, ANY, ANY] + [VMEM] * 4,
        out_specs=(VMEM,) * 3 + (SMEM,) + (ANY,) * 2,
        scratch_shapes=[
            pltpu.VMEM((BLOCKS, *block), BF16),
            pltpu.VMEM((BLOCKS, *block), BF16),
            pltpu.SemaphoreType.DMA((2,)),
            buffers(s1),
            buffers(s1),
            buffers(s1),
            buffers(s2),
            buffers(s3),
            buffers(s1),
            buffers(s2),
            buffers(s3),
            buffers(2 * s4),
            pltpu.VMEM((PARTS, NZ, LANES, *slot), BF16),
            pltpu.VMEM((BLOCKS * 256, 128), F32),
            pltpu.VMEM((HEADS * 8, 256, WINDOW * GROUP), BF16),
            pltpu.VMEM((HEADS * 8, WINDOW * GROUP), F32),
            pltpu.VMEM((HEADS * 8, WINDOW * GROUP), F32),
            pltpu.VMEM((HEADS * 8, 256), F32),
            pltpu.VMEM((8, STEP_ROWS, 1024), F32),
            pltpu.VMEM((HEADS, 16, WINDOW * GROUP), BF16),
            pltpu.VMEM((NZ, 1, 128), I32),
            pltpu.VMEM((2, 1, 128), I32),
            pltpu.SMEM((NZ, 1, 128), I32),
            *[pltpu.VMEM((8, 8, 128), F32)] * 4,
            *[pltpu.VMEM((8, 16, 128), F32)] * 4,
            pltpu.SemaphoreType.DMA((PARTS, 2, 16)),
            pltpu.SemaphoreType.DMA((PARTS, 2, 16)),
            pltpu.SemaphoreType.DMA((PARTS, NZ, LANES)),
            pltpu.SemaphoreType.DMA((PARTS, NZ, LANES)),
            pltpu.SemaphoreType.DMA((10, 8)),
            pltpu.SemaphoreType.DMA((10, 8)),
            pltpu.SemaphoreType.DMA,
        ],
        compiler_params=pltpu.CompilerParams(
            collective_id=collective_id,
            has_side_effects=True,
            vmem_limit_bytes=67_043_328,
        ),
        name="exchange_%d" % s1,
    )(*operands)


def unpack(
    meta, scores, decoded, came_k, came_v, out_scores, out_decoded, out_k, out_v, held, picks, sems
):
    me_lane = lax.axis_index("ctx_1") * 2 + lax.axis_index("ctx_2")

    def choose(source, found):
        z, lane = source // LANES, lax.rem(source, LANES)
        picks[found] = source
        return found + (meta[lane * NZ + z, me_lane] > 0).astype(I32)

    lax.fori_loop(0, NZ * LANES, choose, 0)
    pairs = ((came_k, out_k), (came_v, out_v))

    def take(kind, j):
        return pltpu.make_async_copy(
            pairs[kind][0].at[picks[j]], held.at[kind, j], sems.at[0, kind, j]
        )

    def put(kind, j):
        return pltpu.make_async_copy(held.at[kind, j], pairs[kind][1].at[j], sems.at[1, kind, j])

    for kind in range(2):

        @pl.loop(0, KEEP)
        def _(j, kind=kind):
            take(kind, j).start()

    out_scores[...] = scores[...]
    out_decoded[...] = decoded[...]
    for kind in range(2):

        @pl.loop(0, KEEP)
        def _(j, kind=kind):
            take(kind, j).wait()
            put(kind, j).start()

    for kind in range(2):

        @pl.loop(0, KEEP)
        def _(j, kind=kind):
            put(kind, j).wait()


def run_unpack(meta, scores, decoded, came_k, came_v):
    block = came_k.shape[1:]
    shape = jax.ShapeDtypeStruct((KEEP, *block), BF16)
    return pl.pallas_call(
        unpack,
        out_shape=(
            jax.ShapeDtypeStruct(scores.shape, scores.dtype),
            jax.ShapeDtypeStruct(decoded.shape, decoded.dtype),
            shape,
            shape,
        ),
        in_specs=[SMEM, VMEM, VMEM, ANY, ANY],
        out_specs=(VMEM, VMEM, ANY, ANY),
        scratch_shapes=[
            pltpu.VMEM((2, KEEP, *block), BF16),
            pltpu.SMEM((NZ * LANES + 1,), I32),
            pltpu.SemaphoreType.DMA((2, 2, KEEP)),
        ],
        name="unpack",
    )(meta.reshape(NZ * LANES, 128), scores, decoded, came_k, came_v)


def shards(
    stored_keys,
    stored_values,
    observed_queries,
    decoded_queries,
    step_keys,
    decoded_values,
    keep_lists,
    owner_ids,
    cache_length,
):
    tokens, head_count, width = stored_keys.shape
    scale2 = math.log2(math.e) / math.sqrt(width)
    lists, own, kept, meta = run_plan(keep_lists, owner_ids)
    operands = (
        lists,
        own,
        kept,
        cache_length,
        meta.reshape(NZ, 1, 128),
        stored_keys.reshape(BLOCKS, BLOCK * head_count, width),
        stored_values.reshape(BLOCKS, BLOCK * head_count, width),
        observed_queries.transpose(1, 0, 2).reshape(HEADS, GROUP * WINDOW, width),
        decoded_queries.transpose(1, 0, 2).reshape(STEP_ROWS, width),
        step_keys.reshape(STEPS * HEADS, width),
        decoded_values.reshape(STEPS * HEADS, width),
    )
    first = run_exchange(FITS_MOST, 0, scale2, operands)

    def finish(result):
        scores, decoded, came, _, came_k, came_v = result
        return run_unpack(came, scores, decoded, came_k, came_v)

    scores, decoded, kept_keys, kept_values = lax.cond(
        first[3][0] > 0,
        lambda: finish(run_exchange(FITS_ALL, 1, scale2, operands)),
        lambda: finish(first),
    )
    decoded = decoded.reshape(HEAD_ROWS, STEPS, width).transpose(1, 0, 2)
    shape = (KEEP * BLOCK, head_count, width)
    return scores, kept_keys.reshape(shape), kept_values.reshape(shape), decoded


def solution(mesh):
    split = Mesh(
        mesh.devices.reshape(mesh.shape["batch"], 8, 4, 2, mesh.shape["head"]),
        ("batch", "ctx_0", "ctx_1", "ctx_2", "head"),
    )
    return jax.shard_map(
        shards,
        mesh=split,
        in_specs=(
            P(BATCH_CTX, "head", None),
            P(BATCH_CTX, "head", None),
            P("batch", "head", None),
            P("batch", "head", None),
            P("batch", "head", None),
            P("batch", "head", None),
            P(BATCH_CTX, None),
            P(BATCH_CTX, None),
            P("batch"),
        ),
        out_specs=(
            P(("batch", "head"), CTX),
            P(BATCH_CTX, "head", None),
            P(BATCH_CTX, "head", None),
            P("batch", "head", None),
        ),
        check_vma=False,
    )
```

```python
import functools
import math

import jax
import jax.numpy as jnp
from jax import lax
from jax.experimental import pallas as pl
from jax.experimental.pallas import tpu as pltpu
from jax.sharding import Mesh
from jax.sharding import PartitionSpec as P

BLOCK = 64
CTX = ("ctx_0", "ctx_1", "ctx_2")
BATCH_CTX = ("batch", "ctx_0", "ctx_1", "ctx_2")
MESH = pl.DeviceIdType.MESH
FAR = -1e30
LAMBDA = 0.1
NORM_EPS = 1e-06
NZ = 8
LANES = 8
HALF = NZ // 2
HEADS = 4
GROUP = 5
STEPS = 4
HEAD_ROWS = HEADS * GROUP
STEP_ROWS = STEPS * HEAD_ROWS
WINDOW = 128
KEEP = 26
PARTS = 4
BLOCKS = 32
SECOND = 32
FITS_ALL = (26, 20, 12, 4)
FITS_MOST = (17, 13, 10, 4)
F32, BF16, I32 = jnp.float32, jnp.bfloat16, jnp.int32


def contract_last(a, b):
    return lax.dot_general(a, b, (((1,), (1,)), ((), ())), preferred_element_type=F32)


def row_to_column(row, rows):
    return jnp.transpose(jnp.broadcast_to(row, (128, 128)))[:rows, :1]


def column_to_row(column):
    rows = column.shape[0]
    wide = jnp.concatenate(
        [jnp.broadcast_to(column, (rows, 128)), jnp.zeros((128 - rows, 128), F32)], axis=0
    )
    return jnp.transpose(wide)[:1, :]


def before_64(block):
    row = lax.broadcasted_iota(I32, (64, 64), 0)
    column = lax.broadcasted_iota(I32, (64, 64), 1)
    return jnp.where((column < row) & (column // block == row // block), 1.0, 0.0).astype(BF16)


def spread_rows(block):
    shape = block.shape
    same = lax.broadcasted_iota(I32, shape, 0) == lax.broadcasted_iota(I32, shape, 1)
    return jnp.sum(jnp.where(same, block, 0.0), axis=0, keepdims=True)


def plan(keep, owner, me_z, meta, lists):
    ahead_of_me = (owner + (NZ - me_z) * LANES) & (NZ * LANES - 1)
    match = lax.broadcasted_iota(I32, (NZ * LANES, KEEP), 0) == ahead_of_me
    wide = (NZ * LANES, 128)
    has = jnp.sum(jnp.where(match, 1.0, 0.0), axis=1, keepdims=True)
    has = jnp.broadcast_to(has, wide)
    block = jnp.sum(jnp.where(match, keep.astype(F32), 0.0), axis=1, keepdims=True)
    block = jnp.broadcast_to(block, wide)
    rank = jnp.dot(before_64(LANES), has.astype(BF16), preferred_element_type=F32)

    def plane(values, k):
        return values[k * LANES : (k + 1) * LANES]

    count = [jnp.sum(plane(has, k), axis=0, keepdims=True) for k in range(NZ)]
    n4 = count[HALF]
    ahead, behind = count[1] + count[2] + count[3], count[7] + count[6] + count[5]
    even = jnp.maximum(jnp.floor((n4 + behind - ahead + 1.0) * 0.5), 0.0)
    first = jnp.maximum(jnp.maximum(n4 - 4.0, 0.0), jnp.minimum(jnp.minimum(n4, 4.0), even))
    second = n4 - first
    tails_p = [first, first + count[3], first + count[3] + count[2], first + ahead]
    tails_m = [second, second + count[5], second + count[5] + count[6], second + behind]
    none = jnp.zeros_like(first)
    start = [none, tails_p[2], tails_p[1], tails_p[0], none, tails_m[0], tails_m[1], tails_m[2]]
    needs = [jnp.maximum(p, m) for p, m in zip(tails_p[::-1], tails_m[::-1])]
    lane = lax.broadcasted_iota(I32, (1, 128), 1)
    ways, places = [], []
    for k in range(NZ):
        if k == HALF:
            way = jnp.where(plane(rank, k) >= first, 1.0, 0.0)
        else:
            way = jnp.full((LANES, 128), float(k > HALF), F32)
        place = plane(rank, k) + start[k] - (way * first if k == HALF else 0.0)
        row = spread_rows(plane(has, k) * (place + 1.0 + way * SECOND))
        for n in range(4):
            row = jnp.where(lane == LANES + n, needs[n], row)
        meta[lax.rem(me_z + k, NZ)] = row.astype(I32)
        ways.append(way)
        places.append(place)
    way, place = jnp.concatenate(ways, axis=0), jnp.concatenate(places, axis=0)
    slot = lax.broadcasted_iota(I32, wide, 1).astype(F32)
    travels = (has > 0.5) & (lax.broadcasted_iota(I32, wide, 0) >= LANES)
    fills = travels & (jnp.abs(place - slot) < 0.5)
    for w in range(2):
        chosen = fills & (jnp.abs(way - w) < 0.5)
        row = jnp.sum(jnp.where(chosen, block, 0.0), axis=0, keepdims=True)
        lists[w : w + 1, :] = row.astype(I32)
    lists[2:3, :] = spread_rows(plane(block, 0)).astype(I32)
    named = lax.broadcasted_iota(I32, (BLOCKS, KEEP), 0) == keep
    named = jnp.sum(jnp.where(named, 1.0, 0.0), axis=1, keepdims=True)
    lists[3:4, :] = spread_rows(jnp.broadcast_to(named, (BLOCKS, 128))).astype(I32)
    lists[4:8, :] = jnp.zeros((4, 128), I32)


def exchange(
    slots,
    scale2,
    length,
    keep,
    owner,
    keys_in,
    values_in,
    queries,
    step_queries,
    new_keys,
    new_values,
    out_scores,
    out_decoded,
    out_picks,
    out_over,
    yr_k,
    yr_v,
    keys,
    values,
    in_sem,
    meta,
    plan_rows,
    planned,
    zs_p,
    zs_m,
    zr_p1,
    zr_p2,
    zr_p3,
    zr_m1,
    zr_m2,
    zr_m3,
    zr_4,
    yb,
    kf,
    probs,
    chunk_max,
    chunk_sum,
    redundancy,
    dl,
    rescale,
    meta_ring,
    meta_all,
    needs_pair,
    table,
    stat_out,
    stat_plane,
    stat_ring,
    stat_all,
    sum_out,
    sum_plane,
    sum_ring,
    sum_all,
    z_send,
    z_recv,
    y_send,
    y_recv,
    s_send,
    s_recv,
    t_sem,
):
    me_b = lax.axis_index("batch")
    me_z = lax.axis_index("ctx_0")
    me_lane = lax.axis_index("ctx_1") * 2 + lax.axis_index("ctx_2")
    s1, s2, s3, s4 = slots
    halves = PARTS // 2
    rows_part = keys.shape[1] // halves

    def part_of(pair, part):
        return pair[part // halves], pl.ds(part % halves * rows_part, rows_part)

    def ring_peer(k):
        return {"ctx_0": lax.rem(me_z + (k + NZ), NZ)}

    def plane_peer(i):
        lane = lax.rem(me_lane + i, LANES)
        return {"ctx_1": lane // 2, "ctx_2": lax.rem(lane, 2)}

    def pair_peer(i):
        return {"batch": 1 - me_b}

    loads = [
        pltpu.make_async_copy(source, store, in_sem.at[kind])
        for kind, (source, store) in enumerate(((keys_in, keys), (values_in, values)))
    ]
    for load in loads:
        load.start()

    barrier = pltpu.get_barrier_semaphore()
    for i in range(1, LANES):
        pl.semaphore_signal(barrier, inc=1, device_id=plane_peer(i), device_id_type=MESH)
    for k in range(1, NZ):
        pl.semaphore_signal(barrier, inc=1, device_id=ring_peer(k), device_id_type=MESH)
    pl.semaphore_signal(barrier, inc=1, device_id=pair_peer(0), device_id_type=MESH)

    def block_at(row, slot):
        return lax.max(lax.min(planned[row, slot], BLOCKS - 1), 0)

    def pack(part):
        store, rows = part_of((keys, values), part)

        def fill(slot, carry):
            for way, dst in ((0, zs_p), (1, zs_m)):
                dst[part][slot] = store[block_at(way, slot), rows]
            return carry

        lax.fori_loop(0, s1, fill, 0)

    def pack_own(part):
        store, rows = part_of((keys, values), part)
        for i in range(LANES):
            yb[part, 0, i] = store[block_at(2, lax.rem(me_lane + i, LANES)), rows]

    plan(keep[...], owner[...], me_z, meta, plan_rows)
    to_scalars = pltpu.make_async_copy(plan_rows, planned, t_sem.at[0])
    to_scalars.start()
    to_scalars.wait()
    loads[0].wait()
    for part in range(halves):
        pack(part)
    meta_ring[me_z] = meta[me_z]
    pl.semaphore_wait(barrier, LANES - 1 + NZ - 1 + 1)

    def share(source, buffer, number, at, peer, count):
        copies = []
        for i in range(1, count):
            copy = pltpu.make_async_remote_copy(
                src_ref=source(i),
                dst_ref=buffer.at[at],
                send_sem=s_send.at[number, i],
                recv_sem=s_recv.at[number, i],
                device_id=peer(i),
                device_id_type=MESH,
            )
            copy.start()
            copies.append(copy)
        return copies

    def settle(copies):
        for copy in copies:
            copy.wait()

    metas = share(
        lambda k: meta.at[lax.rem(me_z + k, NZ)], meta_ring, 4, me_z, ring_peer, NZ
    )

    segments = ((0, s4), (s4, s3), (s3, s2), (s2, s1))
    ring = ((zs_p, zr_p1, zr_p2, zr_p3), (zs_m, zr_m1, zr_m2, zr_m3))
    ring_copies = {}

    def ring_start(part, way, q, hop):
        a, b = segments[q]
        if a == b:
            return
        src = ring[way][hop - 1][part].at[pl.ds(a, b - a)]
        if hop < HALF:
            dst = ring[way][hop][part].at[pl.ds(a, b - a)]
        else:
            dst = zr_4[part].at[pl.ds(way * s4 + a, b - a)]
        number = q * HALF + hop - 1
        copy = pltpu.make_async_remote_copy(
            src_ref=src,
            dst_ref=dst,
            send_sem=z_send.at[part, way, number],
            recv_sem=z_recv.at[part, way, number],
            device_id=ring_peer(1 if way == 0 else -1),
            device_id_type=MESH,
        )
        copy.start()
        ring_copies[part, way, q, hop] = copy

    def arrived(part, q, hop):
        for way in range(2):
            if (part, way, q, hop) in ring_copies:
                ring_copies[part, way, q, hop].wait_recv()

    def hand_on(part, hop):
        for q in range(HALF - hop):
            for way in range(2):
                if (part, way, q, hop) in ring_copies:
                    ring_copies[part, way, q, hop].wait_recv()
                ring_start(part, way, q, hop + 1)
        arrived(part, HALF - hop, hop)

    arrivals = {1: zr_p1, 2: zr_p2, 3: zr_p3, 4: zr_4, 5: zr_m3, 6: zr_m2, 7: zr_m1}
    plane_copies = {}

    def plane_pack(part, b):
        source = lax.rem(me_z + (NZ - b), NZ)
        got = arrivals[b][part]
        for i in range(LANES):
            code = table[source, 0, lax.rem(me_lane + i, LANES)]
            is_second = (code > SECOND).astype(I32)
            slot = lax.max(code - 1 - is_second * SECOND, 0)
            if b == HALF:
                slot = lax.min(slot, s4 - 1) + is_second * s4
            else:
                slot = lax.min(slot, got.shape[0] - 1)
            yb[part, b, i] = got[slot]

    def plane_start(part, b):
        result, rows = part_of((yr_k, yr_v), part)
        source = lax.rem(me_z + (NZ - b), NZ) * LANES + me_lane
        for i in range(1, LANES):
            copy = pltpu.make_async_remote_copy(
                src_ref=yb.at[part, b, i],
                dst_ref=result.at[source, rows],
                send_sem=y_send.at[part, b, i],
                recv_sem=y_recv.at[part, b, i],
                device_id=plane_peer(i),
                device_id_type=MESH,
            )
            copy.start()
            plane_copies[part, b, i] = copy
        copy = pltpu.make_async_copy(
            yb.at[part, b, 0], result.at[source, rows], y_send.at[part, b, 0]
        )
        copy.start()
        plane_copies[part, b, 0] = copy

    def across(part, *batches):
        for b in batches:
            plane_pack(part, b)
        for b in batches:
            plane_start(part, b)

    def ring_first(part, *parts):
        for q in parts:
            for way in range(2):
                ring_start(part, way, q, 1)

    every = range(HALF)
    for part in range(halves):
        ring_first(part, *every)
    loads[1].wait()
    for part in range(halves, PARTS):
        pack(part)
    for part in range(halves, PARTS - 1):
        ring_first(part, *every)
    for part in range(PARTS):
        pack_own(part)
    for part in range(PARTS):
        plane_start(part, 0)

    def widen(c, carry):
        kf[pl.ds(pl.multiple_of(c * 256, 256), 256), :] = keys[c].astype(F32)
        return carry

    lax.fori_loop(0, BLOCKS, widen, 0)
    live_here = length[0] - (me_z * LANES + me_lane) * (BLOCKS * BLOCK)
    rows = lax.broadcasted_iota(I32, (256, 256), 0)
    columns = lax.broadcasted_iota(I32, (256, 256), 1)
    lane_256 = lax.broadcasted_iota(I32, (1, 256), 1)

    def score(i, carry):
        g, c = i // 8, lax.rem(i, 8)
        chunk = kf[pl.ds(c * 1024 + g, 256, stride=4), :].astype(BF16)
        live = lax.broadcasted_iota(I32, (256, 128), 0) + c * 256 < live_here
        bias = jnp.where(live, 0.0, FAR)
        logits = contract_last(chunk, queries[g]) + jnp.concatenate([bias] * 5, axis=1)
        largest = jnp.max(logits, axis=0, keepdims=True)
        weights = jnp.exp2((logits - largest) * scale2)
        chunk_max[pl.ds(i, 1), :] = largest
        chunk_sum[pl.ds(i, 1), :] = jnp.sum(weights, axis=0, keepdims=True)
        probs[i] = weights.astype(BF16)
        gram = contract_last(chunk, chunk)
        on_diagonal = jnp.where(rows == columns, gram, 0.0)
        squares = jnp.sum(on_diagonal, axis=0, keepdims=True)
        down = jnp.sum(on_diagonal, axis=1, keepdims=True)
        spread = jnp.where(live[:, :1], 1.0, 0.0) / jnp.sqrt(down + NORM_EPS)
        norm = jnp.sqrt(squares + NORM_EPS)
        together = jnp.where(rows // BLOCK == columns // BLOCK, gram, 0.0)
        row_sum = jnp.sum(together * spread, axis=0, keepdims=True) / norm
        live_lanes = jnp.where(lane_256 + c * 256 < live_here, 1.0, 0.0)
        own_term = live_lanes * squares / (norm * norm)
        in_block = jnp.clip(live_here - c * 256 - lane_256 // BLOCK * BLOCK, 0, BLOCK).astype(F32)
        redundancy[pl.ds(i, 1), :] = (row_sum - own_term) / jnp.maximum(in_block - 1.0, 1.0)
        return carry

    lax.fori_loop(0, HEADS * 8, score, 0)

    row_of = lax.broadcasted_iota(I32, (STEP_ROWS, 128), 0)
    lane_of = lax.broadcasted_iota(I32, (STEP_ROWS, 128), 1)
    row_step = row_of % STEPS
    row_head = jnp.zeros((STEP_ROWS, 128), I32)
    for g in range(1, HEADS):
        row_head = row_head + (row_of >= g * GROUP * STEPS).astype(I32)
    same_head = lane_of % HEADS == row_head
    head_bias = jnp.concatenate([jnp.where(same_head, 0.0, FAR)] * 8, axis=1)
    may_see = same_head & (lane_of // HEADS <= row_step) & (lane_of < STEPS * HEADS)
    new_bias = jnp.where(may_see, 0.0, FAR)

    def padded(ref):
        return jnp.concatenate([ref[...], jnp.zeros((128 - STEPS * HEADS, 128), BF16)], axis=0)

    def decode_logits(c, top):
        chunk = keys[pl.ds(c * 4, 4)].reshape(1024, 128)
        kept_part = jnp.concatenate(
            [
                jnp.where(jnp.full((1, 256), planned[3, c * 4 + part], I32) > 0, 0.0, FAR)
                for part in range(4)
            ],
            axis=1,
        )
        token = lax.broadcasted_iota(I32, (1, 1024), 1) // HEADS + c * 256
        bias = kept_part + jnp.where(token < live_here, 0.0, FAR)
        found = contract_last(step_queries[...], chunk) + head_bias + bias
        dl[c] = found
        for part in range(8):
            top = jnp.maximum(top, found[:, part * 128 : (part + 1) * 128])
        return top

    new_logits = contract_last(step_queries[...], padded(new_keys)) + new_bias
    top = lax.fori_loop(0, 8, decode_logits, new_logits)
    step_top = column_to_row(jnp.max(top, axis=1, keepdims=True))

    maxima, sums = [], []
    for g in range(HEADS):
        part_max = chunk_max[g * 8 : g * 8 + 8, :]
        largest = jnp.max(part_max, axis=0, keepdims=True)
        maxima.append(largest)
        sums.append(
            jnp.sum(
                chunk_sum[g * 8 : g * 8 + 8, :] * jnp.exp2((part_max - largest) * scale2),
                axis=0,
                keepdims=True,
            )
        )
    tiles = [
        tuple(found[g][:, t * 128 : (t + 1) * 128] for found in (maxima, sums))
        for g in range(HEADS)
        for t in range(GROUP)
    ] + [(step_top, jnp.zeros((1, 128), F32))]
    stat_out[...] = jnp.zeros_like(stat_out)
    for n, (tile_max, tile_sum) in enumerate(tiles):
        stat_out[n // 3, n % 3 : n % 3 + 1, :] = tile_max
        stat_out[n // 3, n % 3 + 3 : n % 3 + 4, :] = tile_sum
    stat_plane[me_lane] = stat_out[me_lane]

    def plane_slice(buffer):
        return lambda i: buffer.at[lax.rem(me_lane + i, LANES)]

    settle(metas)
    to_scalars = pltpu.make_async_copy(meta_ring, table, t_sem.at[1])
    to_scalars.start()
    to_scalars.wait()
    meta_all[me_lane] = meta_ring[...]
    stats = share(plane_slice(stat_out), stat_plane, 0, me_lane, plane_peer, LANES)
    metas = share(lambda i: meta_ring, meta_all, 5, me_lane, plane_peer, LANES)

    def merged(buffer):
        largest = buffer[0, 0:3, :]
        for k in range(1, 8):
            largest = jnp.maximum(largest, buffer[k, 0:3, :])
        total = jnp.zeros((3, 128), F32)
        for k in range(8):
            total = total + buffer[k, 3:6, :] * jnp.exp2((buffer[k, 0:3, :] - largest) * scale2)
        return largest, total

    settle(stats)
    largest, total = merged(stat_plane)
    stat_ring[me_z, 0:3, :] = largest
    stat_ring[me_z, 3:6, :] = total
    stats = share(lambda k: stat_ring.at[me_z], stat_ring, 1, me_z, ring_peer, NZ)
    ring_first(PARTS - 1, *every)
    for part in range(PARTS):
        hand_on(part, 1)
        across(part, 1, 7)
    settle(metas)
    most = meta_all[0, 0]
    for lane in range(LANES):
        for z in range(NZ):
            most = jnp.maximum(most, meta_all[lane, z])
    needs_pair[me_b] = most
    coded = jnp.concatenate(
        [meta_all[lane, z] for z in range(NZ) for lane in range(LANES)], axis=0
    ).astype(F32)
    source = lax.broadcasted_iota(I32, (64, 128), 0)
    lane_64 = lax.broadcasted_iota(I32, (64, 128), 1)
    here = jnp.sum(jnp.where(lane_64 == me_lane, coded, 0.0), axis=1, keepdims=True) > 0.5
    here = jnp.broadcast_to(jnp.where(here, 1.0, 0.0), (64, 128))
    rank = jnp.dot(before_64(64), here.astype(BF16), preferred_element_type=F32)
    chosen = (here > 0.5) & (jnp.abs(rank - lane_64.astype(F32)) < 0.5)
    picks = jnp.sum(jnp.where(chosen, source.astype(F32), 0.0), axis=0, keepdims=True)
    out_picks[...] = picks.astype(I32)
    pair = share(lambda i: needs_pair.at[me_b], needs_pair, 6, me_b, pair_peer, 2)

    settle(stats)
    largest, total = merged(stat_ring)
    stat_all[me_lane, 0:3, :] = largest
    stat_all[me_lane, 3:6, :] = total
    stats = share(lambda i: stat_all.at[me_lane], stat_all, 7, me_lane, plane_peer, LANES)
    for part in range(PARTS // 2):
        hand_on(part, 2)
        across(part, 2, 6)

    settle(stats)

    def across_tiles(first, g):
        tiles = range(g * GROUP, (g + 1) * GROUP)
        return jnp.concatenate(
            [stat_all[n // 3, first + n % 3 : first + n % 3 + 1, :] for n in tiles], axis=1
        )

    row_max = [across_tiles(0, g) for g in range(HEADS)]
    row_total = [across_tiles(3, g) for g in range(HEADS)]
    step_column = row_to_column(stat_all[6, 2:3, :], STEP_ROWS)

    def decode_sum(c, carry):
        weighted, total = carry
        part = jnp.exp2((dl[c] - step_column) * scale2)
        for piece in range(8):
            total = total + part[:, piece * 128 : (piece + 1) * 128]
        chunk = values[pl.ds(c * 4, 4)].reshape(1024, 128)
        weighted = weighted + jnp.dot(part.astype(BF16), chunk, preferred_element_type=F32)
        return weighted, total

    nothing = jnp.zeros((STEP_ROWS, 128), F32)
    weighted, total = lax.fori_loop(0, 8, decode_sum, (nothing, nothing))
    bottom = column_to_row(jnp.sum(total, axis=1, keepdims=True))
    each = STEP_ROWS // LANES
    for lane in range(LANES):
        sum_out[lane, 0:each, :] = weighted[lane * each : (lane + 1) * each]
        sum_out[lane, each:16, :] = jnp.broadcast_to(bottom, (16 - each, 128))
    sum_plane[me_lane] = sum_out[me_lane]
    sums = share(plane_slice(sum_out), sum_plane, 2, me_lane, plane_peer, LANES)

    for g in range(HEADS):
        factor = (
            jnp.exp2((chunk_max[g * 8 : g * 8 + 8, :] - row_max[g]) * scale2)
            / row_total[g]
        )
        high = factor.astype(BF16)
        low = (factor - high.astype(F32)).astype(BF16)
        rescale[g] = jnp.concatenate([high.astype(F32), low.astype(F32)], axis=0).astype(BF16)
    share_of_row = jnp.full((1, 256), length[0], I32).astype(F32) / (WINDOW * GROUP)

    def importance(i, carry):
        g, c = i // 8, lax.rem(i, 8)
        found = contract_last(rescale[g], probs[i])
        wanted = lax.rem(lax.broadcasted_iota(I32, (16, 256), 0), 8) == c
        found = jnp.sum(jnp.where(wanted, found, 0.0), axis=0, keepdims=True)
        value = (LAMBDA * share_of_row) * found - (1.0 - LAMBDA) * redundancy[pl.ds(i, 1), :]
        live = lane_256 + c * 256 < live_here
        redundancy[pl.ds(i, 1), :] = jnp.where(live, value, 0.0)
        return carry

    for part in range(PARTS // 2, PARTS):
        hand_on(part, 2)
        across(part, 2, 6)
        piece = part - PARTS // 2
        lax.fori_loop(piece * 64 // PARTS, (piece + 1) * 64 // PARTS, importance, 0)

    def summed(buffer):
        total = buffer[0]
        for k in range(1, 8):
            total = total + buffer[k]
        return total

    settle(sums)
    sum_ring[me_z] = summed(sum_plane)
    sums = share(lambda k: sum_ring.at[me_z], sum_ring, 3, me_z, ring_peer, NZ)
    for part in range(PARTS):
        hand_on(part, 3)
        across(part, 3, 5)
    settle(sums)
    sum_all[me_lane] = summed(sum_ring)
    sums = share(lambda i: sum_all.at[me_lane], sum_all, 8, me_lane, plane_peer, LANES)
    for g in range(HEADS):
        for c in range(8):
            out_scores[g : g + 1, c * 256 : (c + 1) * 256] = redundancy[g * 8 + c : g * 8 + c + 1, :]
    settle(pair)
    over = jnp.maximum(needs_pair[0], needs_pair[1])
    lane = lax.broadcasted_iota(I32, (1, 128), 1)
    for n in range(4):
        over = jnp.where(lane == LANES + n, over - slots[n], over)
    over = jnp.where((lane >= LANES) & (lane < LANES + 4), over, -1)
    out_over[0] = jnp.max(over)

    for part in range(PARTS):
        arrived(part, 0, HALF)
        across(part, HALF)

    settle(sums)
    fresh = jnp.exp2((new_logits - step_column) * scale2)
    weighted = jnp.concatenate([sum_all[lane, 0:each, :] for lane in range(LANES)], axis=0)
    weighted = weighted + jnp.dot(
        fresh.astype(BF16), padded(new_values), preferred_element_type=F32
    )
    bottom = row_to_column(sum_all[0, each : each + 1, :], STEP_ROWS)
    bottom = bottom + jnp.sum(fresh, axis=1, keepdims=True)
    out_decoded[...] = (weighted / bottom).astype(BF16)

    for (part, b, i), copy in plane_copies.items():
        copy.wait()
    for copy in ring_copies.values():
        copy.wait_send()


VMEM, SMEM = pl.BlockSpec(memory_space=pltpu.VMEM), pl.BlockSpec(memory_space=pltpu.SMEM)
ANY = pl.BlockSpec(memory_space=pl.ANY)


def run_exchange(slots, collective_id, scale2, operands):
    s1, s2, s3, s4 = slots
    block = (BLOCKS * 8, 128)

    slot = (block[0] * 2 // PARTS, 128)

    def buffers(count):
        return (pltpu.VMEM((count, *slot), BF16),) * PARTS

    return pl.pallas_call(
        functools.partial(exchange, slots, scale2),
        out_shape=(
            jax.ShapeDtypeStruct((HEADS, BLOCKS * BLOCK), F32),
            jax.ShapeDtypeStruct((STEP_ROWS, 128), BF16),
            jax.ShapeDtypeStruct((1, 128), I32),
            jax.ShapeDtypeStruct((1,), I32),
            jax.ShapeDtypeStruct((NZ * LANES, *block), BF16),
            jax.ShapeDtypeStruct((NZ * LANES, *block), BF16),
        ),
        in_specs=[SMEM, VMEM, VMEM, ANY, ANY] + [VMEM] * 4,
        out_specs=(VMEM,) * 3 + (SMEM,) + (ANY,) * 2,
        scratch_shapes=[
            pltpu.VMEM((BLOCKS, *block), BF16),
            pltpu.VMEM((BLOCKS, *block), BF16),
            pltpu.SemaphoreType.DMA((2,)),
            pltpu.VMEM((NZ, 1, 128), I32),
            pltpu.VMEM((8, 128), I32),
            pltpu.SMEM((8, 128), I32),
            buffers(s1),
            buffers(s1),
            buffers(s1),
            buffers(s2),
            buffers(s3),
            buffers(s1),
            buffers(s2),
            buffers(s3),
            buffers(2 * s4),
            pltpu.VMEM((PARTS, NZ, LANES, *slot), BF16),
            pltpu.VMEM((BLOCKS * 256, 128), F32),
            pltpu.VMEM((HEADS * 8, 256, WINDOW * GROUP), BF16),
            pltpu.VMEM((HEADS * 8, WINDOW * GROUP), F32),
            pltpu.VMEM((HEADS * 8, WINDOW * GROUP), F32),
            pltpu.VMEM((HEADS * 8, 256), F32),
            pltpu.VMEM((8, STEP_ROWS, 1024), F32),
            pltpu.VMEM((HEADS, 16, WINDOW * GROUP), BF16),
            pltpu.VMEM((NZ, 1, 128), I32),
            pltpu.VMEM((LANES, NZ, 1, 128), I32),
            pltpu.VMEM((2, 1, 128), I32),
            pltpu.SMEM((NZ, 1, 128), I32),
            *[pltpu.VMEM((8, 8, 128), F32)] * 4,
            *[pltpu.VMEM((8, 16, 128), F32)] * 4,
            pltpu.SemaphoreType.DMA((PARTS, 2, 16)),
            pltpu.SemaphoreType.DMA((PARTS, 2, 16)),
            pltpu.SemaphoreType.DMA((PARTS, NZ, LANES)),
            pltpu.SemaphoreType.DMA((PARTS, NZ, LANES)),
            pltpu.SemaphoreType.DMA((10, 8)),
            pltpu.SemaphoreType.DMA((10, 8)),
            pltpu.SemaphoreType.DMA((2,)),
        ],
        compiler_params=pltpu.CompilerParams(
            collective_id=collective_id,
            has_side_effects=True,
            vmem_limit_bytes=67_043_328,
        ),
        name="exchange_%d" % s1,
    )(*operands)


def unpack(
    picks, scores, decoded, came_k, came_v, out_scores, out_decoded, out_k, out_v, held, sems
):
    pairs = ((came_k, out_k), (came_v, out_v))

    def take(kind, j):
        return pltpu.make_async_copy(
            pairs[kind][0].at[picks[0, j]], held.at[kind, j], sems.at[0, kind, j]
        )

    def put(kind, j):
        return pltpu.make_async_copy(held.at[kind, j], pairs[kind][1].at[j], sems.at[1, kind, j])

    for kind in range(2):

        @pl.loop(0, KEEP)
        def _(j, kind=kind):
            take(kind, j).start()

    out_scores[...] = scores[...]
    out_decoded[...] = decoded[...]
    for kind in range(2):

        @pl.loop(0, KEEP)
        def _(j, kind=kind):
            take(kind, j).wait()
            put(kind, j).start()

    for kind in range(2):

        @pl.loop(0, KEEP)
        def _(j, kind=kind):
            put(kind, j).wait()


def run_unpack(picks, scores, decoded, came_k, came_v):
    block = came_k.shape[1:]
    shape = jax.ShapeDtypeStruct((KEEP, *block), BF16)
    return pl.pallas_call(
        unpack,
        out_shape=(
            jax.ShapeDtypeStruct(scores.shape, scores.dtype),
            jax.ShapeDtypeStruct(decoded.shape, decoded.dtype),
            shape,
            shape,
        ),
        in_specs=[SMEM, VMEM, VMEM, ANY, ANY],
        out_specs=(VMEM, VMEM, ANY, ANY),
        scratch_shapes=[
            pltpu.VMEM((2, KEEP, *block), BF16),
            pltpu.SemaphoreType.DMA((2, 2, KEEP)),
        ],
        name="unpack",
    )(picks, scores, decoded, came_k, came_v)


def shards(
    stored_keys,
    stored_values,
    observed_queries,
    decoded_queries,
    step_keys,
    decoded_values,
    keep_lists,
    owner_ids,
    cache_length,
):
    tokens, head_count, width = stored_keys.shape
    scale2 = math.log2(math.e) / math.sqrt(width)
    operands = (
        cache_length,
        keep_lists,
        owner_ids,
        stored_keys.reshape(BLOCKS, BLOCK * head_count, width),
        stored_values.reshape(BLOCKS, BLOCK * head_count, width),
        observed_queries.transpose(1, 0, 2).reshape(HEADS, GROUP * WINDOW, width),
        decoded_queries.transpose(1, 0, 2).reshape(STEP_ROWS, width),
        step_keys.reshape(STEPS * HEADS, width),
        decoded_values.reshape(STEPS * HEADS, width),
    )
    first = run_exchange(FITS_MOST, 0, scale2, operands)

    def finish(result):
        scores, decoded, picks, _, came_k, came_v = result
        return run_unpack(picks, scores, decoded, came_k, came_v)

    scores, decoded, kept_keys, kept_values = lax.cond(
        first[3][0] > 0,
        lambda: finish(run_exchange(FITS_ALL, 1, scale2, operands)),
        lambda: finish(first),
    )
    decoded = decoded.reshape(HEAD_ROWS, STEPS, width).transpose(1, 0, 2)
    shape = (KEEP * BLOCK, head_count, width)
    return scores, kept_keys.reshape(shape), kept_values.reshape(shape), decoded


def solution(mesh):
    split = Mesh(
        mesh.devices.reshape(mesh.shape["batch"], 8, 4, 2, mesh.shape["head"]),
        ("batch", "ctx_0", "ctx_1", "ctx_2", "head"),
    )
    return jax.shard_map(
        shards,
        mesh=split,
        in_specs=(
            P(BATCH_CTX, "head", None),
            P(BATCH_CTX, "head", None),
            P("batch", "head", None),
            P("batch", "head", None),
            P("batch", "head", None),
            P("batch", "head", None),
            P(BATCH_CTX, None),
            P(BATCH_CTX, None),
            P("batch"),
        ),
        out_specs=(
            P(("batch", "head"), CTX),
            P(BATCH_CTX, "head", None),
            P(BATCH_CTX, "head", None),
            P("batch", "head", None),
        ),
        check_vma=False,
    )
```

```python
import functools
import math

import jax
import jax.numpy as jnp
from jax import lax
from jax.experimental import pallas as pl
from jax.experimental.pallas import tpu as pltpu
from jax.sharding import Mesh
from jax.sharding import PartitionSpec as P

BLOCK = 64
CTX = ("ctx_0", "ctx_1", "ctx_2")
BATCH_CTX = ("batch", "ctx_0", "ctx_1", "ctx_2")
MESH = pl.DeviceIdType.MESH
FAR = -1e30
LAMBDA = 0.1
NORM_EPS = 1e-06
NZ = 8
LANES = 8
HALF = NZ // 2
HEADS = 4
GROUP = 5
STEPS = 4
HEAD_ROWS = HEADS * GROUP
STEP_ROWS = STEPS * HEAD_ROWS
WINDOW = 128
KEEP = 26
PARTS = 4
BLOCKS = 32
SECOND = 32
FITS_ALL = (26, 20, 12, 4)
FITS_MOST = (17, 13, 10, 4)
F32, BF16, I32 = jnp.float32, jnp.bfloat16, jnp.int32


def contract_last(a, b):
    return lax.dot_general(a, b, (((1,), (1,)), ((), ())), preferred_element_type=F32)


def row_to_column(row, rows):
    return jnp.transpose(jnp.broadcast_to(row, (128, 128)))[:rows, :1]


def column_to_row(column):
    rows = column.shape[0]
    wide = jnp.concatenate(
        [jnp.broadcast_to(column, (rows, 128)), jnp.zeros((128 - rows, 128), F32)], axis=0
    )
    return jnp.transpose(wide)[:1, :]


def before_64(block):
    row = lax.broadcasted_iota(I32, (64, 64), 0)
    column = lax.broadcasted_iota(I32, (64, 64), 1)
    return jnp.where((column < row) & (column // block == row // block), 1.0, 0.0).astype(BF16)


def spread_rows(block):
    shape = block.shape
    same = lax.broadcasted_iota(I32, shape, 0) == lax.broadcasted_iota(I32, shape, 1)
    return jnp.sum(jnp.where(same, block, 0.0), axis=0, keepdims=True)


def plan(keep, owner, me_z, meta, lists):
    ahead_of_me = (owner + (NZ - me_z) * LANES) & (NZ * LANES - 1)
    match = lax.broadcasted_iota(I32, (NZ * LANES, KEEP), 0) == ahead_of_me
    wide = (NZ * LANES, 128)
    has = jnp.sum(jnp.where(match, 1.0, 0.0), axis=1, keepdims=True)
    has = jnp.broadcast_to(has, wide)
    block = jnp.sum(jnp.where(match, keep.astype(F32), 0.0), axis=1, keepdims=True)
    block = jnp.broadcast_to(block, wide)
    rank = jnp.dot(before_64(LANES), has.astype(BF16), preferred_element_type=F32)

    def plane(values, k):
        return values[k * LANES : (k + 1) * LANES]

    count = [jnp.sum(plane(has, k), axis=0, keepdims=True) for k in range(NZ)]
    n4 = count[HALF]
    ahead, behind = count[1] + count[2] + count[3], count[7] + count[6] + count[5]
    even = jnp.maximum(jnp.floor((n4 + behind - ahead + 1.0) * 0.5), 0.0)
    first = jnp.maximum(jnp.maximum(n4 - 4.0, 0.0), jnp.minimum(jnp.minimum(n4, 4.0), even))
    second = n4 - first
    tails_p = [first, first + count[3], first + count[3] + count[2], first + ahead]
    tails_m = [second, second + count[5], second + count[5] + count[6], second + behind]
    none = jnp.zeros_like(first)
    start = [none, tails_p[2], tails_p[1], tails_p[0], none, tails_m[0], tails_m[1], tails_m[2]]
    needs = [jnp.maximum(p, m) for p, m in zip(tails_p[::-1], tails_m[::-1])]
    lane = lax.broadcasted_iota(I32, (1, 128), 1)
    ways, places = [], []
    for k in range(NZ):
        if k == HALF:
            way = jnp.where(plane(rank, k) >= first, 1.0, 0.0)
        else:
            way = jnp.full((LANES, 128), float(k > HALF), F32)
        place = plane(rank, k) + start[k] - (way * first if k == HALF else 0.0)
        row = spread_rows(plane(has, k) * (place + 1.0 + way * SECOND))
        for n in range(4):
            row = jnp.where(lane == LANES + n, needs[n], row)
        meta[lax.rem(me_z + k, NZ)] = row.astype(I32)
        ways.append(way)
        places.append(place)
    way, place = jnp.concatenate(ways, axis=0), jnp.concatenate(places, axis=0)
    slot = lax.broadcasted_iota(I32, wide, 1).astype(F32)
    travels = (has > 0.5) & (lax.broadcasted_iota(I32, wide, 0) >= LANES)
    fills = travels & (jnp.abs(place - slot) < 0.5)
    for w in range(2):
        chosen = fills & (jnp.abs(way - w) < 0.5)
        row = jnp.sum(jnp.where(chosen, block, 0.0), axis=0, keepdims=True)
        lists[w : w + 1, :] = row.astype(I32)
    lists[2:3, :] = spread_rows(plane(block, 0)).astype(I32)
    named = lax.broadcasted_iota(I32, (BLOCKS, KEEP), 0) == keep
    named = jnp.sum(jnp.where(named, 1.0, 0.0), axis=1, keepdims=True)
    lists[3:4, :] = spread_rows(jnp.broadcast_to(named, (BLOCKS, 128))).astype(I32)
    lists[4:8, :] = jnp.zeros((4, 128), I32)


def exchange(
    slots,
    scale2,
    length,
    keep,
    owner,
    keys_in,
    values_in,
    queries_in,
    step_queries,
    new_keys,
    new_values,
    out_scores,
    out_decoded,
    out_picks,
    out_over,
    yr_k,
    yr_v,
    keys,
    values,
    queries,
    in_sem,
    meta,
    plan_rows,
    planned,
    zs_p,
    zs_m,
    zr_p1,
    zr_p2,
    zr_p3,
    zr_m1,
    zr_m2,
    zr_m3,
    zr_4,
    yb,
    kf,
    probs,
    chunk_max,
    chunk_sum,
    redundancy,
    dl,
    rescale,
    meta_ring,
    meta_all,
    needs_pair,
    table,
    stat_out,
    stat_plane,
    stat_ring,
    stat_all,
    sum_out,
    sum_plane,
    sum_ring,
    sum_all,
    z_send,
    z_recv,
    y_send,
    y_recv,
    s_send,
    s_recv,
    t_sem,
):
    me_b = lax.axis_index("batch")
    me_z = lax.axis_index("ctx_0")
    me_lane = lax.axis_index("ctx_1") * 2 + lax.axis_index("ctx_2")
    s1, s2, s3, s4 = slots
    halves = PARTS // 2
    rows_part = keys.shape[1] // halves

    def part_of(pair, part):
        return pair[part // halves], pl.ds(part % halves * rows_part, rows_part)

    def ring_peer(k):
        return {"ctx_0": lax.rem(me_z + (k + NZ), NZ)}

    def plane_peer(i):
        lane = lax.rem(me_lane + i, LANES)
        return {"ctx_1": lane // 2, "ctx_2": lax.rem(lane, 2)}

    def pair_peer(i):
        return {"batch": 1 - me_b}

    loads = [
        pltpu.make_async_copy(source, store, in_sem.at[kind])
        for kind, (source, store) in enumerate(
            ((keys_in, keys), (values_in, values), (queries_in, queries))
        )
    ]
    for load in loads:
        load.start()

    barrier = pltpu.get_barrier_semaphore()
    for i in range(1, LANES):
        pl.semaphore_signal(barrier, inc=1, device_id=plane_peer(i), device_id_type=MESH)
    for k in range(1, NZ):
        pl.semaphore_signal(barrier, inc=1, device_id=ring_peer(k), device_id_type=MESH)
    pl.semaphore_signal(barrier, inc=1, device_id=pair_peer(0), device_id_type=MESH)

    def block_at(row, slot):
        return lax.max(lax.min(planned[row, slot], BLOCKS - 1), 0)

    def pack(part):
        store, rows = part_of((keys, values), part)

        def fill(slot, carry):
            for way, dst in ((0, zs_p), (1, zs_m)):
                dst[part][slot] = store[block_at(way, slot), rows]
            return carry

        lax.fori_loop(0, s1, fill, 0)

    def pack_own(part):
        store, rows = part_of((keys, values), part)
        for i in range(LANES):
            yb[part, 0, i] = store[block_at(2, lax.rem(me_lane + i, LANES)), rows]

    plan(keep[...], owner[...], me_z, meta, plan_rows)
    to_scalars = pltpu.make_async_copy(plan_rows, planned, t_sem.at[0])
    to_scalars.start()
    to_scalars.wait()
    loads[0].wait()
    pack(0)
    meta_ring[me_z] = meta[me_z]
    pl.semaphore_wait(barrier, LANES - 1 + NZ - 1 + 1)

    def share(source, buffer, number, at, peer, count):
        copies = []
        for i in range(1, count):
            copy = pltpu.make_async_remote_copy(
                src_ref=source(i),
                dst_ref=buffer.at[at],
                send_sem=s_send.at[number, i],
                recv_sem=s_recv.at[number, i],
                device_id=peer(i),
                device_id_type=MESH,
            )
            copy.start()
            copies.append(copy)
        return copies

    def settle(copies):
        for copy in copies:
            copy.wait()

    metas = share(
        lambda k: meta.at[lax.rem(me_z + k, NZ)], meta_ring, 4, me_z, ring_peer, NZ
    )

    segments = ((0, s4), (s4, s3), (s3, s2), (s2, s1))
    ring = ((zs_p, zr_p1, zr_p2, zr_p3), (zs_m, zr_m1, zr_m2, zr_m3))
    ring_copies = {}

    def ring_start(part, way, q, hop):
        a, b = segments[q]
        if a == b:
            return
        src = ring[way][hop - 1][part].at[pl.ds(a, b - a)]
        if hop < HALF:
            dst = ring[way][hop][part].at[pl.ds(a, b - a)]
        else:
            dst = zr_4[part].at[pl.ds(way * s4 + a, b - a)]
        number = q * HALF + hop - 1
        copy = pltpu.make_async_remote_copy(
            src_ref=src,
            dst_ref=dst,
            send_sem=z_send.at[part, way, number],
            recv_sem=z_recv.at[part, way, number],
            device_id=ring_peer(1 if way == 0 else -1),
            device_id_type=MESH,
        )
        copy.start()
        ring_copies[part, way, q, hop] = copy

    def arrived(part, q, hop):
        for way in range(2):
            if (part, way, q, hop) in ring_copies:
                ring_copies[part, way, q, hop].wait_recv()

    def hand_on(part, hop):
        for q in range(HALF - hop):
            for way in range(2):
                if (part, way, q, hop) in ring_copies:
                    ring_copies[part, way, q, hop].wait_recv()
                ring_start(part, way, q, hop + 1)
        arrived(part, HALF - hop, hop)

    arrivals = {1: zr_p1, 2: zr_p2, 3: zr_p3, 4: zr_4, 5: zr_m3, 6: zr_m2, 7: zr_m1}
    plane_copies = {}

    def plane_pack(part, b):
        source = lax.rem(me_z + (NZ - b), NZ)
        got = arrivals[b][part]
        for i in range(LANES):
            code = table[source, 0, lax.rem(me_lane + i, LANES)]
            is_second = (code > SECOND).astype(I32)
            slot = lax.max(code - 1 - is_second * SECOND, 0)
            if b == HALF:
                slot = lax.min(slot, s4 - 1) + is_second * s4
            else:
                slot = lax.min(slot, got.shape[0] - 1)
            yb[part, b, i] = got[slot]

    def plane_start(part, b):
        result, rows = part_of((yr_k, yr_v), part)
        source = lax.rem(me_z + (NZ - b), NZ) * LANES + me_lane
        for i in range(1, LANES):
            copy = pltpu.make_async_remote_copy(
                src_ref=yb.at[part, b, i],
                dst_ref=result.at[source, rows],
                send_sem=y_send.at[part, b, i],
                recv_sem=y_recv.at[part, b, i],
                device_id=plane_peer(i),
                device_id_type=MESH,
            )
            copy.start()
            plane_copies[part, b, i] = copy
        copy = pltpu.make_async_copy(
            yb.at[part, b, 0], result.at[source, rows], y_send.at[part, b, 0]
        )
        copy.start()
        plane_copies[part, b, 0] = copy

    def across(part, *batches):
        for b in batches:
            plane_pack(part, b)
        for b in batches:
            plane_start(part, b)

    def ring_first(part, *parts):
        for q in parts:
            for way in range(2):
                ring_start(part, way, q, 1)

    every = range(HALF)
    ring_first(0, *every)
    for part in range(1, halves):
        pack(part)
        ring_first(part, *every)
    loads[1].wait()
    for part in range(halves, PARTS):
        pack(part)
    for part in range(halves, PARTS - 1):
        ring_first(part, *every)
    for part in range(PARTS):
        pack_own(part)
    for part in range(PARTS):
        plane_start(part, 0)

    def widen(c, carry):
        kf[pl.ds(pl.multiple_of(c * 256, 256), 256), :] = keys[c].astype(F32)
        return carry

    lax.fori_loop(0, BLOCKS, widen, 0)
    live_here = length[0] - (me_z * LANES + me_lane) * (BLOCKS * BLOCK)
    rows = lax.broadcasted_iota(I32, (256, 256), 0)
    columns = lax.broadcasted_iota(I32, (256, 256), 1)
    lane_256 = lax.broadcasted_iota(I32, (1, 256), 1)

    def score(i, carry):
        g, c = i // 8, lax.rem(i, 8)
        chunk = kf[pl.ds(c * 1024 + g, 256, stride=4), :].astype(BF16)
        live = lax.broadcasted_iota(I32, (256, 128), 0) + c * 256 < live_here
        bias = jnp.where(live, 0.0, FAR)
        logits = contract_last(chunk, queries[g]) + jnp.concatenate([bias] * 5, axis=1)
        largest = jnp.max(logits, axis=0, keepdims=True)
        weights = jnp.exp2((logits - largest) * scale2)
        chunk_max[pl.ds(i, 1), :] = largest
        chunk_sum[pl.ds(i, 1), :] = jnp.sum(weights, axis=0, keepdims=True)
        probs[i] = weights.astype(BF16)
        gram = contract_last(chunk, chunk)
        on_diagonal = jnp.where(rows == columns, gram, 0.0)
        squares = jnp.sum(on_diagonal, axis=0, keepdims=True)
        down = jnp.sum(on_diagonal, axis=1, keepdims=True)
        spread = jnp.where(live[:, :1], 1.0, 0.0) / jnp.sqrt(down + NORM_EPS)
        norm = jnp.sqrt(squares + NORM_EPS)
        together = jnp.where(rows // BLOCK == columns // BLOCK, gram, 0.0)
        row_sum = jnp.sum(together * spread, axis=0, keepdims=True) / norm
        live_lanes = jnp.where(lane_256 + c * 256 < live_here, 1.0, 0.0)
        own_term = live_lanes * squares / (norm * norm)
        in_block = jnp.clip(live_here - c * 256 - lane_256 // BLOCK * BLOCK, 0, BLOCK).astype(F32)
        redundancy[pl.ds(i, 1), :] = (row_sum - own_term) / jnp.maximum(in_block - 1.0, 1.0)
        return carry

    loads[2].wait()
    lax.fori_loop(0, HEADS * 8, score, 0)

    row_of = lax.broadcasted_iota(I32, (STEP_ROWS, 128), 0)
    lane_of = lax.broadcasted_iota(I32, (STEP_ROWS, 128), 1)
    row_step = row_of % STEPS
    row_head = jnp.zeros((STEP_ROWS, 128), I32)
    for g in range(1, HEADS):
        row_head = row_head + (row_of >= g * GROUP * STEPS).astype(I32)
    same_head = lane_of % HEADS == row_head
    head_bias = jnp.concatenate([jnp.where(same_head, 0.0, FAR)] * 8, axis=1)
    may_see = same_head & (lane_of // HEADS <= row_step) & (lane_of < STEPS * HEADS)
    new_bias = jnp.where(may_see, 0.0, FAR)

    def padded(ref):
        return jnp.concatenate([ref[...], jnp.zeros((128 - STEPS * HEADS, 128), BF16)], axis=0)

    def decode_logits(c, top):
        chunk = keys[pl.ds(c * 4, 4)].reshape(1024, 128)
        kept_part = jnp.concatenate(
            [
                jnp.where(jnp.full((1, 256), planned[3, c * 4 + part], I32) > 0, 0.0, FAR)
                for part in range(4)
            ],
            axis=1,
        )
        token = lax.broadcasted_iota(I32, (1, 1024), 1) // HEADS + c * 256
        bias = kept_part + jnp.where(token < live_here, 0.0, FAR)
        found = contract_last(step_queries[...], chunk) + head_bias + bias
        dl[c] = found
        for part in range(8):
            top = jnp.maximum(top, found[:, part * 128 : (part + 1) * 128])
        return top

    new_logits = contract_last(step_queries[...], padded(new_keys)) + new_bias
    top = lax.fori_loop(0, 8, decode_logits, new_logits)
    step_top = column_to_row(jnp.max(top, axis=1, keepdims=True))

    maxima, sums = [], []
    for g in range(HEADS):
        part_max = chunk_max[g * 8 : g * 8 + 8, :]
        largest = jnp.max(part_max, axis=0, keepdims=True)
        maxima.append(largest)
        sums.append(
            jnp.sum(
                chunk_sum[g * 8 : g * 8 + 8, :] * jnp.exp2((part_max - largest) * scale2),
                axis=0,
                keepdims=True,
            )
        )
    tiles = [
        tuple(found[g][:, t * 128 : (t + 1) * 128] for found in (maxima, sums))
        for g in range(HEADS)
        for t in range(GROUP)
    ] + [(step_top, jnp.zeros((1, 128), F32))]
    stat_out[...] = jnp.zeros_like(stat_out)
    for n, (tile_max, tile_sum) in enumerate(tiles):
        stat_out[n // 3, n % 3 : n % 3 + 1, :] = tile_max
        stat_out[n // 3, n % 3 + 3 : n % 3 + 4, :] = tile_sum
    stat_plane[me_lane] = stat_out[me_lane]

    def plane_slice(buffer):
        return lambda i: buffer.at[lax.rem(me_lane + i, LANES)]

    settle(metas)
    to_scalars = pltpu.make_async_copy(meta_ring, table, t_sem.at[1])
    to_scalars.start()
    to_scalars.wait()
    meta_all[me_lane] = meta_ring[...]
    stats = share(plane_slice(stat_out), stat_plane, 0, me_lane, plane_peer, LANES)
    metas = share(lambda i: meta_ring, meta_all, 5, me_lane, plane_peer, LANES)

    def merged(buffer):
        largest = buffer[0, 0:3, :]
        for k in range(1, 8):
            largest = jnp.maximum(largest, buffer[k, 0:3, :])
        total = jnp.zeros((3, 128), F32)
        for k in range(8):
            total = total + buffer[k, 3:6, :] * jnp.exp2((buffer[k, 0:3, :] - largest) * scale2)
        return largest, total

    settle(stats)
    largest, total = merged(stat_plane)
    stat_ring[me_z, 0:3, :] = largest
    stat_ring[me_z, 3:6, :] = total
    stats = share(lambda k: stat_ring.at[me_z], stat_ring, 1, me_z, ring_peer, NZ)
    ring_first(PARTS - 1, *every)
    for part in range(PARTS):
        hand_on(part, 1)
        across(part, 1, 7)
    settle(metas)
    most = meta_all[0, 0]
    for lane in range(LANES):
        for z in range(NZ):
            most = jnp.maximum(most, meta_all[lane, z])
    needs_pair[me_b] = most
    coded = jnp.concatenate(
        [meta_all[lane, z] for z in range(NZ) for lane in range(LANES)], axis=0
    ).astype(F32)
    source = lax.broadcasted_iota(I32, (64, 128), 0)
    lane_64 = lax.broadcasted_iota(I32, (64, 128), 1)
    here = jnp.sum(jnp.where(lane_64 == me_lane, coded, 0.0), axis=1, keepdims=True) > 0.5
    here = jnp.broadcast_to(jnp.where(here, 1.0, 0.0), (64, 128))
    rank = jnp.dot(before_64(64), here.astype(BF16), preferred_element_type=F32)
    chosen = (here > 0.5) & (jnp.abs(rank - lane_64.astype(F32)) < 0.5)
    picks = jnp.sum(jnp.where(chosen, source.astype(F32), 0.0), axis=0, keepdims=True)
    out_picks[...] = picks.astype(I32)
    pair = share(lambda i: needs_pair.at[me_b], needs_pair, 6, me_b, pair_peer, 2)

    settle(stats)
    largest, total = merged(stat_ring)
    stat_all[me_lane, 0:3, :] = largest
    stat_all[me_lane, 3:6, :] = total
    stats = share(lambda i: stat_all.at[me_lane], stat_all, 7, me_lane, plane_peer, LANES)
    for part in range(PARTS // 2):
        hand_on(part, 2)
        across(part, 2, 6)

    settle(stats)

    def across_tiles(first, g):
        tiles = range(g * GROUP, (g + 1) * GROUP)
        return jnp.concatenate(
            [stat_all[n // 3, first + n % 3 : first + n % 3 + 1, :] for n in tiles], axis=1
        )

    row_max = [across_tiles(0, g) for g in range(HEADS)]
    row_total = [across_tiles(3, g) for g in range(HEADS)]
    step_column = row_to_column(stat_all[6, 2:3, :], STEP_ROWS)

    def decode_sum(c, carry):
        weighted, total = carry
        part = jnp.exp2((dl[c] - step_column) * scale2)
        for piece in range(8):
            total = total + part[:, piece * 128 : (piece + 1) * 128]
        chunk = values[pl.ds(c * 4, 4)].reshape(1024, 128)
        weighted = weighted + jnp.dot(part.astype(BF16), chunk, preferred_element_type=F32)
        return weighted, total

    nothing = jnp.zeros((STEP_ROWS, 128), F32)
    weighted, total = lax.fori_loop(0, 8, decode_sum, (nothing, nothing))
    bottom = column_to_row(jnp.sum(total, axis=1, keepdims=True))
    each = STEP_ROWS // LANES
    for lane in range(LANES):
        sum_out[lane, 0:each, :] = weighted[lane * each : (lane + 1) * each]
        sum_out[lane, each:16, :] = jnp.broadcast_to(bottom, (16 - each, 128))
    sum_plane[me_lane] = sum_out[me_lane]
    sums = share(plane_slice(sum_out), sum_plane, 2, me_lane, plane_peer, LANES)

    for g in range(HEADS):
        factor = (
            jnp.exp2((chunk_max[g * 8 : g * 8 + 8, :] - row_max[g]) * scale2)
            / row_total[g]
        )
        high = factor.astype(BF16)
        low = (factor - high.astype(F32)).astype(BF16)
        rescale[g] = jnp.concatenate([high.astype(F32), low.astype(F32)], axis=0).astype(BF16)
    share_of_row = jnp.full((1, 256), length[0], I32).astype(F32) / (WINDOW * GROUP)

    def importance(i, carry):
        g, c = i // 8, lax.rem(i, 8)
        found = contract_last(rescale[g], probs[i])
        wanted = lax.rem(lax.broadcasted_iota(I32, (16, 256), 0), 8) == c
        found = jnp.sum(jnp.where(wanted, found, 0.0), axis=0, keepdims=True)
        value = (LAMBDA * share_of_row) * found - (1.0 - LAMBDA) * redundancy[pl.ds(i, 1), :]
        live = lane_256 + c * 256 < live_here
        redundancy[pl.ds(i, 1), :] = jnp.where(live, value, 0.0)
        return carry

    for part in range(PARTS // 2, PARTS):
        hand_on(part, 2)
        across(part, 2, 6)
        piece = part - PARTS // 2
        lax.fori_loop(piece * 64 // PARTS, (piece + 1) * 64 // PARTS, importance, 0)

    def summed(buffer):
        total = buffer[0]
        for k in range(1, 8):
            total = total + buffer[k]
        return total

    settle(sums)
    sum_ring[me_z] = summed(sum_plane)
    sums = share(lambda k: sum_ring.at[me_z], sum_ring, 3, me_z, ring_peer, NZ)
    for part in range(PARTS):
        hand_on(part, 3)
        across(part, 3, 5)
    settle(sums)
    sum_all[me_lane] = summed(sum_ring)
    sums = share(lambda i: sum_all.at[me_lane], sum_all, 8, me_lane, plane_peer, LANES)
    for g in range(HEADS):
        for c in range(8):
            out_scores[g : g + 1, c * 256 : (c + 1) * 256] = redundancy[g * 8 + c : g * 8 + c + 1, :]
    settle(pair)
    over = jnp.maximum(needs_pair[0], needs_pair[1])
    lane = lax.broadcasted_iota(I32, (1, 128), 1)
    for n in range(4):
        over = jnp.where(lane == LANES + n, over - slots[n], over)
    over = jnp.where((lane >= LANES) & (lane < LANES + 4), over, -1)
    out_over[0] = jnp.max(over)

    for part in range(PARTS):
        arrived(part, 0, HALF)
        across(part, HALF)

    settle(sums)
    fresh = jnp.exp2((new_logits - step_column) * scale2)
    weighted = jnp.concatenate([sum_all[lane, 0:each, :] for lane in range(LANES)], axis=0)
    weighted = weighted + jnp.dot(
        fresh.astype(BF16), padded(new_values), preferred_element_type=F32
    )
    bottom = row_to_column(sum_all[0, each : each + 1, :], STEP_ROWS)
    bottom = bottom + jnp.sum(fresh, axis=1, keepdims=True)
    out_decoded[...] = (weighted / bottom).astype(BF16)

    for (part, b, i), copy in plane_copies.items():
        copy.wait()
    for copy in ring_copies.values():
        copy.wait_send()


VMEM, SMEM = pl.BlockSpec(memory_space=pltpu.VMEM), pl.BlockSpec(memory_space=pltpu.SMEM)
ANY = pl.BlockSpec(memory_space=pl.ANY)


def run_exchange(slots, collective_id, scale2, operands):
    s1, s2, s3, s4 = slots
    block = (BLOCKS * 8, 128)

    slot = (block[0] * 2 // PARTS, 128)

    def buffers(count):
        return (pltpu.VMEM((count, *slot), BF16),) * PARTS

    return pl.pallas_call(
        functools.partial(exchange, slots, scale2),
        out_shape=(
            jax.ShapeDtypeStruct((HEADS, BLOCKS * BLOCK), F32),
            jax.ShapeDtypeStruct((STEP_ROWS, 128), BF16),
            jax.ShapeDtypeStruct((1, 128), I32),
            jax.ShapeDtypeStruct((1,), I32),
            jax.ShapeDtypeStruct((NZ * LANES, *block), BF16),
            jax.ShapeDtypeStruct((NZ * LANES, *block), BF16),
        ),
        in_specs=[SMEM, VMEM, VMEM] + [ANY] * 3 + [VMEM] * 3,
        out_specs=(VMEM,) * 3 + (SMEM,) + (ANY,) * 2,
        scratch_shapes=[
            pltpu.VMEM((BLOCKS, *block), BF16),
            pltpu.VMEM((BLOCKS, *block), BF16),
            pltpu.VMEM((HEADS, WINDOW * GROUP, 128), BF16),
            pltpu.SemaphoreType.DMA((3,)),
            pltpu.VMEM((NZ, 1, 128), I32),
            pltpu.VMEM((8, 128), I32),
            pltpu.SMEM((8, 128), I32),
            buffers(s1),
            buffers(s1),
            buffers(s1),
            buffers(s2),
            buffers(s3),
            buffers(s1),
            buffers(s2),
            buffers(s3),
            buffers(2 * s4),
            pltpu.VMEM((PARTS, NZ, LANES, *slot), BF16),
            pltpu.VMEM((BLOCKS * 256, 128), F32),
            pltpu.VMEM((HEADS * 8, 256, WINDOW * GROUP), BF16),
            pltpu.VMEM((HEADS * 8, WINDOW * GROUP), F32),
            pltpu.VMEM((HEADS * 8, WINDOW * GROUP), F32),
            pltpu.VMEM((HEADS * 8, 256), F32),
            pltpu.VMEM((8, STEP_ROWS, 1024), F32),
            pltpu.VMEM((HEADS, 16, WINDOW * GROUP), BF16),
            pltpu.VMEM((NZ, 1, 128), I32),
            pltpu.VMEM((LANES, NZ, 1, 128), I32),
            pltpu.VMEM((2, 1, 128), I32),
            pltpu.SMEM((NZ, 1, 128), I32),
            *[pltpu.VMEM((8, 8, 128), F32)] * 4,
            *[pltpu.VMEM((8, 16, 128), F32)] * 4,
            pltpu.SemaphoreType.DMA((PARTS, 2, 16)),
            pltpu.SemaphoreType.DMA((PARTS, 2, 16)),
            pltpu.SemaphoreType.DMA((PARTS, NZ, LANES)),
            pltpu.SemaphoreType.DMA((PARTS, NZ, LANES)),
            pltpu.SemaphoreType.DMA((10, 8)),
            pltpu.SemaphoreType.DMA((10, 8)),
            pltpu.SemaphoreType.DMA((2,)),
        ],
        compiler_params=pltpu.CompilerParams(
            collective_id=collective_id,
            has_side_effects=True,
            vmem_limit_bytes=67_043_328,
        ),
        name="exchange_%d" % s1,
    )(*operands)


def unpack(
    picks, scores, decoded, came_k, came_v, out_scores, out_decoded, out_k, out_v, held, sems
):
    pairs = ((came_k, out_k), (came_v, out_v))

    def take(kind, j):
        return pltpu.make_async_copy(
            pairs[kind][0].at[picks[0, j]], held.at[kind, j], sems.at[0, kind, j]
        )

    def put(kind, j):
        return pltpu.make_async_copy(held.at[kind, j], pairs[kind][1].at[j], sems.at[1, kind, j])

    for kind in range(2):

        @pl.loop(0, KEEP)
        def _(j, kind=kind):
            take(kind, j).start()

    out_scores[...] = scores[...]
    out_decoded[...] = decoded[...]
    for kind in range(2):

        @pl.loop(0, KEEP)
        def _(j, kind=kind):
            take(kind, j).wait()
            put(kind, j).start()

    for kind in range(2):

        @pl.loop(0, KEEP)
        def _(j, kind=kind):
            put(kind, j).wait()


def run_unpack(picks, scores, decoded, came_k, came_v):
    block = came_k.shape[1:]
    shape = jax.ShapeDtypeStruct((KEEP, *block), BF16)
    return pl.pallas_call(
        unpack,
        out_shape=(
            jax.ShapeDtypeStruct(scores.shape, scores.dtype),
            jax.ShapeDtypeStruct(decoded.shape, decoded.dtype),
            shape,
            shape,
        ),
        in_specs=[SMEM, VMEM, VMEM, ANY, ANY],
        out_specs=(VMEM, VMEM, ANY, ANY),
        scratch_shapes=[
            pltpu.VMEM((2, KEEP, *block), BF16),
            pltpu.SemaphoreType.DMA((2, 2, KEEP)),
        ],
        name="unpack",
    )(picks, scores, decoded, came_k, came_v)


def shards(
    stored_keys,
    stored_values,
    observed_queries,
    decoded_queries,
    step_keys,
    decoded_values,
    keep_lists,
    owner_ids,
    cache_length,
):
    tokens, head_count, width = stored_keys.shape
    scale2 = math.log2(math.e) / math.sqrt(width)
    operands = (
        cache_length,
        keep_lists,
        owner_ids,
        stored_keys.reshape(BLOCKS, BLOCK * head_count, width),
        stored_values.reshape(BLOCKS, BLOCK * head_count, width),
        observed_queries.transpose(1, 0, 2).reshape(HEADS, GROUP * WINDOW, width),
        decoded_queries.transpose(1, 0, 2).reshape(STEP_ROWS, width),
        step_keys.reshape(STEPS * HEADS, width),
        decoded_values.reshape(STEPS * HEADS, width),
    )
    first = run_exchange(FITS_MOST, 0, scale2, operands)

    def finish(result):
        scores, decoded, picks, _, came_k, came_v = result
        return run_unpack(picks, scores, decoded, came_k, came_v)

    scores, decoded, kept_keys, kept_values = lax.cond(
        first[3][0] > 0,
        lambda: finish(run_exchange(FITS_ALL, 1, scale2, operands)),
        lambda: finish(first),
    )
    decoded = decoded.reshape(HEAD_ROWS, STEPS, width).transpose(1, 0, 2)
    shape = (KEEP * BLOCK, head_count, width)
    return scores, kept_keys.reshape(shape), kept_values.reshape(shape), decoded


def solution(mesh):
    split = Mesh(
        mesh.devices.reshape(mesh.shape["batch"], 8, 4, 2, mesh.shape["head"]),
        ("batch", "ctx_0", "ctx_1", "ctx_2", "head"),
    )
    return jax.shard_map(
        shards,
        mesh=split,
        in_specs=(
            P(BATCH_CTX, "head", None),
            P(BATCH_CTX, "head", None),
            P("batch", "head", None),
            P("batch", "head", None),
            P("batch", "head", None),
            P("batch", "head", None),
            P(BATCH_CTX, None),
            P(BATCH_CTX, None),
            P("batch"),
        ),
        out_specs=(
            P(("batch", "head"), CTX),
            P(BATCH_CTX, "head", None),
            P(BATCH_CTX, "head", None),
            P("batch", "head", None),
        ),
        check_vma=False,
    )
```

```python
import functools
import math

import jax
import jax.numpy as jnp
from jax import lax
from jax.experimental import pallas as pl
from jax.experimental.pallas import tpu as pltpu
from jax.sharding import Mesh
from jax.sharding import PartitionSpec as P

BLOCK = 64
CTX = ("ctx_0", "ctx_1", "ctx_2")
BATCH_CTX = ("batch", "ctx_0", "ctx_1", "ctx_2")
MESH = pl.DeviceIdType.MESH
FAR = -1e30
LAMBDA = 0.1
NORM_EPS = 1e-06
NZ = 8
LANES = 8
HALF = NZ // 2
HEADS = 4
GROUP = 5
STEPS = 4
HEAD_ROWS = HEADS * GROUP
STEP_ROWS = STEPS * HEAD_ROWS
WINDOW = 128
KEEP = 26
PARTS = 4
BLOCKS = 32
SECOND = 32
FITS_ALL = (26, 20, 12, 4)
FITS_MOST = (17, 13, 9, 4)
F32, BF16, I32 = jnp.float32, jnp.bfloat16, jnp.int32


def contract_last(a, b):
    return lax.dot_general(a, b, (((1,), (1,)), ((), ())), preferred_element_type=F32)


def row_to_column(row, rows):
    return jnp.transpose(jnp.broadcast_to(row, (128, 128)))[:rows, :1]


def column_to_row(column):
    rows = column.shape[0]
    wide = jnp.concatenate(
        [jnp.broadcast_to(column, (rows, 128)), jnp.zeros((128 - rows, 128), F32)], axis=0
    )
    return jnp.transpose(wide)[:1, :]


def before_64(block):
    row = lax.broadcasted_iota(I32, (64, 64), 0)
    column = lax.broadcasted_iota(I32, (64, 64), 1)
    return jnp.where((column < row) & (column // block == row // block), 1.0, 0.0).astype(BF16)


def spread_rows(block):
    shape = block.shape
    same = lax.broadcasted_iota(I32, shape, 0) == lax.broadcasted_iota(I32, shape, 1)
    return jnp.sum(jnp.where(same, block, 0.0), axis=0, keepdims=True)


def plan(slots, keep, owner, me_z, meta, lists):
    ahead_of_me = (owner + (NZ - me_z) * LANES) & (NZ * LANES - 1)
    match = lax.broadcasted_iota(I32, (NZ * LANES, KEEP), 0) == ahead_of_me
    wide = (NZ * LANES, 128)
    has = jnp.sum(jnp.where(match, 1.0, 0.0), axis=1, keepdims=True)
    has = jnp.broadcast_to(has, wide)
    block = jnp.sum(jnp.where(match, keep.astype(F32), 0.0), axis=1, keepdims=True)
    block = jnp.broadcast_to(block, wide)
    rank = jnp.dot(before_64(LANES), has.astype(BF16), preferred_element_type=F32)

    def plane(values, k):
        return values[k * LANES : (k + 1) * LANES]

    count = [jnp.sum(plane(has, k), axis=0, keepdims=True) for k in range(NZ)]
    n4 = count[HALF]
    ahead, behind = count[1] + count[2] + count[3], count[7] + count[6] + count[5]
    even = jnp.maximum(jnp.floor((n4 + behind - ahead + 1.0) * 0.5), 0.0)

    def room(three, two, near):
        return jnp.minimum(
            jnp.minimum(slots[2] - three, slots[1] - three - two), slots[0] - three - two - near
        )

    first = jnp.maximum(even, n4 - room(count[5], count[6], count[7]))
    first = jnp.minimum(first, room(count[3], count[2], count[1]))
    first = jnp.maximum(jnp.maximum(n4 - 4.0, 0.0), jnp.minimum(jnp.minimum(n4, 4.0), first))
    second = n4 - first
    tails_p = [first, first + count[3], first + count[3] + count[2], first + ahead]
    tails_m = [second, second + count[5], second + count[5] + count[6], second + behind]
    none = jnp.zeros_like(first)
    start = [none, tails_p[2], tails_p[1], tails_p[0], none, tails_m[0], tails_m[1], tails_m[2]]
    needs = [jnp.maximum(p, m) for p, m in zip(tails_p[::-1], tails_m[::-1])]
    lane = lax.broadcasted_iota(I32, (1, 128), 1)
    ways, places = [], []
    for k in range(NZ):
        if k == HALF:
            way = jnp.where(plane(rank, k) >= first, 1.0, 0.0)
        else:
            way = jnp.full((LANES, 128), float(k > HALF), F32)
        place = plane(rank, k) + start[k] - (way * first if k == HALF else 0.0)
        row = spread_rows(plane(has, k) * (place + 1.0 + way * SECOND))
        for n in range(4):
            row = jnp.where(lane == LANES + n, needs[n], row)
        meta[lax.rem(me_z + k, NZ)] = row.astype(I32)
        ways.append(way)
        places.append(place)
    way, place = jnp.concatenate(ways, axis=0), jnp.concatenate(places, axis=0)
    slot = lax.broadcasted_iota(I32, wide, 1).astype(F32)
    travels = (has > 0.5) & (lax.broadcasted_iota(I32, wide, 0) >= LANES)
    fills = travels & (jnp.abs(place - slot) < 0.5)
    for w in range(2):
        chosen = fills & (jnp.abs(way - w) < 0.5)
        row = jnp.sum(jnp.where(chosen, block, 0.0), axis=0, keepdims=True)
        lists[w : w + 1, :] = row.astype(I32)
    lists[2:3, :] = spread_rows(plane(block, 0)).astype(I32)
    named = lax.broadcasted_iota(I32, (BLOCKS, KEEP), 0) == keep
    named = jnp.sum(jnp.where(named, 1.0, 0.0), axis=1, keepdims=True)
    lists[3:4, :] = spread_rows(jnp.broadcast_to(named, (BLOCKS, 128))).astype(I32)
    lists[4:8, :] = jnp.zeros((4, 128), I32)


def exchange(
    slots,
    scale2,
    length,
    keep,
    owner,
    keys_in,
    values_in,
    queries_in,
    step_queries,
    new_keys,
    new_values,
    out_scores,
    out_decoded,
    out_picks,
    out_over,
    yr_k,
    yr_v,
    keys,
    values,
    queries,
    in_sem,
    meta,
    plan_rows,
    planned,
    zs_p,
    zs_m,
    zr_p1,
    zr_p2,
    zr_p3,
    zr_m1,
    zr_m2,
    zr_m3,
    zr_4,
    yb,
    kf,
    probs,
    chunk_max,
    chunk_sum,
    redundancy,
    dl,
    rescale,
    meta_ring,
    meta_all,
    needs_pair,
    table,
    stat_out,
    stat_plane,
    stat_ring,
    stat_all,
    sum_out,
    sum_plane,
    sum_ring,
    sum_all,
    z_send,
    z_recv,
    y_send,
    y_recv,
    s_send,
    s_recv,
    t_sem,
):
    me_b = lax.axis_index("batch")
    me_z = lax.axis_index("ctx_0")
    me_lane = lax.axis_index("ctx_1") * 2 + lax.axis_index("ctx_2")
    s1, s2, s3, s4 = slots
    halves = PARTS // 2
    rows_part = keys.shape[1] // halves

    def part_of(pair, part):
        return pair[part // halves], pl.ds(part % halves * rows_part, rows_part)

    def ring_peer(k):
        return {"ctx_0": lax.rem(me_z + (k + NZ), NZ)}

    def plane_peer(i):
        lane = lax.rem(me_lane + i, LANES)
        return {"ctx_1": lane // 2, "ctx_2": lax.rem(lane, 2)}

    def pair_peer(i):
        return {"batch": 1 - me_b}

    loads = [
        pltpu.make_async_copy(source, store, in_sem.at[kind])
        for kind, (source, store) in enumerate(
            ((keys_in, keys), (values_in, values), (queries_in, queries))
        )
    ]
    for load in loads:
        load.start()

    barrier = pltpu.get_barrier_semaphore()
    for i in range(1, LANES):
        pl.semaphore_signal(barrier, inc=1, device_id=plane_peer(i), device_id_type=MESH)
    for k in range(1, NZ):
        pl.semaphore_signal(barrier, inc=1, device_id=ring_peer(k), device_id_type=MESH)
    pl.semaphore_signal(barrier, inc=1, device_id=pair_peer(0), device_id_type=MESH)

    def block_at(row, slot):
        return lax.max(lax.min(planned[row, slot], BLOCKS - 1), 0)

    def pack(part):
        store, rows = part_of((keys, values), part)

        def fill(slot, carry):
            for way, dst in ((0, zs_p), (1, zs_m)):
                dst[part][slot] = store[block_at(way, slot), rows]
            return carry

        lax.fori_loop(0, s1, fill, 0)

    def pack_own(part):
        store, rows = part_of((keys, values), part)
        for i in range(LANES):
            yb[part, 0, i] = store[block_at(2, lax.rem(me_lane + i, LANES)), rows]

    plan(slots, keep[...], owner[...], me_z, meta, plan_rows)
    to_scalars = pltpu.make_async_copy(plan_rows, planned, t_sem.at[0])
    to_scalars.start()
    to_scalars.wait()
    loads[0].wait()
    pack(0)
    meta_ring[me_z] = meta[me_z]
    pl.semaphore_wait(barrier, LANES - 1 + NZ - 1 + 1)

    def share(source, buffer, number, at, peer, count):
        copies = []
        for i in range(1, count):
            copy = pltpu.make_async_remote_copy(
                src_ref=source(i),
                dst_ref=buffer.at[at],
                send_sem=s_send.at[number, i],
                recv_sem=s_recv.at[number, i],
                device_id=peer(i),
                device_id_type=MESH,
            )
            copy.start()
            copies.append(copy)
        return copies

    def settle(copies):
        for copy in copies:
            copy.wait()

    metas = share(
        lambda k: meta.at[lax.rem(me_z + k, NZ)], meta_ring, 4, me_z, ring_peer, NZ
    )

    segments = ((0, s4), (s4, s3), (s3, s2), (s2, s1))
    ring = ((zs_p, zr_p1, zr_p2, zr_p3), (zs_m, zr_m1, zr_m2, zr_m3))
    ring_copies = {}

    def ring_start(part, way, q, hop):
        a, b = segments[q]
        if a == b:
            return
        src = ring[way][hop - 1][part].at[pl.ds(a, b - a)]
        if hop < HALF:
            dst = ring[way][hop][part].at[pl.ds(a, b - a)]
        else:
            dst = zr_4[part].at[pl.ds(way * s4 + a, b - a)]
        number = q * HALF + hop - 1
        copy = pltpu.make_async_remote_copy(
            src_ref=src,
            dst_ref=dst,
            send_sem=z_send.at[part, way, number],
            recv_sem=z_recv.at[part, way, number],
            device_id=ring_peer(1 if way == 0 else -1),
            device_id_type=MESH,
        )
        copy.start()
        ring_copies[part, way, q, hop] = copy

    def arrived(part, q, hop):
        for way in range(2):
            if (part, way, q, hop) in ring_copies:
                ring_copies[part, way, q, hop].wait_recv()

    def hand_on(part, hop):
        for q in range(HALF - hop):
            for way in range(2):
                if (part, way, q, hop) in ring_copies:
                    ring_copies[part, way, q, hop].wait_recv()
                ring_start(part, way, q, hop + 1)
        arrived(part, HALF - hop, hop)

    arrivals = {1: zr_p1, 2: zr_p2, 3: zr_p3, 4: zr_4, 5: zr_m3, 6: zr_m2, 7: zr_m1}
    plane_copies = {}

    def plane_pack(part, b):
        source = lax.rem(me_z + (NZ - b), NZ)
        got = arrivals[b][part]
        for i in range(LANES):
            code = table[source, 0, lax.rem(me_lane + i, LANES)]
            is_second = (code > SECOND).astype(I32)
            slot = lax.max(code - 1 - is_second * SECOND, 0)
            if b == HALF:
                slot = lax.min(slot, s4 - 1) + is_second * s4
            else:
                slot = lax.min(slot, got.shape[0] - 1)
            yb[part, b, i] = got[slot]

    def plane_start(part, b):
        result, rows = part_of((yr_k, yr_v), part)
        source = lax.rem(me_z + (NZ - b), NZ) * LANES + me_lane
        for i in range(1, LANES):
            copy = pltpu.make_async_remote_copy(
                src_ref=yb.at[part, b, i],
                dst_ref=result.at[source, rows],
                send_sem=y_send.at[part, b, i],
                recv_sem=y_recv.at[part, b, i],
                device_id=plane_peer(i),
                device_id_type=MESH,
            )
            copy.start()
            plane_copies[part, b, i] = copy
        copy = pltpu.make_async_copy(
            yb.at[part, b, 0], result.at[source, rows], y_send.at[part, b, 0]
        )
        copy.start()
        plane_copies[part, b, 0] = copy

    def across(part, *batches):
        for b in batches:
            plane_pack(part, b)
        for b in batches:
            plane_start(part, b)

    def ring_first(part, *parts):
        for q in parts:
            for way in range(2):
                ring_start(part, way, q, 1)

    every = range(HALF)
    ring_first(0, *every)
    for part in range(1, halves):
        pack(part)
        ring_first(part, *every)
    loads[1].wait()
    for part in range(halves, PARTS):
        pack(part)
    for part in range(halves, PARTS - 1):
        ring_first(part, *every)
    for part in range(PARTS):
        pack_own(part)
    for part in range(PARTS):
        plane_start(part, 0)

    def widen(c, carry):
        kf[pl.ds(pl.multiple_of(c * 256, 256), 256), :] = keys[c].astype(F32)
        return carry

    lax.fori_loop(0, BLOCKS, widen, 0)
    live_here = length[0] - (me_z * LANES + me_lane) * (BLOCKS * BLOCK)
    rows = lax.broadcasted_iota(I32, (256, 256), 0)
    columns = lax.broadcasted_iota(I32, (256, 256), 1)
    lane_256 = lax.broadcasted_iota(I32, (1, 256), 1)

    def score(i, carry):
        g, c = i // 8, lax.rem(i, 8)
        chunk = kf[pl.ds(c * 1024 + g, 256, stride=4), :].astype(BF16)
        live = lax.broadcasted_iota(I32, (256, 128), 0) + c * 256 < live_here
        bias = jnp.where(live, 0.0, FAR)
        logits = contract_last(chunk, queries[g]) + jnp.concatenate([bias] * 5, axis=1)
        largest = jnp.max(logits, axis=0, keepdims=True)
        weights = jnp.exp2((logits - largest) * scale2)
        chunk_max[pl.ds(i, 1), :] = largest
        chunk_sum[pl.ds(i, 1), :] = jnp.sum(weights, axis=0, keepdims=True)
        probs[i] = weights.astype(BF16)
        gram = contract_last(chunk, chunk)
        on_diagonal = jnp.where(rows == columns, gram, 0.0)
        squares = jnp.sum(on_diagonal, axis=0, keepdims=True)
        down = jnp.sum(on_diagonal, axis=1, keepdims=True)
        spread = jnp.where(live[:, :1], 1.0, 0.0) / jnp.sqrt(down + NORM_EPS)
        norm = jnp.sqrt(squares + NORM_EPS)
        together = jnp.where(rows // BLOCK == columns // BLOCK, gram, 0.0)
        row_sum = jnp.sum(together * spread, axis=0, keepdims=True) / norm
        live_lanes = jnp.where(lane_256 + c * 256 < live_here, 1.0, 0.0)
        own_term = live_lanes * squares / (norm * norm)
        in_block = jnp.clip(live_here - c * 256 - lane_256 // BLOCK * BLOCK, 0, BLOCK).astype(F32)
        redundancy[pl.ds(i, 1), :] = (row_sum - own_term) / jnp.maximum(in_block - 1.0, 1.0)
        return carry

    loads[2].wait()
    lax.fori_loop(0, HEADS * 8, score, 0)

    row_of = lax.broadcasted_iota(I32, (STEP_ROWS, 128), 0)
    lane_of = lax.broadcasted_iota(I32, (STEP_ROWS, 128), 1)
    row_step = row_of % STEPS
    row_head = jnp.zeros((STEP_ROWS, 128), I32)
    for g in range(1, HEADS):
        row_head = row_head + (row_of >= g * GROUP * STEPS).astype(I32)
    same_head = lane_of % HEADS == row_head
    head_bias = jnp.concatenate([jnp.where(same_head, 0.0, FAR)] * 8, axis=1)
    may_see = same_head & (lane_of // HEADS <= row_step) & (lane_of < STEPS * HEADS)
    new_bias = jnp.where(may_see, 0.0, FAR)

    def padded(ref):
        return jnp.concatenate([ref[...], jnp.zeros((128 - STEPS * HEADS, 128), BF16)], axis=0)

    def decode_logits(c, top):
        chunk = keys[pl.ds(c * 4, 4)].reshape(1024, 128)
        kept_part = jnp.concatenate(
            [
                jnp.where(jnp.full((1, 256), planned[3, c * 4 + part], I32) > 0, 0.0, FAR)
                for part in range(4)
            ],
            axis=1,
        )
        token = lax.broadcasted_iota(I32, (1, 1024), 1) // HEADS + c * 256
        bias = kept_part + jnp.where(token < live_here, 0.0, FAR)
        found = contract_last(step_queries[...], chunk) + head_bias + bias
        dl[c] = found
        for part in range(8):
            top = jnp.maximum(top, found[:, part * 128 : (part + 1) * 128])
        return top

    new_logits = contract_last(step_queries[...], padded(new_keys)) + new_bias
    top = lax.fori_loop(0, 8, decode_logits, new_logits)
    step_top = column_to_row(jnp.max(top, axis=1, keepdims=True))

    maxima, sums = [], []
    for g in range(HEADS):
        part_max = chunk_max[g * 8 : g * 8 + 8, :]
        largest = jnp.max(part_max, axis=0, keepdims=True)
        maxima.append(largest)
        sums.append(
            jnp.sum(
                chunk_sum[g * 8 : g * 8 + 8, :] * jnp.exp2((part_max - largest) * scale2),
                axis=0,
                keepdims=True,
            )
        )
    tiles = [
        tuple(found[g][:, t * 128 : (t + 1) * 128] for found in (maxima, sums))
        for g in range(HEADS)
        for t in range(GROUP)
    ] + [(step_top, jnp.zeros((1, 128), F32))]
    stat_out[...] = jnp.zeros_like(stat_out)
    for n, (tile_max, tile_sum) in enumerate(tiles):
        stat_out[n // 3, n % 3 : n % 3 + 1, :] = tile_max
        stat_out[n // 3, n % 3 + 3 : n % 3 + 4, :] = tile_sum
    stat_plane[me_lane] = stat_out[me_lane]

    def plane_slice(buffer):
        return lambda i: buffer.at[lax.rem(me_lane + i, LANES)]

    settle(metas)
    to_scalars = pltpu.make_async_copy(meta_ring, table, t_sem.at[1])
    to_scalars.start()
    to_scalars.wait()
    meta_all[me_lane] = meta_ring[...]
    stats = share(plane_slice(stat_out), stat_plane, 0, me_lane, plane_peer, LANES)
    metas = share(lambda i: meta_ring, meta_all, 5, me_lane, plane_peer, LANES)

    def merged(buffer):
        largest = buffer[0, 0:3, :]
        for k in range(1, 8):
            largest = jnp.maximum(largest, buffer[k, 0:3, :])
        total = jnp.zeros((3, 128), F32)
        for k in range(8):
            total = total + buffer[k, 3:6, :] * jnp.exp2((buffer[k, 0:3, :] - largest) * scale2)
        return largest, total

    settle(stats)
    largest, total = merged(stat_plane)
    stat_ring[me_z, 0:3, :] = largest
    stat_ring[me_z, 3:6, :] = total
    stats = share(lambda k: stat_ring.at[me_z], stat_ring, 1, me_z, ring_peer, NZ)
    ring_first(PARTS - 1, *every)
    for part in range(PARTS):
        hand_on(part, 1)
        across(part, 1, 7)
    settle(metas)
    most = meta_all[0, 0]
    for lane in range(LANES):
        for z in range(NZ):
            most = jnp.maximum(most, meta_all[lane, z])
    needs_pair[me_b] = most
    coded = jnp.concatenate(
        [meta_all[lane, z] for z in range(NZ) for lane in range(LANES)], axis=0
    ).astype(F32)
    source = lax.broadcasted_iota(I32, (64, 128), 0)
    lane_64 = lax.broadcasted_iota(I32, (64, 128), 1)
    here = jnp.sum(jnp.where(lane_64 == me_lane, coded, 0.0), axis=1, keepdims=True) > 0.5
    here = jnp.broadcast_to(jnp.where(here, 1.0, 0.0), (64, 128))
    rank = jnp.dot(before_64(64), here.astype(BF16), preferred_element_type=F32)
    chosen = (here > 0.5) & (jnp.abs(rank - lane_64.astype(F32)) < 0.5)
    picks = jnp.sum(jnp.where(chosen, source.astype(F32), 0.0), axis=0, keepdims=True)
    out_picks[...] = picks.astype(I32)
    pair = share(lambda i: needs_pair.at[me_b], needs_pair, 6, me_b, pair_peer, 2)

    settle(stats)
    largest, total = merged(stat_ring)
    stat_all[me_lane, 0:3, :] = largest
    stat_all[me_lane, 3:6, :] = total
    stats = share(lambda i: stat_all.at[me_lane], stat_all, 7, me_lane, plane_peer, LANES)
    for part in range(PARTS // 2):
        hand_on(part, 2)
        across(part, 2, 6)

    settle(stats)

    def across_tiles(first, g):
        tiles = range(g * GROUP, (g + 1) * GROUP)
        return jnp.concatenate(
            [stat_all[n // 3, first + n % 3 : first + n % 3 + 1, :] for n in tiles], axis=1
        )

    row_max = [across_tiles(0, g) for g in range(HEADS)]
    row_total = [across_tiles(3, g) for g in range(HEADS)]
    step_column = row_to_column(stat_all[6, 2:3, :], STEP_ROWS)

    def decode_sum(c, carry):
        weighted, total = carry
        part = jnp.exp2((dl[c] - step_column) * scale2)
        for piece in range(8):
            total = total + part[:, piece * 128 : (piece + 1) * 128]
        chunk = values[pl.ds(c * 4, 4)].reshape(1024, 128)
        weighted = weighted + jnp.dot(part.astype(BF16), chunk, preferred_element_type=F32)
        return weighted, total

    nothing = jnp.zeros((STEP_ROWS, 128), F32)
    weighted, total = lax.fori_loop(0, 8, decode_sum, (nothing, nothing))
    bottom = column_to_row(jnp.sum(total, axis=1, keepdims=True))
    each = STEP_ROWS // LANES
    for lane in range(LANES):
        sum_out[lane, 0:each, :] = weighted[lane * each : (lane + 1) * each]
        sum_out[lane, each:16, :] = jnp.broadcast_to(bottom, (16 - each, 128))
    sum_plane[me_lane] = sum_out[me_lane]
    sums = share(plane_slice(sum_out), sum_plane, 2, me_lane, plane_peer, LANES)

    for g in range(HEADS):
        factor = (
            jnp.exp2((chunk_max[g * 8 : g * 8 + 8, :] - row_max[g]) * scale2)
            / row_total[g]
        )
        high = factor.astype(BF16)
        low = (factor - high.astype(F32)).astype(BF16)
        rescale[g] = jnp.concatenate([high.astype(F32), low.astype(F32)], axis=0).astype(BF16)
    share_of_row = jnp.full((1, 256), length[0], I32).astype(F32) / (WINDOW * GROUP)

    def importance(i, carry):
        g, c = i // 8, lax.rem(i, 8)
        found = contract_last(rescale[g], probs[i])
        wanted = lax.rem(lax.broadcasted_iota(I32, (16, 256), 0), 8) == c
        found = jnp.sum(jnp.where(wanted, found, 0.0), axis=0, keepdims=True)
        value = (LAMBDA * share_of_row) * found - (1.0 - LAMBDA) * redundancy[pl.ds(i, 1), :]
        live = lane_256 + c * 256 < live_here
        redundancy[pl.ds(i, 1), :] = jnp.where(live, value, 0.0)
        return carry

    for part in range(PARTS // 2, PARTS):
        hand_on(part, 2)
        across(part, 2, 6)
        piece = part - PARTS // 2
        lax.fori_loop(piece * 64 // PARTS, (piece + 1) * 64 // PARTS, importance, 0)

    def summed(buffer):
        total = buffer[0]
        for k in range(1, 8):
            total = total + buffer[k]
        return total

    settle(sums)
    sum_ring[me_z] = summed(sum_plane)
    sums = share(lambda k: sum_ring.at[me_z], sum_ring, 3, me_z, ring_peer, NZ)
    for part in range(PARTS):
        hand_on(part, 3)
        across(part, 3, 5)
    settle(sums)
    sum_all[me_lane] = summed(sum_ring)
    sums = share(lambda i: sum_all.at[me_lane], sum_all, 8, me_lane, plane_peer, LANES)
    for g in range(HEADS):
        for c in range(8):
            out_scores[g : g + 1, c * 256 : (c + 1) * 256] = redundancy[g * 8 + c : g * 8 + c + 1, :]
    settle(pair)
    over = jnp.maximum(needs_pair[0], needs_pair[1])
    lane = lax.broadcasted_iota(I32, (1, 128), 1)
    for n in range(4):
        over = jnp.where(lane == LANES + n, over - slots[n], over)
    over = jnp.where((lane >= LANES) & (lane < LANES + 4), over, -1)
    out_over[0] = jnp.max(over)

    for part in range(PARTS):
        arrived(part, 0, HALF)
        across(part, HALF)

    settle(sums)
    fresh = jnp.exp2((new_logits - step_column) * scale2)
    weighted = jnp.concatenate([sum_all[lane, 0:each, :] for lane in range(LANES)], axis=0)
    weighted = weighted + jnp.dot(
        fresh.astype(BF16), padded(new_values), preferred_element_type=F32
    )
    bottom = row_to_column(sum_all[0, each : each + 1, :], STEP_ROWS)
    bottom = bottom + jnp.sum(fresh, axis=1, keepdims=True)
    out_decoded[...] = (weighted / bottom).astype(BF16)

    for (part, b, i), copy in plane_copies.items():
        copy.wait()
    for copy in ring_copies.values():
        copy.wait_send()


VMEM, SMEM = pl.BlockSpec(memory_space=pltpu.VMEM), pl.BlockSpec(memory_space=pltpu.SMEM)
ANY = pl.BlockSpec(memory_space=pl.ANY)


def run_exchange(slots, collective_id, scale2, operands):
    s1, s2, s3, s4 = slots
    block = (BLOCKS * 8, 128)

    slot = (block[0] * 2 // PARTS, 128)

    def buffers(count):
        return (pltpu.VMEM((count, *slot), BF16),) * PARTS

    return pl.pallas_call(
        functools.partial(exchange, slots, scale2),
        out_shape=(
            jax.ShapeDtypeStruct((HEADS, BLOCKS * BLOCK), F32),
            jax.ShapeDtypeStruct((STEP_ROWS, 128), BF16),
            jax.ShapeDtypeStruct((1, 128), I32),
            jax.ShapeDtypeStruct((1,), I32),
            jax.ShapeDtypeStruct((NZ * LANES, *block), BF16),
            jax.ShapeDtypeStruct((NZ * LANES, *block), BF16),
        ),
        in_specs=[SMEM, VMEM, VMEM] + [ANY] * 3 + [VMEM] * 3,
        out_specs=(VMEM,) * 3 + (SMEM,) + (ANY,) * 2,
        scratch_shapes=[
            pltpu.VMEM((BLOCKS, *block), BF16),
            pltpu.VMEM((BLOCKS, *block), BF16),
            pltpu.VMEM((HEADS, WINDOW * GROUP, 128), BF16),
            pltpu.SemaphoreType.DMA((3,)),
            pltpu.VMEM((NZ, 1, 128), I32),
            pltpu.VMEM((8, 128), I32),
            pltpu.SMEM((8, 128), I32),
            buffers(s1),
            buffers(s1),
            buffers(s1),
            buffers(s2),
            buffers(s3),
            buffers(s1),
            buffers(s2),
            buffers(s3),
            buffers(2 * s4),
            pltpu.VMEM((PARTS, NZ, LANES, *slot), BF16),
            pltpu.VMEM((BLOCKS * 256, 128), F32),
            pltpu.VMEM((HEADS * 8, 256, WINDOW * GROUP), BF16),
            pltpu.VMEM((HEADS * 8, WINDOW * GROUP), F32),
            pltpu.VMEM((HEADS * 8, WINDOW * GROUP), F32),
            pltpu.VMEM((HEADS * 8, 256), F32),
            pltpu.VMEM((8, STEP_ROWS, 1024), F32),
            pltpu.VMEM((HEADS, 16, WINDOW * GROUP), BF16),
            pltpu.VMEM((NZ, 1, 128), I32),
            pltpu.VMEM((LANES, NZ, 1, 128), I32),
            pltpu.VMEM((2, 1, 128), I32),
            pltpu.SMEM((NZ, 1, 128), I32),
            *[pltpu.VMEM((8, 8, 128), F32)] * 4,
            *[pltpu.VMEM((8, 16, 128), F32)] * 4,
            pltpu.SemaphoreType.DMA((PARTS, 2, 16)),
            pltpu.SemaphoreType.DMA((PARTS, 2, 16)),
            pltpu.SemaphoreType.DMA((PARTS, NZ, LANES)),
            pltpu.SemaphoreType.DMA((PARTS, NZ, LANES)),
            pltpu.SemaphoreType.DMA((10, 8)),
            pltpu.SemaphoreType.DMA((10, 8)),
            pltpu.SemaphoreType.DMA((2,)),
        ],
        compiler_params=pltpu.CompilerParams(
            collective_id=collective_id,
            has_side_effects=True,
            vmem_limit_bytes=67_043_328,
        ),
        name="exchange_%d" % s1,
    )(*operands)


def unpack(
    picks, scores, decoded, came_k, came_v, out_scores, out_decoded, out_k, out_v, held, sems
):
    pairs = ((came_k, out_k), (came_v, out_v))

    def take(kind, j):
        return pltpu.make_async_copy(
            pairs[kind][0].at[picks[0, j]], held.at[kind, j], sems.at[0, kind, j]
        )

    def put(kind, j):
        return pltpu.make_async_copy(held.at[kind, j], pairs[kind][1].at[j], sems.at[1, kind, j])

    for kind in range(2):

        @pl.loop(0, KEEP)
        def _(j, kind=kind):
            take(kind, j).start()

    out_scores[...] = scores[...]
    out_decoded[...] = decoded[...]
    for kind in range(2):

        @pl.loop(0, KEEP)
        def _(j, kind=kind):
            take(kind, j).wait()
            put(kind, j).start()

    for kind in range(2):

        @pl.loop(0, KEEP)
        def _(j, kind=kind):
            put(kind, j).wait()


def run_unpack(picks, scores, decoded, came_k, came_v):
    block = came_k.shape[1:]
    shape = jax.ShapeDtypeStruct((KEEP, *block), BF16)
    return pl.pallas_call(
        unpack,
        out_shape=(
            jax.ShapeDtypeStruct(scores.shape, scores.dtype),
            jax.ShapeDtypeStruct(decoded.shape, decoded.dtype),
            shape,
            shape,
        ),
        in_specs=[SMEM, VMEM, VMEM, ANY, ANY],
        out_specs=(VMEM, VMEM, ANY, ANY),
        scratch_shapes=[
            pltpu.VMEM((2, KEEP, *block), BF16),
            pltpu.SemaphoreType.DMA((2, 2, KEEP)),
        ],
        name="unpack",
    )(picks, scores, decoded, came_k, came_v)


def shards(
    stored_keys,
    stored_values,
    observed_queries,
    decoded_queries,
    step_keys,
    decoded_values,
    keep_lists,
    owner_ids,
    cache_length,
):
    tokens, head_count, width = stored_keys.shape
    scale2 = math.log2(math.e) / math.sqrt(width)
    operands = (
        cache_length,
        keep_lists,
        owner_ids,
        stored_keys.reshape(BLOCKS, BLOCK * head_count, width),
        stored_values.reshape(BLOCKS, BLOCK * head_count, width),
        observed_queries.transpose(1, 0, 2).reshape(HEADS, GROUP * WINDOW, width),
        decoded_queries.transpose(1, 0, 2).reshape(STEP_ROWS, width),
        step_keys.reshape(STEPS * HEADS, width),
        decoded_values.reshape(STEPS * HEADS, width),
    )
    first = run_exchange(FITS_MOST, 0, scale2, operands)

    def finish(result):
        scores, decoded, picks, _, came_k, came_v = result
        return run_unpack(picks, scores, decoded, came_k, came_v)

    scores, decoded, kept_keys, kept_values = lax.cond(
        first[3][0] > 0,
        lambda: finish(run_exchange(FITS_ALL, 1, scale2, operands)),
        lambda: finish(first),
    )
    decoded = decoded.reshape(HEAD_ROWS, STEPS, width).transpose(1, 0, 2)
    shape = (KEEP * BLOCK, head_count, width)
    return scores, kept_keys.reshape(shape), kept_values.reshape(shape), decoded


def solution(mesh):
    split = Mesh(
        mesh.devices.reshape(mesh.shape["batch"], 8, 4, 2, mesh.shape["head"]),
        ("batch", "ctx_0", "ctx_1", "ctx_2", "head"),
    )
    return jax.shard_map(
        shards,
        mesh=split,
        in_specs=(
            P(BATCH_CTX, "head", None),
            P(BATCH_CTX, "head", None),
            P("batch", "head", None),
            P("batch", "head", None),
            P("batch", "head", None),
            P("batch", "head", None),
            P(BATCH_CTX, None),
            P(BATCH_CTX, None),
            P("batch"),
        ),
        out_specs=(
            P(("batch", "head"), CTX),
            P(BATCH_CTX, "head", None),
            P(BATCH_CTX, "head", None),
            P("batch", "head", None),
        ),
        check_vma=False,
    )
```
